32 devices in a mesh: dp: 8 (over z, y), tensor: 4 (over x, core).
Axes of the slice: x: 2, y: 2, z: 4, core: 2. Of those that a mesh axis runs over, the one named last changes fastest.
Arguments:
- tokens: bfloat16 [16384, 768], P(('dp', 'tensor')), may hold values from -6 to 6
- time_emb: bfloat16 [16, 128], P('dp'), may hold values from -5 to 5
- prefix_len: int32 [16], P('dp'), may hold values from 0 to 511
- noise_mask: int32 [16384], P(('dp', 'tensor')), may hold values 0 or 1
- mask_embed: bfloat16 [768], replicated, may hold values from -5 to 5
- gain_attn: bfloat16 [768], replicated, may hold values from 0.25 to 1.75
- gain_mlp: bfloat16 [768], replicated, may hold values from 0.25 to 1.75
- ada_weight: bfloat16 [128, 4608], replicated, may hold values from -0.5 to 0.5
- ada_bias: bfloat16 [4608], replicated, may hold values from -3 to 3
- qkv_weight: bfloat16 [768, 3, 768], P(None, None, 'tensor'), may hold values from -0.21875 to 0.21875
- out_weight: bfloat16 [768, 768], P('tensor'), may hold values from -0.75 to 0.75
- up_weight: bfloat16 [768, 3072], P(None, 'tensor'), may hold values from -0.21875 to 0.21875
- up_bias: bfloat16 [3072], P('tensor'), may hold values from -3 to 3
- down_weight: bfloat16 [3072, 768], P('tensor'), may hold values from -0.109375 to 0.109375
- down_bias: bfloat16 [768], replicated, may hold values from -3 to 3
- cotangent: bfloat16 [16384, 768], P(('dp', 'tensor')), may hold values from -6 to 6
Outputs:
- output: bfloat16 [16384, 768], P(('dp', 'tensor'))
- grad_tokens: float32 [16384, 768], P(('dp', 'tensor'))
- grad_time: float32 [16, 128], P('dp')
- grad_mask_embed: float32 [768], replicated
- grad_gain_attn: float32 [768], replicated
- grad_gain_mlp: float32 [768], replicated
- grad_ada_weight: float32 [128, 4608], replicated
- grad_ada_bias: float32 [4608], replicated
- grad_qkv: float32 [768, 3, 768], P(None, None, 'tensor')
- grad_out: float32 [768, 768], P('tensor')
- grad_up: float32 [768, 3072], P(None, 'tensor')
- grad_up_bias: float32 [3072], P('tensor')
- grad_down: float32 [3072, 768], P('tensor')
- grad_down_bias: float32 [768], replicated
The draws below stay inside these ranges and needn't reach their ends.
All inputs are finite; a program needn't handle non-finite values. No bound on the sum of `noise_mask` on one device may be relied on, other than what follows from the above.
Results may differ from the reference program's by a relative error of at most 0.012.
The reference program's roundings to bfloat16 on the way count: a program that leaves them out, or rounds other values in their place, can miss the bound.
Values may be sent and summed in bfloat16 or wider, within the bound.
A program may use at most 128 MiB of HBM per device.

```python
import jax
import jax.numpy as jnp
from jax import lax

D = 768
HEADS = 12
HD = 64
FF = 3072
COND = 128
LEN = 1024
SEQ_DEV = 2
SEQS = 16
TOKENS = 16384
N_DP = 8


def with_ends(values, own_key, least, largest):
    spot = [jax.random.randint(jax.random.fold_in(own_key, axis), (), 0, length) for axis, length in enumerate(values.shape)]
    widest = values.shape.index(max(values.shape))
    next_to = spot[:widest] + [(spot[widest] + 1) % values.shape[widest]] + spot[widest + 1:]
    return values.at[tuple(spot)].set(least).at[tuple(next_to)].set(largest)


def level_of(stream_key, extent, pieces, least, largest):
    def one(dim, shards_of):
        steps = jax.random.uniform(jax.random.fold_in(jax.random.fold_in(stream_key, 6), dim), (shards_of,), jnp.float32, least / len(pieces), largest / len(pieces))
        return jnp.repeat(jnp.exp(steps), extent[dim] // shards_of).reshape((-1,) + (1,) * (len(extent) - dim - 1))

    loudness = one(*pieces[0])
    for cut in pieces[1:]:
        loudness = loudness * one(*cut)
    return loudness


def noise(key, dims, spread, bound, cuts=(), kind=jnp.bfloat16):
    entries = jax.random.normal(key, dims, jnp.float32) * spread
    if len(cuts) > 0:
        entries = level_of(key, dims, cuts, -0.22, 0.18) * entries
    return jnp.clip(entries, min=-bound, max=bound).astype(kind)


def setup_inputs(seed: int = 0) -> dict:
    arg_keys = jax.random.split(jax.random.key(seed), 17)
    tokens = noise(arg_keys[0], (TOKENS, D), 1.0, 6.0, ((0, 32),))
    time_emb = noise(arg_keys[1], (SEQS, COND), 1.0, 5.0, ((0, 8),))
    prefix_len = with_ends(jax.random.randint(arg_keys[2], (SEQS,), 0, LEN // 2), jax.random.fold_in(arg_keys[2], 1), 0, (LEN // 2) - 1).astype(jnp.int32)
    noise_mask = with_ends((jax.random.randint(arg_keys[3], (TOKENS,), 0, 2) < 1).astype(jnp.int32), jax.random.fold_in(arg_keys[3], 1), 0, 1)
    mask_embed = noise(arg_keys[4], (D,), 1.0, 5.0)
    gain_attn = jnp.clip(1.0 + 0.15 * jax.random.normal(arg_keys[5], (D,), jnp.float32), 0.25, 1.75).astype(jnp.bfloat16)
    gain_mlp = jnp.clip(1.0 + 0.15 * jax.random.normal(arg_keys[6], (D,), jnp.float32), 0.25, 1.75).astype(jnp.bfloat16)
    ada_weight = noise(arg_keys[7], (COND, 6 * D), COND ** -0.5, 0.5)
    ada_bias = noise(arg_keys[8], (6 * D,), 0.5, 3.0)
    qkv_weight = noise(arg_keys[9], (D, 3, D), D ** -0.5, 0.21875, ((2, 4),))
    out_weight = noise(arg_keys[10], (D, D), HD ** -0.5, 0.75, ((0, 4),))
    up_weight = noise(arg_keys[11], (D, FF), D ** -0.5, 0.21875, ((1, 4),))
    up_bias = noise(arg_keys[12], (FF,), 0.5, 3.0, ((0, 4),))
    down_weight = noise(arg_keys[13], (FF, D), FF ** -0.5, 0.109375, ((0, 4),))
    down_bias = noise(arg_keys[14], (D,), 0.5, 3.0)
    cotangent = noise(arg_keys[15], (TOKENS, D), 1.0, 6.0, ((0, 32),))
    return dict(tokens=tokens, time_emb=time_emb, prefix_len=prefix_len, noise_mask=noise_mask, mask_embed=mask_embed, gain_attn=gain_attn, gain_mlp=gain_mlp, ada_weight=ada_weight, ada_bias=ada_bias, qkv_weight=qkv_weight, out_weight=out_weight, up_weight=up_weight, up_bias=up_bias, down_weight=down_weight, down_bias=down_bias, cotangent=cotangent)


@jax.custom_vjp
def low(v):
    return lax.optimization_barrier(v.astype(jnp.bfloat16)).astype(jnp.float32)

@jax.custom_vjp
def low_back(v):
    return v

def low_keep(v):
    return (low(v), None)

def low_pass(kept, grad):
    return (grad,)

def back_keep(v):
    return (v, None)

def back_low(kept, grad):
    return (low(grad),)
low.defvjp(low_keep, low_pass)
low_back.defvjp(back_keep, back_low)
norm_eps = 1e-05
gelu_coef = 0.7978845608028654
cubic_coef = 0.044715

def matmul_high(left, right):
    return jnp.dot(left, right, precision=lax.Precision.HIGHEST, preferred_element_type=jnp.float32)

def normalize(values):
    centered = values - lax.optimization_barrier(jnp.mean(values, axis=-1, keepdims=True))
    return centered * lax.rsqrt(lax.optimization_barrier(jnp.mean(centered * centered, axis=-1, keepdims=True)) + norm_eps)

def rotate_half(vectors):
    first = vectors[..., :HD // 2]
    second = vectors[..., HD // 2:]
    return jnp.concatenate([-second, first], axis=-1)

def rotary_tables():
    frequency = 10000.0 ** (-2.0 * jnp.arange(HD // 2, dtype=jnp.float32) / HD)
    angles = jnp.arange(LEN, dtype=jnp.float32)[:, None] * frequency[None, :]
    angles = jnp.concatenate([angles, angles], axis=-1)
    return (jnp.cos(angles), jnp.sin(angles))

def gelu_tanh(values):
    return 0.5 * values * (1.0 + jnp.tanh(gelu_coef * (values + cubic_coef * values * values * values)))

@jax.checkpoint
def attend_pair(operands):
    queries, key_rows, value_rows = operands
    scores = low_back(matmul_high(queries, key_rows.T) * 0.125)
    shifted = scores - lax.optimization_barrier(jnp.max(scores, axis=-1, keepdims=True))
    weights = jnp.exp(shifted)
    probs = weights / lax.optimization_barrier(jnp.sum(weights, axis=-1, keepdims=True))
    return matmul_high(low(probs), value_rows)

def layer(prefix_len, noise_mask, tokens, time_emb, mask_embed, gain_attn, gain_mlp, ada_weight, ada_bias, qkv_weight, out_weight, up_weight, up_bias, down_weight, down_bias):
    row_count = SEQ_DEV * LEN
    position = jnp.arange(row_count, dtype=jnp.int32) % LEN
    sequence = jnp.arange(row_count, dtype=jnp.int32) // LEN
    noised = (noise_mask == 1) & (position >= prefix_len[sequence])
    inputs = jnp.where(noised[:, None], mask_embed[None, :], tokens)
    modulation = matmul_high(jax.nn.silu(time_emb), ada_weight) + ada_bias
    per_row = modulation[sequence]
    shift_attn, scale_attn, gate_attn, shift_mlp, scale_mlp, gate_mlp = jnp.split(per_row, 6, axis=1)
    hidden_attn = low(normalize(inputs) * gain_attn * (1.0 + scale_attn) + shift_attn)
    projected = low_back(jnp.einsum('rd,dcf->rcf', hidden_attn, qkv_weight, precision=lax.Precision.HIGHEST))
    projected = projected.reshape(SEQ_DEV, LEN, 3, HEADS, HD)
    cosine, sine = rotary_tables()
    cosine = cosine[None, :, None, :]
    sine = sine[None, :, None, :]
    raw_query = projected[:, :, 0]
    raw_key = projected[:, :, 1]
    queries = low(raw_query * cosine + rotate_half(raw_query) * sine)
    key_rows = low(raw_key * cosine + rotate_half(raw_key) * sine)
    value_rows = low(projected[:, :, 2])

    def by_head(values):
        return values.transpose(0, 2, 1, 3).reshape(SEQ_DEV * HEADS, LEN, HD)
    attended = lax.map(attend_pair, (by_head(queries), by_head(key_rows), by_head(value_rows)))
    attended = attended.reshape(SEQ_DEV, HEADS, LEN, HD).transpose(0, 2, 1, 3).reshape(row_count, D)
    attended = low(low_back(attended))
    branch_attn = low_back(matmul_high(attended, out_weight))
    mixed = inputs + gate_attn * branch_attn
    hidden_mlp = low(normalize(mixed) * gain_mlp * (1.0 + scale_mlp) + shift_mlp)
    upper = low_back(matmul_high(hidden_mlp, up_weight) + up_bias)
    active = low(gelu_tanh(upper))
    branch_mlp = low_back(matmul_high(active, down_weight) + down_bias)
    return mixed + gate_mlp * branch_mlp

def reference(tokens, time_emb, prefix_len, noise_mask, mask_embed, gain_attn, gain_mlp, ada_weight, ada_bias, qkv_weight, out_weight, up_weight, up_bias, down_weight, down_bias, cotangent):
    weights = tuple((item.astype(jnp.float32) for item in (mask_embed, gain_attn, gain_mlp, ada_weight, ada_bias, qkv_weight, out_weight, up_weight, up_bias, down_weight, down_bias)))
    row_count = SEQ_DEV * LEN
    token_groups = tokens.astype(jnp.float32).reshape(N_DP, row_count, D)
    time_groups = time_emb.astype(jnp.float32).reshape(N_DP, SEQ_DEV, COND)
    prefix_groups = prefix_len.reshape(N_DP, SEQ_DEV)
    noise_groups = noise_mask.reshape(N_DP, row_count)
    cot_groups = cotangent.astype(jnp.float32).reshape(N_DP, row_count, D)

    def group_step(totals, slices):
        group_tok, group_time, group_prefix, group_noise, group_cot = slices

        def closed(*operands):
            return layer(group_prefix, group_noise, *operands)
        result, pullback = jax.vjp(closed, group_tok, group_time, *weights)
        grads = pullback(group_cot)
        new_totals = tuple((old + new for old, new in zip(totals, grads[2:])))
        return (new_totals, (result.astype(jnp.bfloat16), grads[0], grads[1]))
    zeros = tuple((jnp.zeros_like(item) for item in weights))
    totals, (outputs, grad_tok, grad_time) = lax.scan(group_step, zeros, (token_groups, time_groups, prefix_groups, noise_groups, cot_groups))
    output = outputs.reshape(TOKENS, D)
    grad_tokens = grad_tok.reshape(TOKENS, D)
    grad_time = grad_time.reshape(SEQS, COND)
    return (output, grad_tokens, grad_time, totals[0], totals[1], totals[2], totals[3], totals[4], totals[5], totals[6], totals[7], totals[8], totals[9], totals[10])
```

```python
import functools

import jax
import jax.numpy as jnp
import numpy as np
from jax import lax
from jax.experimental import pallas as pl
from jax.experimental.pallas import tpu as pltpu
from jax.sharding import PartitionSpec as P

BF = jnp.bfloat16
F = jnp.float32
HD = 64
LEN = 1024
EPS = 1e-05
GELU_COEF = 0.7978845608028654
CUBIC_COEF = 0.044715
SCALE = 0.125
LOG2E = 1.4426950408889634
EXP_SCALE = SCALE * LOG2E
MIB = 1 << 20


def nn(a, b):
    return lax.dot_general(a, b, (((1,), (0,)), ((), ())), preferred_element_type=F)


def nt(a, b):
    return lax.dot_general(a, b, (((1,), (1,)), ((), ())), preferred_element_type=F)


def tn(a, b):
    return lax.dot_general(a, b, (((0,), (0,)), ((), ())), preferred_element_type=F)


def matmul_high(left, right):
    return jnp.dot(left, right, precision=lax.Precision.HIGHEST, preferred_element_type=F)


def normalize(values):
    centered = values - jnp.mean(values, axis=-1, keepdims=True)
    inv = lax.rsqrt(jnp.mean(centered * centered, axis=-1, keepdims=True) + EPS)
    return centered * inv, inv


def layer_back(grad_norm, normed, inv):
    mean_grad = jnp.mean(grad_norm, axis=-1, keepdims=True)
    mean_cross = jnp.mean(grad_norm * normed, axis=-1, keepdims=True)
    return inv * (grad_norm - mean_grad - normed * mean_cross)


def halves_turned(v):
    parts = []
    for h in range(v.shape[1] // HD):
        lo = v[:, h * HD : h * HD + HD // 2]
        hi = v[:, h * HD + HD // 2 : (h + 1) * HD]
        parts += [-hi, lo]
    return jnp.concatenate(parts, axis=1)


def halves_back(v):
    parts = []
    for h in range(v.shape[1] // HD):
        lo = v[:, h * HD : h * HD + HD // 2]
        hi = v[:, h * HD + HD // 2 : (h + 1) * HD]
        parts += [hi, -lo]
    return jnp.concatenate(parts, axis=1)


def tables(block, heads):
    cos, sin = block[:, :HD], block[:, HD:]
    return jnp.concatenate([cos] * heads, axis=1), jnp.concatenate([sin] * heads, axis=1)


def call(kernel, outs, args, flops, grid=None, in_specs=None, out_specs=None, scratch=(), aliases=None, vmem=48, name=None):
    nbytes = sum(a.size * a.dtype.itemsize for a in args) + sum(o.size * o.dtype.itemsize for o in outs)
    kwargs = {}
    if grid is not None:
        kwargs["grid"] = grid
    if in_specs is None:
        in_specs = [pl.BlockSpec(memory_space=pltpu.VMEM)] * len(args)
    if out_specs is None:
        out_specs = [pl.BlockSpec(memory_space=pltpu.VMEM)] * len(outs)
    return pl.pallas_call(
        kernel,
        out_shape=tuple(outs),
        in_specs=in_specs,
        out_specs=tuple(out_specs),
        scratch_shapes=list(scratch),
        input_output_aliases=aliases or {},
        compiler_params=pltpu.CompilerParams(vmem_limit_bytes=vmem * MIB),
        cost_estimate=pl.CostEstimate(flops=flops, bytes_accessed=nbytes, transcendentals=0),
        name=name,
        **kwargs,
    )(*args)


def sds(shape, dtype):
    return jax.ShapeDtypeStruct(shape, dtype)


def head_kernel(tok, noised, cot, mask, gain, time, ada_w, ada_b, mod_o, h1_o, gm_o, gdb_o):
    d = tok.shape[1]
    tv = jnp.broadcast_to(time[...].astype(F), (16, time.shape[1]))
    s = tv / (1.0 + jnp.exp(-tv))
    hi = s.astype(BF).astype(F)
    mid = (s - hi).astype(BF).astype(F)
    low = (s - hi - mid).astype(BF).astype(F)
    stacked = jnp.concatenate([hi, mid, low], axis=0).astype(BF)
    for i in range(6):
        cols = pl.ds(i * d, d)
        m = nn(stacked, ada_w[:, cols])
        m = m[0:1] + m[16:17] + m[32:33] + ada_b[:, cols].astype(F)
        mod_o[i : i + 1, :] = m
    inputs = jnp.where(noised[...] > 0.5, mask[...].astype(F), tok[...].astype(F))
    n1, _ = normalize(inputs)
    h1 = n1 * gain[...].astype(F) * (1.0 + mod_o[1:2, :]) + mod_o[0:1, :]
    h1_o[...] = h1.astype(BF)
    gm = (mod_o[5:6, :] * cot[...].astype(F)).astype(BF)
    gm_o[...] = gm
    gdb_o[...] = jnp.sum(gm.astype(F), axis=0, keepdims=True)


def attn_kernel(h1o, h1p, wt, cs, q_o, k_o, v_o, att_o, st_o, qm, st):
    rows = h1o.shape[0]
    width = q_o.shape[1]
    heads = width // HD
    cos, sin = tables(cs[0:rows, :], heads)
    q = nt(h1o[...], wt[0:width, :])
    q = (q * cos + halves_turned(q) * sin).astype(BF)
    q_o[...] = q
    qf = q.astype(F)
    lane_q = lax.broadcasted_iota(jnp.int32, (rows, width), 1) // HD
    for h in range(heads):
        qm[h] = jnp.where(lane_q == h, qf, 0.0).astype(BF)
    k = nt(h1o[...], wt[width : 2 * width, :])
    k_o[0:rows, :] = (k * cos + halves_turned(k) * sin).astype(BF)
    v_o[0:rows, :] = nt(h1o[...], wt[2 * width : 3 * width, :]).astype(BF)
    cos, sin = tables(cs[rows : 2 * rows, :], heads)
    k = nt(h1p[...], wt[width : 2 * width, :])
    k_o[rows : 2 * rows, :] = (k * cos + halves_turned(k) * sin).astype(BF)
    v_o[rows : 2 * rows, :] = nt(h1p[...], wt[2 * width : 3 * width, :]).astype(BF)
    tile = 256
    lane = lax.broadcasted_iota(jnp.int32, (tile, width), 1) // HD
    lane_s = lax.broadcasted_iota(jnp.int32, (tile, 128), 1)

    def body(i, carry):
        rs = pl.ds(pl.multiple_of(i * tile, tile), tile)
        acc = jnp.zeros((tile, width), F)
        stats = jnp.zeros((tile, 128), F)
        for h in range(heads):
            s = nt(qm[h, rs, :], k_o[...])
            m = jnp.max(s, axis=1, keepdims=True)
            e = jnp.exp2((s - m) * EXP_SCALE)
            total = jnp.sum(e, axis=1, keepdims=True)
            p = (e * (1.0 / total)).astype(BF)
            o = nn(p, v_o[...])
            acc = jnp.where(lane == h, o, acc)
            stats = jnp.where(lane_s == h, m * EXP_SCALE + jnp.log2(total), stats)
        att_o[rs, :] = acc.astype(BF)
        st[rs, :] = stats
        return carry

    lax.fori_loop(0, rows // tile, body, 0)
    st_o[...] = st[...].T[0:8, :]


def mid_kernel(a0, a1, a2, a3, w0, w1, w2, w3, tok, noised, mask, gain, mod, branch_o, mixed_o, h2_o):
    branch = nn(a0[...], w0[...]) + nn(a1[...], w1[...]) + nn(a2[...], w2[...]) + nn(a3[...], w3[...])
    inputs = jnp.where(noised[...] > 0.5, mask[...].astype(F), tok[...].astype(F))
    mixed = inputs + mod[2:3, :] * branch
    n2, _ = normalize(mixed)
    h2 = n2 * gain[...].astype(F) * (1.0 + mod[4:5, :]) + mod[3:4, :]
    branch_o[...] = branch
    mixed_o[...] = mixed
    h2_o[...] = h2.astype(BF)


def mlp_kernel(has_acc, has_add, h2, gm, wu, bu, wd, *refs):
    refs = list(refs)
    if has_acc:
        bin_, gin = refs[0], refs[1]
        refs = refs[2:]
    if has_add:
        dda, dua = refs[0], refs[1]
        refs = refs[2:]
    b_o, g_o, dd_o, du_o, gub_o = refs
    u = nn(h2[...], wu[...]) + bu[...].astype(F)
    th = jnp.tanh(GELU_COEF * (u + CUBIC_COEF * u * u * u))
    act = (0.5 * u * (1.0 + th)).astype(BF)
    slope = 0.5 * (1.0 + th) + 0.5 * u * (1.0 - th * th) * GELU_COEF * (1.0 + 3.0 * CUBIC_COEF * u * u)
    ga = nt(gm[...], wd[...])
    gu_f = (ga * slope).astype(BF).astype(F)
    gu = gu_f.astype(BF)
    gub_o[...] = jnp.sum(gu_f, axis=0, keepdims=True)
    b_new = nn(act, wd[...])
    g_new = nt(gu, wu[...])
    first = pl.program_id(0) == 0

    @pl.when(first)
    def _():
        if has_acc:
            b_o[...] = bin_[...] + b_new
            g_o[...] = gin[...] + g_new
        else:
            b_o[...] = b_new
            g_o[...] = g_new

    @pl.when(jnp.logical_not(first))
    def _():
        b_o[...] += b_new
        g_o[...] += g_new

    dd = tn(act, gm[...])
    du = tn(h2[...], gu)
    if has_add:
        dd = dd + dda[...].astype(F)
        du = du + dua[...].astype(F)
    dd_o[...] = dd.astype(dd_o.dtype)
    du_o[...] = du.astype(du_o.dtype)


def mlp_part(h2, gm, wu, bu, wd, acc, add, dtype, name):
    rows, d = h2.shape
    hidden = wu.shape[1]
    hc = 256
    const = lambda i: (0, 0)
    full = pl.BlockSpec((rows, d), const)
    up = pl.BlockSpec((d, hc), lambda i: (0, i))
    down = pl.BlockSpec((hc, d), lambda i: (i, 0))
    vec = pl.BlockSpec((1, hc), lambda i: (0, i))
    args = [h2, gm, wu, bu, wd]
    specs = [full, full, up, vec, down]
    aliases = {}
    if acc is not None:
        aliases = {5: 0, 6: 1}
        args += list(acc)
        specs += [full, full]
    if add is not None:
        args += list(add)
        specs += [down, up]
    return call(
        functools.partial(mlp_kernel, acc is not None, add is not None),
        [sds((rows, d), F), sds((rows, d), F), sds((hidden, d), dtype), sds((d, hidden), dtype), sds((1, hidden), F)],
        args,
        12 * rows * d * hidden,
        grid=(hidden // hc,),
        in_specs=specs,
        out_specs=[full, full, down, up, vec],
        aliases=aliases,
        name=name,
    )


def post_kernel(bm, gh, mixed, cot, branch, a0, a1, a2, a3, w0, w1, w2, w3, gain, mod, db, out_o, gmix_o, ga0, ga1, ga2, ga3, dw_o, sums_o):
    n2, inv = normalize(mixed[...])
    gain2 = gain[...].astype(F)
    scale1 = 1.0 + mod[4:5, :]
    c = cot[...].astype(F)
    bmlp = bm[...] + db[...].astype(F)
    out_o[...] = (mixed[...] + mod[5:6, :] * bmlp).astype(BF)
    g = gh[...]
    gs = g * scale1
    grad_mixed = c + layer_back(gs * gain2, n2, inv)
    gmix_o[...] = grad_mixed
    rows = [
        jnp.sum(gs * n2, axis=0, keepdims=True),
        jnp.sum(grad_mixed * branch[...], axis=0, keepdims=True),
        jnp.sum(g, axis=0, keepdims=True),
        jnp.sum(g * n2 * gain2, axis=0, keepdims=True),
        jnp.sum(c * bmlp, axis=0, keepdims=True),
    ]
    sums = jnp.concatenate(rows + [jnp.zeros((3, g.shape[1]), F)], axis=0)
    gba = (mod[2:3, :] * grad_mixed).astype(BF)
    wide = a0.shape[1]
    first = pl.program_id(0) == 0
    for r, (a, w, ga) in enumerate(((a0, w0, ga0), (a1, w1, ga1), (a2, w2, ga2), (a3, w3, ga3))):
        ga[...] = nt(gba, w[...]).astype(BF)
        dw = tn(a[...], gba)
        place = pl.ds(r * wide, wide)

        @pl.when(first)
        def _():
            dw_o[place, :] = dw

        @pl.when(jnp.logical_not(first))
        def _():
            dw_o[place, :] += dw

    @pl.when(first)
    def _():
        sums_o[...] = sums

    @pl.when(jnp.logical_not(first))
    def _():
        sums_o[...] += sums


def back_kernel(q, k, v, go, st, cs, dq_o, own_o, par_o, dk, dv, km, dq):
    rows, width = q.shape
    heads = width // HD
    keys = k.shape[0]
    kf = k[...].astype(F)
    lane_k = lax.broadcasted_iota(jnp.int32, (keys, width), 1) // HD
    for h in range(heads):
        km[h] = jnp.where(lane_k == h, kf, 0.0).astype(BF)
    dk[...] = jnp.zeros_like(dk)
    dv[...] = jnp.zeros_like(dv)
    tile = 256
    lane = lax.broadcasted_iota(jnp.int32, (tile, width), 1) // HD

    def body(i, carry):
        rs = pl.ds(pl.multiple_of(i * tile, tile), tile)
        qt = q[rs, :].astype(F)
        gt = go[rs, :].astype(F)
        acc = jnp.zeros((tile, width), F)
        for h in range(heads):
            qm = jnp.where(lane == h, qt, 0.0).astype(BF)
            gm = jnp.where(lane == h, gt, 0.0).astype(BF)
            s = nt(k[...], qm)
            p = jnp.exp2(s * EXP_SCALE - st[h : h + 1, rs])
            dp = nt(v[...], gm)
            inner = jnp.sum(p * dp, axis=0, keepdims=True)
            ds = (p * (dp - inner)).astype(BF)
            dv[...] += nn(p.astype(BF), gm)
            dk[...] += nn(ds, qm)
            acc = acc + tn(ds, km[h])
        dq[rs, :] = acc
        return carry

    lax.fori_loop(0, rows // tile, body, 0)
    cos, sin = tables(cs[...], heads)
    g = dq[...] * SCALE
    dq_o[...] = (g * cos + halves_back(g * sin)).astype(BF)
    own_o[...] = jnp.concatenate([dk[0:rows, :] * SCALE, dv[0:rows, :]], axis=1)
    par_o[...] = jnp.concatenate([dk[rows : 2 * rows, :] * SCALE, dv[rows : 2 * rows, :]], axis=1)


def proj_kernel(has_acc, has_add, dq, own, rcv, cs, h1, wt, *refs):
    refs = list(refs)
    if has_acc:
        gin = refs.pop(0)
    if has_add:
        dwa = refs.pop(0)
    g_o, dw_o = refs
    width = dq.shape[1]
    cos, sin = tables(cs[...], width // HD)
    gkv = own[...] + rcv[...]
    gk = gkv[:, :width]
    gk = (gk * cos + halves_back(gk * sin)).astype(BF)
    gv = gkv[:, width:].astype(BF)
    parts = (dq[...], gk, gv)
    g = gin[...] if has_acc else 0.0
    for i, part in enumerate(parts):
        place = slice(i * width, (i + 1) * width)
        g = g + nn(part, wt[place, :])
        dw = tn(part, h1[...])
        if has_add:
            dw = dw + dwa[place, :].astype(F)
        dw_o[place, :] = dw.astype(dw_o.dtype)
    g_o[...] = g


def tail_kernel(gh, gmix, tok, noised, mask, gain, mod, gt_o, sums_o):
    mask_on = noised[...] > 0.5
    inputs = jnp.where(mask_on, mask[...].astype(F), tok[...].astype(F))
    n1, inv = normalize(inputs)
    gain1 = gain[...].astype(F)
    g = gh[...]
    gs = g * (1.0 + mod[1:2, :])
    gi = gmix[...] + layer_back(gs * gain1, n1, inv)
    gt_o[...] = jnp.where(mask_on, 0.0, gi)
    rows = [
        jnp.sum(gs * n1, axis=0, keepdims=True),
        jnp.sum(jnp.where(mask_on, gi, 0.0), axis=0, keepdims=True),
        jnp.sum(g, axis=0, keepdims=True),
        jnp.sum(g * n1 * gain1, axis=0, keepdims=True),
    ]
    sums_o[...] = jnp.concatenate(rows + [jnp.zeros((4, g.shape[1]), F)], axis=0)


def swap(value, axis, bit):
    return lax.ppermute(value, axis, [(i, i ^ bit) for i in range(lax.axis_size(axis))])


def bit_of(index, bit):
    return (index // bit) % 2


def joined(mine, other, bit, axis=0):
    return jnp.where(bit == 0, jnp.concatenate([mine, other], axis), jnp.concatenate([other, mine], axis))


def reduce_dp(total, dp, n_dp):
    rows = total.shape[0]
    bits = []
    step = 1
    while step < n_dp:
        bits.append(step)
        step *= 2
    halved = bits[:3]
    for b in halved:
        rows //= 2
        mine = bit_of(dp, b)
        keep = lax.dynamic_slice_in_dim(total, mine * rows, rows, 0)
        send = lax.dynamic_slice_in_dim(total, (1 - mine) * rows, rows, 0).astype(BF)
        total = keep + swap(send, "dp", b).astype(F)
    for b in bits[3:]:
        total = total + swap(total, "dp", b)
    out = total.astype(BF)
    for b in reversed(halved):
        out = joined(out, swap(out, "dp", b), bit_of(dp, b))
    return out.astype(F)


def rotary_block():
    freq = np.float32(10000.0) ** (np.float32(-2.0) * np.arange(HD // 2, dtype=np.float32) / np.float32(HD))
    angle = np.arange(LEN, dtype=np.float32)[:, None] * freq[None, :].astype(np.float32)
    angle = np.concatenate([angle, angle], axis=1)
    return np.concatenate([np.cos(angle), np.sin(angle)], axis=1).astype(np.float32)


def per_device(tokens, time_emb, prefix_len, noise_mask, mask_embed, gain_attn, gain_mlp, ada_weight, ada_bias, qkv_weight, out_weight, up_weight, up_bias, down_weight, down_bias, cotangent):
    rows, d = tokens.shape
    n_dp = lax.axis_size("dp")
    assert lax.axis_size("tensor") == 4 and time_emb.shape[0] == 2 and 2 * rows == LEN
    t = lax.axis_index("tensor")
    dp = lax.axis_index("dp")
    xb, cb = t // 2, t % 2
    width = qkv_weight.shape[2]

    wt = qkv_weight.transpose(1, 2, 0).reshape(3 * width, d)
    bu = up_bias.reshape(1, -1)
    own = (wt, out_weight, up_weight, down_weight, bu)
    near = tuple(swap(w, "tensor", 1) for w in own)
    far = tuple(swap(w, "tensor", 2) for w in own)
    far_near = tuple(swap(w, "tensor", 1) for w in far)
    wts, wos, wus, wds, bus = zip(own, near, far, far_near)

    position = cb * rows + jnp.arange(rows, dtype=jnp.int32)
    prefix = lax.dynamic_slice_in_dim(prefix_len, xb, 1, 0)
    noised = ((noise_mask == 1) & (position >= prefix)).astype(F).reshape(rows, 1)
    time_row = lax.dynamic_slice_in_dim(time_emb, xb, 1, 0)
    table = jnp.asarray(rotary_block())
    cs = jnp.where(cb == 0, table, jnp.concatenate([table[rows:], table[:rows]], axis=0))
    cs_own = cs[:rows]
    vec = lambda v: v.reshape(1, -1)
    mask, gain1, gain2, db = vec(mask_embed), vec(gain_attn), vec(gain_mlp), vec(down_bias)

    mod, h1, gm, g_db = call(
        head_kernel,
        [sds((6, d), F), sds((rows, d), BF), sds((rows, d), BF), sds((1, d), F)],
        [tokens, noised, cotangent, mask, gain1, time_row, ada_weight, vec(ada_bias)],
        2 * 48 * 128 * 6 * d,
        name="head",
    )
    h1p = swap(h1, "tensor", 1)

    fwd = []
    for r in range(4):
        fwd.append(
            call(
                attn_kernel,
                [sds((rows, width), BF), sds((2 * rows, width), BF), sds((2 * rows, width), BF), sds((rows, width), BF), sds((8, rows), F)],
                [h1, h1p, wts[r], cs],
                2 * rows * d * width * 5 + 4 * rows * 2 * rows * 256 * 3,
                scratch=[pltpu.VMEM((width // HD, rows, width), BF), pltpu.VMEM((rows, 128), F)],
                name=f"attn{r}",
            )
        )
    atts = [f[3] for f in fwd]

    tile = 256
    tiled = lambda w: pl.BlockSpec((tile, w), lambda i: (i, 0))
    fixed = lambda a: pl.BlockSpec(a.shape, lambda i: (0, 0))
    branch, mixed, h2 = call(
        mid_kernel,
        [sds((rows, d), F), sds((rows, d), F), sds((rows, d), BF)],
        atts + list(wos) + [tokens, noised, mask, gain2, mod],
        2 * rows * d * 4 * width,
        grid=(rows // tile,),
        in_specs=[tiled(width)] * 4 + [fixed(w) for w in wos] + [tiled(d), tiled(1), fixed(mask), fixed(gain2), fixed(mod)],
        out_specs=[tiled(d)] * 3,
        name="mid",
    )

    b1, g1, dd1, du1, gub1 = mlp_part(h2, gm, wus[1], bus[1], wds[1], None, None, BF, "mlp1")
    add0 = (swap(dd1, "tensor", 1), swap(du1, "tensor", 1))
    b3, g3, dd3, du3, gub3 = mlp_part(h2, gm, wus[3], bus[3], wds[3], (b1, g1), None, BF, "mlp3")
    add2 = (swap(dd3, "tensor", 1), swap(du3, "tensor", 1))
    b2, g2, dd2, du2, gub2 = mlp_part(h2, gm, wus[2], bus[2], wds[2], (b3, g3), add2, BF, "mlp2")
    b0, g0, dd0, du0, gub0 = mlp_part(h2, gm, wus[0], bus[0], wds[0], (b2, g2), add0, F, "mlp0")
    down_total = dd0 + swap(dd2, "tensor", 2).astype(F)
    up_total = du0 + swap(du2, "tensor", 2).astype(F)
    grad_down = reduce_dp(down_total, dp, n_dp)
    grad_up = reduce_dp(up_total, dp, n_dp)

    post = call(
        post_kernel,
        [sds((rows, d), BF), sds((rows, d), F)] + [sds((rows, width), BF)] * 4 + [sds((4 * width, d), F), sds((8, d), F)],
        [b0, g0, mixed, cotangent, branch] + atts + list(wos) + [gain2, mod, db],
        4 * rows * d * 4 * width,
        grid=(rows // tile,),
        in_specs=[tiled(d)] * 5 + [tiled(width)] * 4 + [fixed(w) for w in wos] + [fixed(gain2), fixed(mod), fixed(db)],
        out_specs=[tiled(d)] * 2 + [tiled(width)] * 4 + [pl.BlockSpec((4 * width, d), lambda i: (0, 0)), pl.BlockSpec((8, d), lambda i: (0, 0))],
        name="post",
    )
    output, grad_mixed = post[0], post[1]
    g_att = post[2:6]
    dwo, sums_two = post[6], post[7]
    part = lambda r: dwo[r * width : (r + 1) * width]
    o1 = swap(part(1).astype(BF), "tensor", 1)
    o3 = swap(part(3).astype(BF), "tensor", 1)
    o2 = swap((part(2) + o3.astype(F)).astype(BF), "tensor", 2)
    grad_out = reduce_dp(part(0) + o1.astype(F) + o2.astype(F), dp, n_dp)

    gh1 = None
    dws = {}
    for pair in ((3, 2), (1, 0)):
        backs = {}
        for r in pair:
            q, k, v, _, st = fwd[r]
            backs[r] = call(
                back_kernel,
                [sds((rows, width), BF), sds((rows, 2 * width), F), sds((rows, 2 * width), F)],
                [q, k, v, g_att[r], st, cs_own],
                10 * rows * 2 * rows * 256 * 3,
                scratch=[pltpu.VMEM((2 * rows, width), F), pltpu.VMEM((2 * rows, width), F), pltpu.VMEM((width // HD, 2 * rows, width), BF), pltpu.VMEM((rows, width), F)],
                name=f"back{r}",
            )
        for r in pair:
            dq, own_kv, _ = backs[r]
            rcv_kv = swap(backs[r ^ 1][2], "tensor", 1)
            args = [dq, own_kv, rcv_kv, cs_own, h1, wts[r]]
            aliases = {}
            if gh1 is not None:
                aliases = {len(args): 0}
                args.append(gh1)
            add = {2: 3, 0: 1}.get(r)
            if add is not None:
                args.append(swap(dws[add], "tensor", 1))
            gh1, dws[r] = call(
                functools.partial(proj_kernel, gh1 is not None, add is not None),
                [sds((rows, d), F), sds((3 * width, d), F if r == 0 else BF)],
                args,
                4 * rows * d * 3 * width,
                aliases=aliases,
                name=f"proj{r}",
            )
    qkv_total = dws[0] + swap(dws[2], "tensor", 2).astype(F)
    grad_qkv = reduce_dp(qkv_total, dp, n_dp).reshape(3, width, d).transpose(2, 0, 1)

    grad_tokens, sums_one = call(
        tail_kernel,
        [sds((rows, d), F), sds((8, d), F)],
        [gh1, grad_mixed, tokens, noised, mask, gain1, mod],
        10 * rows * d,
        name="tail",
    )

    hid = jnp.concatenate([gub0, gub1, gub2, gub3], axis=0)
    mods = jnp.concatenate([sums_one[2:4], sums_two[1:5]], axis=0)
    shared = jnp.concatenate([sums_one[0:2], sums_two[0:1], g_db], axis=0)
    got = swap(jnp.concatenate([hid[1:2], hid[3:4], shared, mods], axis=0), "tensor", 1)
    hid = hid[0::2] + got[0:2]
    shared = shared + got[2:6]
    mods = mods + got[6:]
    got = swap(jnp.concatenate([hid[1:2], shared, mods], axis=0), "tensor", 2)
    shared = jnp.concatenate([hid[0:1] + got[0:1], shared + got[1:5]], axis=0)
    mods = joined(mods[None], got[5:][None], xb)
    pair_mods = mods.reshape(2, 6 * d)
    times = time_emb
    step = 1
    while step < n_dp:
        got = swap(jnp.concatenate([shared, mods.reshape(-1, d)], axis=0), "dp", step)
        shared = shared + got[0:5]
        mods = joined(mods, got[5:].reshape(mods.shape), bit_of(dp, step))
        times = joined(times, swap(times, "dp", step), bit_of(dp, step))
        step *= 2
    mods = mods.reshape(-1, 6 * d)
    ada_full = ada_weight.astype(F)
    tv = time_emb.astype(F)
    sig = jax.nn.sigmoid(tv)
    grad_time = matmul_high(pair_mods, ada_full.T) * sig * (1.0 + tv * (1.0 - sig))
    silu = jax.nn.silu(times.astype(F))
    grad_ada_weight = lax.dot_general(silu, mods, (((0,), (0,)), ((), ())), precision=lax.Precision.HIGHEST, preferred_element_type=F)
    grad_ada_bias = jnp.sum(mods, axis=0)
    return (
        output,
        grad_tokens,
        grad_time,
        shared[2],
        shared[1],
        shared[3],
        grad_ada_weight,
        grad_ada_bias,
        grad_qkv,
        grad_out,
        grad_up,
        shared[0],
        grad_down,
        shared[4],
    )


def solution(mesh):
    group = ("dp", "tensor")
    in_specs = (P(group, None), P("dp", None), P("dp"), P(group), P(), P(), P(), P(), P(), P(None, None, "tensor"), P("tensor", None), P(None, "tensor"), P("tensor"), P("tensor", None), P(), P(group, None))
    out_specs = (P(group, None), P(group, None), P("dp", None), P(), P(), P(), P(), P(), P(None, None, "tensor"), P("tensor", None), P(None, "tensor"), P("tensor"), P("tensor", None), P())
    return jax.shard_map(per_device, mesh=mesh, in_specs=in_specs, out_specs=out_specs, check_vma=False)
```

```python
import functools

import jax
import jax.numpy as jnp
import numpy as np
from jax import lax
from jax.experimental import pallas as pl
from jax.experimental.pallas import tpu as pltpu
from jax.sharding import PartitionSpec as P

BF = jnp.bfloat16
F = jnp.float32
HD = 64
LEN = 1024
EPS = 1e-05
GELU_COEF = 0.7978845608028654
CUBIC_COEF = 0.044715
SCALE = 0.125
LOG2E = 1.4426950408889634
EXP_SCALE = SCALE * LOG2E
MIB = 1 << 20


def nn(a, b):
    return lax.dot_general(a, b, (((1,), (0,)), ((), ())), preferred_element_type=F)


def nt(a, b):
    return lax.dot_general(a, b, (((1,), (1,)), ((), ())), preferred_element_type=F)


def tn(a, b):
    return lax.dot_general(a, b, (((0,), (0,)), ((), ())), preferred_element_type=F)


def matmul_high(left, right):
    return jnp.dot(left, right, precision=lax.Precision.HIGHEST, preferred_element_type=F)


def normalize(values):
    centered = values - jnp.mean(values, axis=-1, keepdims=True)
    inv = lax.rsqrt(jnp.mean(centered * centered, axis=-1, keepdims=True) + EPS)
    return centered * inv, inv


def layer_back(grad_norm, normed, inv):
    mean_grad = jnp.mean(grad_norm, axis=-1, keepdims=True)
    mean_cross = jnp.mean(grad_norm * normed, axis=-1, keepdims=True)
    return inv * (grad_norm - mean_grad - normed * mean_cross)


def halves_turned(v):
    parts = []
    for h in range(v.shape[1] // HD):
        lo = v[:, h * HD : h * HD + HD // 2]
        hi = v[:, h * HD + HD // 2 : (h + 1) * HD]
        parts += [-hi, lo]
    return jnp.concatenate(parts, axis=1)


def halves_back(v):
    parts = []
    for h in range(v.shape[1] // HD):
        lo = v[:, h * HD : h * HD + HD // 2]
        hi = v[:, h * HD + HD // 2 : (h + 1) * HD]
        parts += [hi, -lo]
    return jnp.concatenate(parts, axis=1)


def tables(block, heads):
    cos, sin = block[:, :HD], block[:, HD:]
    return jnp.concatenate([cos] * heads, axis=1), jnp.concatenate([sin] * heads, axis=1)


def call(kernel, outs, args, flops, grid=None, in_specs=None, out_specs=None, scratch=(), aliases=None, vmem=48, name=None):
    nbytes = sum(a.size * a.dtype.itemsize for a in args) + sum(o.size * o.dtype.itemsize for o in outs)
    kwargs = {}
    if grid is not None:
        kwargs["grid"] = grid
    if in_specs is None:
        in_specs = [pl.BlockSpec(memory_space=pltpu.VMEM)] * len(args)
    if out_specs is None:
        out_specs = [pl.BlockSpec(memory_space=pltpu.VMEM)] * len(outs)
    return pl.pallas_call(
        kernel,
        out_shape=tuple(outs),
        in_specs=in_specs,
        out_specs=tuple(out_specs),
        scratch_shapes=list(scratch),
        input_output_aliases=aliases or {},
        compiler_params=pltpu.CompilerParams(vmem_limit_bytes=vmem * MIB),
        cost_estimate=pl.CostEstimate(flops=flops, bytes_accessed=nbytes, transcendentals=0),
        name=name,
        **kwargs,
    )(*args)


def sds(shape, dtype):
    return jax.ShapeDtypeStruct(shape, dtype)


PIECE = 192
N_PIECES = 12
HALF = PIECE // 2
MESH = pl.DeviceIdType.MESH


def forward_kernel(
    tok_h, cot_h, noise, prefix, vecs, time, ada_h, table_h, wt_h, wo_h, wu_h, wd_h, bu,
    q_o, k_o, v_o, att_o, st_o, h1_o, gm_o, branch_o, mixed_o, h2_o, w_o, mod_o, gdb_o, nz_o, bus_o,
    w, tok, cot, ada, cs, h1o, h1p, q, k, v, att, st, qm, st_col, branch, mixed, h2, gm,
    loc, xs, xr, ys, yr, cs_s, cs_r, ns, nr, hs, hr, bs, br, outs,
):
    rows, d = tok.shape
    width = q.shape[2]
    heads = width // HD
    dp = lax.axis_index("dp")
    t = lax.axis_index("tensor")
    xb, cb, yb = t // 2, t % 2, dp % 2
    core = (dp, t + 1 - 2 * cb)
    chip = (dp, t + 2 - 4 * xb)
    side = (dp + 1 - 2 * yb, t)
    sources = [(wt_h, i * PIECE) for i in range(3)] + [(wo_h, 0)]
    sources += [(wu_h, i * PIECE) for i in range(4)] + [(wd_h, i * PIECE) for i in range(4)]

    barrier = pltpu.get_barrier_semaphore()
    for other in (core, chip, side):
        pl.semaphore_signal(barrier, inc=1, device_id=other, device_id_type=MESH)
    pl.semaphore_wait(barrier, 3)

    def remote(src, dst, send, recv, to):
        return pltpu.make_async_remote_copy(src_ref=src, dst_ref=dst, send_sem=send, recv_sem=recv, device_id=to, device_id_type=MESH)

    def half(j, which):
        return pl.ds(pl.multiple_of(j * PIECE + which * HALF, 32), HALF)

    def far_send(j):
        src, base = sources[j]
        return remote(src.at[pl.ds(pl.multiple_of(base + yb * HALF, 32), HALF)], w.at[2, half(j, yb)], xs.at[j], xr.at[j], chip)

    def far_wait(j):
        return remote(w.at[2, half(j, yb)], w.at[2, half(j, yb)], xs.at[j], xr.at[j], chip)

    def side_copy(j):
        return remote(w.at[2, half(j, yb)], w.at[2, half(j, yb)], ys.at[j], yr.at[j], side)

    def core_copy(j, which):
        return remote(w.at[2, half(j, (yb + which) % 2)], w.at[3, half(j, (yb + which) % 2)], cs_s.at[j, which], cs_r.at[j, which], core)

    def near_copy(j):
        src, base = sources[j]
        return remote(src.at[pl.ds(base, PIECE)], w.at[1, pl.ds(j * PIECE, PIECE)], ns.at[j], nr.at[j], core)

    own_copies = [pltpu.make_async_copy(tok_h, tok, loc.at[0]), pltpu.make_async_copy(ada_h, ada, loc.at[1])]
    own_copies += [pltpu.make_async_copy(cot_h, cot, loc.at[2])]
    own_copies += [pltpu.make_async_copy(table_h.at[pl.ds(pl.multiple_of(cb * rows, rows), rows)], cs.at[pl.ds(0, rows)], loc.at[3])]
    own_copies += [pltpu.make_async_copy(table_h.at[pl.ds(pl.multiple_of((1 - cb) * rows, rows), rows)], cs.at[pl.ds(rows, rows)], loc.at[4])]
    for c in own_copies:
        c.start()
    far_send(0).start()
    far_send(1).start()
    own_w = []
    for i, (ref, start) in enumerate(((wt_h, 0), (wo_h, 3 * PIECE), (wu_h, 4 * PIECE), (wd_h, 8 * PIECE))):
        own_w.append(pltpu.make_async_copy(ref, w.at[0, pl.ds(start, ref.shape[0])], loc.at[5 + i]))
        own_w[-1].start()
    for j in range(3):
        near_copy(j).start()
    bus_o[0] = bu[...]
    bias_far = remote(bu, bus_o.at[2], bs.at[0], br.at[0], chip)
    bias_near = remote(bu, bus_o.at[1], bs.at[1], br.at[1], core)
    bias_far.start()
    bias_near.start()

    tv = jnp.where(xb == 0, time[0:1, :].astype(F), time[1:2, :].astype(F))
    tv = jnp.broadcast_to(tv, (16, tv.shape[1]))
    s = tv / (1.0 + jnp.exp(-tv))
    hi = s.astype(BF).astype(F)
    mid = (s - hi).astype(BF).astype(F)
    low = (s - hi - mid).astype(BF).astype(F)
    stacked = jnp.concatenate([hi, mid, low], axis=0).astype(BF)
    own_copies[1].wait()
    for i in range(6):
        m = nn(stacked, ada[:, pl.ds(i * d, d)])
        mod_o[i : i + 1, :] = m[0:1] + m[16:17] + m[32:33] + vecs[8 + i : 9 + i, :]
    place = lax.broadcasted_iota(jnp.int32, (4, 128), 0) * 128 + lax.broadcasted_iota(jnp.int32, (4, 128), 1) + cb * rows
    limit = jnp.where(xb == 0, prefix[0], prefix[1])
    on = jnp.where((noise[...] == 1) & (place >= limit), 1.0, 0.0)
    on = jnp.concatenate([on, jnp.zeros((12, 128), F)], axis=0).astype(BF)
    eye = jnp.where(lax.broadcasted_iota(jnp.int32, (128, 128), 0) == lax.broadcasted_iota(jnp.int32, (128, 128), 1), 1.0, 0.0).astype(BF)
    cols = nt(eye, on)
    for i in range(4):
        nz_o[i * 128 : (i + 1) * 128, :] = cols[:, i : i + 1]
    own_copies[0].wait()
    inputs = jnp.where(nz_o[...] > 0.5, vecs[0:1, :], tok[...].astype(F))
    n1, _ = normalize(inputs)
    h1o[...] = (n1 * vecs[1:2, :] * (1.0 + mod_o[1:2, :]) + mod_o[0:1, :]).astype(BF)
    h1_copy = remote(h1o, h1p, hs.at[0], hr.at[0], core)
    h1_copy.start()
    own_copies[2].wait()
    gmv = (mod_o[5:6, :] * cot[...].astype(F)).astype(BF)
    gm[...] = gmv
    gdb_o[...] = jnp.sum(gmv.astype(F), axis=0, keepdims=True)
    own_copies[3].wait()
    own_copies[4].wait()
    own_w[0].wait()
    h1_copy.wait()
    for j in range(3, N_PIECES):
        near_copy(j).start()
    bias_far.wait_recv()
    bias_cross = remote(bus_o.at[2], bus_o.at[3], bs.at[2], br.at[2], core)
    bias_cross.start()

    def arrived(j):
        far_wait(j).wait_recv()
        if j + 2 < N_PIECES:
            far_send(j + 2).start()
        side_copy(j).start()
        core_copy(j, 0).start()

    def passed(j):
        side_copy(j).wait_recv()
        core_copy(j, 1).start()

    tile = 256
    lane_q = lax.broadcasted_iota(jnp.int32, (rows, width), 1) // HD
    lane = lax.broadcasted_iota(jnp.int32, (tile, width), 1) // HD
    lane_s = lax.broadcasted_iota(jnp.int32, (tile, 128), 1)

    def project(r):
        cos, sin = tables(cs[0:rows, :], heads)
        qv = nt(h1o[...], w[r, 0:width, :])
        qv = (qv * cos + halves_turned(qv) * sin).astype(BF)
        q[r] = qv
        qf = qv.astype(F)
        for h in range(heads):
            qm[h] = jnp.where(lane_q == h, qf, 0.0).astype(BF)
        kv = nt(h1o[...], w[r, width : 2 * width, :])
        k[r, 0:rows, :] = (kv * cos + halves_turned(kv) * sin).astype(BF)
        v[r, 0:rows, :] = nt(h1o[...], w[r, 2 * width : 3 * width, :]).astype(BF)
        cos, sin = tables(cs[rows : 2 * rows, :], heads)
        kv = nt(h1p[...], w[r, width : 2 * width, :])
        k[r, rows : 2 * rows, :] = (kv * cos + halves_turned(kv) * sin).astype(BF)
        v[r, rows : 2 * rows, :] = nt(h1p[...], w[r, 2 * width : 3 * width, :]).astype(BF)

    def attend(r, i):
        rs = pl.ds(pl.multiple_of(i * tile, tile), tile)
        acc = jnp.zeros((tile, width), F)
        stats = jnp.zeros((tile, 128), F)
        for h in range(heads):
            s = nt(qm[h, rs, :], k[r])
            m = jnp.max(s, axis=1, keepdims=True)
            e = jnp.exp2((s - m) * EXP_SCALE)
            total = jnp.sum(e, axis=1, keepdims=True)
            p = (e * (1.0 / total)).astype(BF)
            o = nn(p, v[r])
            acc = jnp.where(lane == h, o, acc)
            stats = jnp.where(lane_s == h, m * EXP_SCALE + jnp.log2(total), stats)
        att[r, rs, :] = acc.astype(BF)
        st_col[rs, :] = stats

    done_in = done_side = 0
    for r in range(4):
        if r == 1:
            for j in range(3):
                near_copy(j).wait_recv()
        if r == 2:
            while done_side < 3:
                passed(done_side)
                done_side += 1
        if r == 3:
            for j in range(3):
                core_copy(j, 0).wait_recv()
                core_copy(j, 1).wait_recv()
        project(r)
        for i in range(rows // tile):
            arrived(done_in)
            done_in += 1
            if done_side < done_in - 2:
                passed(done_side)
                done_side += 1
            attend(r, i)
        st[r] = st_col[...].T[0:8, :]
    while done_in < N_PIECES:
        arrived(done_in)
        done_in += 1
    while done_side < N_PIECES:
        passed(done_side)
        done_side += 1
    own_w[1].wait()
    near_copy(3).wait_recv()
    core_copy(3, 0).wait_recv()
    core_copy(3, 1).wait_recv()

    @pl.loop(0, rows // tile)
    def _(i):
        rs = pl.ds(pl.multiple_of(i * tile, tile), tile)
        b = nn(att[0, rs, :], w[0, 576:768, :])
        for r in range(1, 4):
            b = b + nn(att[r, rs, :], w[r, 576:768, :])
        x = jnp.where(nz_o[rs, :] > 0.5, vecs[0:1, :], tok[rs, :].astype(F)) + mod_o[2:3, :] * b
        n2, _ = normalize(x)
        branch[rs, :] = b
        mixed[rs, :] = x
        h2[rs, :] = (n2 * vecs[2:3, :] * (1.0 + mod_o[4:5, :]) + mod_o[3:4, :]).astype(BF)

    own_w[2].wait()
    own_w[3].wait()
    for j in range(4, N_PIECES):
        near_copy(j).wait_recv()
        core_copy(j, 0).wait_recv()
        core_copy(j, 1).wait_recv()
    bias_near.wait()
    bias_far.wait_send()
    bias_cross.wait()
    for j in range(N_PIECES):
        far_wait(j).wait_send()
        side_copy(j).wait_send()
        core_copy(j, 0).wait_send()
        core_copy(j, 1).wait_send()
        near_copy(j).wait_send()
    out = []
    for i, (a, b) in enumerate(((q, q_o), (k, k_o), (v, v_o), (att, att_o), (st, st_o), (h1o, h1_o), (gm, gm_o), (branch, branch_o), (mixed, mixed_o), (h2, h2_o), (w, w_o))):
        out.append(pltpu.make_async_copy(a, b, outs.at[i]))
        out[-1].start()
    for c in out:
        c.wait()


def mlp_kernel(has_acc, has_add, h2, gm, wu, bu, wd, *refs):
    refs = list(refs)
    if has_acc:
        bin_, gin = refs[0], refs[1]
        refs = refs[2:]
    if has_add:
        dda, dua = refs[0], refs[1]
        refs = refs[2:]
    b_o, g_o, dd_o, du_o, gub_o = refs
    u = nn(h2[...], wu[...]) + bu[...].astype(F)
    th = jnp.tanh(GELU_COEF * (u + CUBIC_COEF * u * u * u))
    act = (0.5 * u * (1.0 + th)).astype(BF)
    slope = 0.5 * (1.0 + th) + 0.5 * u * (1.0 - th * th) * GELU_COEF * (1.0 + 3.0 * CUBIC_COEF * u * u)
    ga = nt(gm[...], wd[...])
    gu_f = (ga * slope).astype(BF).astype(F)
    gu = gu_f.astype(BF)
    gub_o[...] = jnp.sum(gu_f, axis=0, keepdims=True)
    b_new = nn(act, wd[...])
    g_new = nt(gu, wu[...])
    first = pl.program_id(0) == 0

    @pl.when(first)
    def _():
        if has_acc:
            b_o[...] = bin_[...] + b_new
            g_o[...] = gin[...] + g_new
        else:
            b_o[...] = b_new
            g_o[...] = g_new

    @pl.when(jnp.logical_not(first))
    def _():
        b_o[...] += b_new
        g_o[...] += g_new

    dd = tn(act, gm[...])
    du = tn(h2[...], gu)
    if has_add:
        dd = dd + dda[...].astype(F)
        du = du + dua[...].astype(F)
    dd_o[...] = dd.astype(dd_o.dtype)
    du_o[...] = du.astype(du_o.dtype)


def mlp_part(h2, gm, wu, bu, wd, acc, add, dtype, name):
    rows, d = h2.shape
    hidden = wu.shape[1]
    hc = 256
    const = lambda i: (0, 0)
    full = pl.BlockSpec((rows, d), const)
    up = pl.BlockSpec((d, hc), lambda i: (0, i))
    down = pl.BlockSpec((hc, d), lambda i: (i, 0))
    vec = pl.BlockSpec((1, hc), lambda i: (0, i))
    args = [h2, gm, wu, bu, wd]
    specs = [full, full, up, vec, down]
    aliases = {}
    if acc is not None:
        aliases = {5: 0, 6: 1}
        args += list(acc)
        specs += [full, full]
    if add is not None:
        args += list(add)
        specs += [down, up]
    return call(
        functools.partial(mlp_kernel, acc is not None, add is not None),
        [sds((rows, d), F), sds((rows, d), F), sds((hidden, d), dtype), sds((d, hidden), dtype), sds((1, hidden), F)],
        args,
        12 * rows * d * hidden,
        grid=(hidden // hc,),
        in_specs=specs,
        out_specs=[full, full, down, up, vec],
        aliases=aliases,
        name=name,
    )


def post_kernel(bm, gh, mixed, cot, branch, a0, a1, a2, a3, w0, w1, w2, w3, gain, mod, db, out_o, gmix_o, ga0, ga1, ga2, ga3, dw_o, sums_o):
    n2, inv = normalize(mixed[...])
    gain2 = gain[...].astype(F)
    scale1 = 1.0 + mod[4:5, :]
    c = cot[...].astype(F)
    bmlp = bm[...] + db[...].astype(F)
    out_o[...] = (mixed[...] + mod[5:6, :] * bmlp).astype(BF)
    g = gh[...]
    gs = g * scale1
    grad_mixed = c + layer_back(gs * gain2, n2, inv)
    gmix_o[...] = grad_mixed
    rows = [
        jnp.sum(gs * n2, axis=0, keepdims=True),
        jnp.sum(grad_mixed * branch[...], axis=0, keepdims=True),
        jnp.sum(g, axis=0, keepdims=True),
        jnp.sum(g * n2 * gain2, axis=0, keepdims=True),
        jnp.sum(c * bmlp, axis=0, keepdims=True),
    ]
    sums = jnp.concatenate(rows + [jnp.zeros((3, g.shape[1]), F)], axis=0)
    gba = (mod[2:3, :] * grad_mixed).astype(BF)
    wide = a0.shape[1]
    first = pl.program_id(0) == 0
    for r, (a, w, ga) in enumerate(((a0, w0, ga0), (a1, w1, ga1), (a2, w2, ga2), (a3, w3, ga3))):
        ga[...] = nt(gba, w[...]).astype(BF)
        dw = tn(a[...], gba)
        place = pl.ds(r * wide, wide)

        @pl.when(first)
        def _():
            dw_o[place, :] = dw

        @pl.when(jnp.logical_not(first))
        def _():
            dw_o[place, :] += dw

    @pl.when(first)
    def _():
        sums_o[...] = sums

    @pl.when(jnp.logical_not(first))
    def _():
        sums_o[...] += sums


def back_kernel(q, k, v, go, st, cs, dq_o, own_o, par_o, dk, dv, km, dq):
    rows, width = q.shape
    heads = width // HD
    keys = k.shape[0]
    kf = k[...].astype(F)
    lane_k = lax.broadcasted_iota(jnp.int32, (keys, width), 1) // HD
    for h in range(heads):
        km[h] = jnp.where(lane_k == h, kf, 0.0).astype(BF)
    dk[...] = jnp.zeros_like(dk)
    dv[...] = jnp.zeros_like(dv)
    tile = 256
    lane = lax.broadcasted_iota(jnp.int32, (tile, width), 1) // HD

    def body(i, carry):
        rs = pl.ds(pl.multiple_of(i * tile, tile), tile)
        qt = q[rs, :].astype(F)
        gt = go[rs, :].astype(F)
        acc = jnp.zeros((tile, width), F)
        for h in range(heads):
            qm = jnp.where(lane == h, qt, 0.0).astype(BF)
            gm = jnp.where(lane == h, gt, 0.0).astype(BF)
            s = nt(k[...], qm)
            p = jnp.exp2(s * EXP_SCALE - st[h : h + 1, rs])
            dp = nt(v[...], gm)
            inner = jnp.sum(p * dp, axis=0, keepdims=True)
            ds = (p * (dp - inner)).astype(BF)
            dv[...] += nn(p.astype(BF), gm)
            dk[...] += nn(ds, qm)
            acc = acc + tn(ds, km[h])
        dq[rs, :] = acc
        return carry

    lax.fori_loop(0, rows // tile, body, 0)
    cos, sin = tables(cs[...], heads)
    g = dq[...] * SCALE
    dq_o[...] = (g * cos + halves_back(g * sin)).astype(BF)
    own_o[...] = jnp.concatenate([dk[0:rows, :] * SCALE, dv[0:rows, :]], axis=1)
    par_o[...] = jnp.concatenate([dk[rows : 2 * rows, :] * SCALE, dv[rows : 2 * rows, :]], axis=1)


def proj_kernel(has_acc, has_add, dq, own, rcv, cs, h1, wt, *refs):
    refs = list(refs)
    if has_acc:
        gin = refs.pop(0)
    if has_add:
        dwa = refs.pop(0)
    g_o, dw_o = refs
    width = dq.shape[1]
    cos, sin = tables(cs[...], width // HD)
    gkv = own[...] + rcv[...]
    gk = gkv[:, :width]
    gk = (gk * cos + halves_back(gk * sin)).astype(BF)
    gv = gkv[:, width:].astype(BF)
    parts = (dq[...], gk, gv)
    g = gin[...] if has_acc else 0.0
    for i, part in enumerate(parts):
        place = slice(i * width, (i + 1) * width)
        g = g + nn(part, wt[place, :])
        dw = tn(part, h1[...])
        if has_add:
            dw = dw + dwa[place, :].astype(F)
        dw_o[place, :] = dw.astype(dw_o.dtype)
    g_o[...] = g


def tail_kernel(gh, gmix, tok, noised, mask, gain, mod, gt_o, sums_o):
    mask_on = noised[...] > 0.5
    inputs = jnp.where(mask_on, mask[...].astype(F), tok[...].astype(F))
    n1, inv = normalize(inputs)
    gain1 = gain[...].astype(F)
    g = gh[...]
    gs = g * (1.0 + mod[1:2, :])
    gi = gmix[...] + layer_back(gs * gain1, n1, inv)
    gt_o[...] = jnp.where(mask_on, 0.0, gi)
    rows = [
        jnp.sum(gs * n1, axis=0, keepdims=True),
        jnp.sum(jnp.where(mask_on, gi, 0.0), axis=0, keepdims=True),
        jnp.sum(g, axis=0, keepdims=True),
        jnp.sum(g * n1 * gain1, axis=0, keepdims=True),
    ]
    sums_o[...] = jnp.concatenate(rows + [jnp.zeros((4, g.shape[1]), F)], axis=0)


def swap(value, axis, bit):
    return lax.ppermute(value, axis, [(i, i ^ bit) for i in range(lax.axis_size(axis))])


def bit_of(index, bit):
    return (index // bit) % 2


def joined(mine, other, bit, axis=0):
    return jnp.where(bit == 0, jnp.concatenate([mine, other], axis), jnp.concatenate([other, mine], axis))


def reduce_dp(total, dp, n_dp):
    rows = total.shape[0]
    bits = []
    step = 1
    while step < n_dp:
        bits.append(step)
        step *= 2
    halved = bits[:3]
    for b in halved:
        rows //= 2
        mine = bit_of(dp, b)
        keep = lax.dynamic_slice_in_dim(total, mine * rows, rows, 0)
        send = lax.dynamic_slice_in_dim(total, (1 - mine) * rows, rows, 0).astype(BF)
        total = keep + swap(send, "dp", b).astype(F)
    for b in bits[3:]:
        total = total + swap(total, "dp", b)
    out = total.astype(BF)
    for b in reversed(halved):
        out = joined(out, swap(out, "dp", b), bit_of(dp, b))
    return out.astype(F)


def rotary_block():
    freq = np.float32(10000.0) ** (np.float32(-2.0) * np.arange(HD // 2, dtype=np.float32) / np.float32(HD))
    angle = np.arange(LEN, dtype=np.float32)[:, None] * freq[None, :].astype(np.float32)
    angle = np.concatenate([angle, angle], axis=1)
    return np.concatenate([np.cos(angle), np.sin(angle)], axis=1).astype(np.float32)


def per_device(tokens, time_emb, prefix_len, noise_mask, mask_embed, gain_attn, gain_mlp, ada_weight, ada_bias, qkv_weight, out_weight, up_weight, up_bias, down_weight, down_bias, cotangent):
    rows, d = tokens.shape
    n_dp = lax.axis_size("dp")
    assert lax.axis_size("tensor") == 4 and time_emb.shape[0] == 2 and 2 * rows == LEN
    t = lax.axis_index("tensor")
    dp = lax.axis_index("dp")
    xb, cb = t // 2, t % 2
    width = qkv_weight.shape[2]

    wt = qkv_weight.transpose(1, 2, 0).reshape(3 * width, d)
    table = jnp.asarray(rotary_block())
    vecs = jnp.concatenate([mask_embed, gain_attn, gain_mlp, down_bias, jnp.zeros((4 * d,), BF), ada_bias, jnp.zeros((2 * d,), BF)]).astype(F).reshape(16, d)
    bu16 = jnp.broadcast_to(up_bias.astype(F)[None], (8, up_bias.shape[0]))
    anyspace = pl.BlockSpec(memory_space=pl.ANY)
    vspace = pl.BlockSpec(memory_space=pltpu.VMEM)
    sspace = pl.BlockSpec(memory_space=pltpu.SMEM)
    vm = pltpu.VMEM
    dma = pltpu.SemaphoreType.DMA
    handed = [
        sds((4, rows, width), BF), sds((4, 2 * rows, width), BF), sds((4, 2 * rows, width), BF), sds((4, rows, width), BF), sds((4, 8, rows), F),
        sds((rows, d), BF), sds((rows, d), BF), sds((rows, d), F), sds((rows, d), F), sds((rows, d), BF), sds((4, N_PIECES * PIECE, d), BF),
    ]
    small = [sds((6, d), F), sds((1, d), F), sds((rows, 1), F), sds((4, 8, d), F)]
    q, k, v, att, st, h1, gm, branch, mixed, h2, w, mod, g_db, noised, bus = pl.pallas_call(
        forward_kernel,
        out_shape=tuple(handed + small),
        in_specs=[anyspace, anyspace, vspace, sspace, vspace, vspace, anyspace, anyspace, anyspace, anyspace, anyspace, anyspace, vspace],
        out_specs=tuple([anyspace] * len(handed) + [vspace] * len(small)),
        scratch_shapes=[
            vm((4, N_PIECES * PIECE, d), BF), vm((rows, d), BF), vm((rows, d), BF), vm(ada_weight.shape, BF), vm((2 * rows, 2 * HD), F),
            vm((rows, d), BF), vm((rows, d), BF), vm((4, rows, width), BF), vm((4, 2 * rows, width), BF), vm((4, 2 * rows, width), BF),
            vm((4, rows, width), BF), vm((4, 8, rows), F), vm((width // HD, rows, width), BF), vm((rows, 128), F),
            vm((rows, d), F), vm((rows, d), F), vm((rows, d), BF), vm((rows, d), BF),
            dma((9,)), dma((N_PIECES,)), dma((N_PIECES,)), dma((N_PIECES,)), dma((N_PIECES,)), dma((N_PIECES, 2)), dma((N_PIECES, 2)),
            dma((N_PIECES,)), dma((N_PIECES,)), dma((1,)), dma((1,)), dma((3,)), dma((3,)), dma((11,)),
        ],
        compiler_params=pltpu.CompilerParams(vmem_limit_bytes=56 * MIB, collective_id=0, has_side_effects=True),
        cost_estimate=pl.CostEstimate(flops=10**10, bytes_accessed=10**7, transcendentals=0),
        name="forward",
    )(tokens, cotangent, noise_mask.reshape(4, 128), prefix_len, vecs, time_emb, ada_weight, table, wt, out_weight, up_weight, down_weight, bu16)
    cs_own = lax.dynamic_slice_in_dim(table, cb * rows, rows, 0)
    vec = lambda v: v.reshape(1, -1)
    mask, gain1, gain2, db = vec(mask_embed), vec(gain_attn), vec(gain_mlp), vec(down_bias)
    tile = 256
    tiled = lambda w: pl.BlockSpec((tile, w), lambda i: (i, 0))
    fixed = lambda a: pl.BlockSpec(a.shape, lambda i: (0, 0))
    wts = [w[r, 0:576] for r in range(4)]
    wos = [w[r, 576:768] for r in range(4)]
    wus = [w[r, 768:1536] for r in range(4)]
    wds = [w[r, 1536:2304] for r in range(4)]
    bus = [bus[r, 0:1] for r in range(4)]
    atts = [att[r] for r in range(4)]
    fwd = [(q[r], k[r], v[r], None, st[r]) for r in range(4)]

    b1, g1, dd1, du1, gub1 = mlp_part(h2, gm, wus[1], bus[1], wds[1], None, None, BF, "mlp1")
    add0 = (swap(dd1, "tensor", 1), swap(du1, "tensor", 1))
    b3, g3, dd3, du3, gub3 = mlp_part(h2, gm, wus[3], bus[3], wds[3], (b1, g1), None, BF, "mlp3")
    add2 = (swap(dd3, "tensor", 1), swap(du3, "tensor", 1))
    b2, g2, dd2, du2, gub2 = mlp_part(h2, gm, wus[2], bus[2], wds[2], (b3, g3), add2, BF, "mlp2")
    b0, g0, dd0, du0, gub0 = mlp_part(h2, gm, wus[0], bus[0], wds[0], (b2, g2), add0, F, "mlp0")
    down_total = dd0 + swap(dd2, "tensor", 2).astype(F)
    up_total = du0 + swap(du2, "tensor", 2).astype(F)
    grad_down = reduce_dp(down_total, dp, n_dp)
    grad_up = reduce_dp(up_total, dp, n_dp)

    post = call(
        post_kernel,
        [sds((rows, d), BF), sds((rows, d), F)] + [sds((rows, width), BF)] * 4 + [sds((4 * width, d), F), sds((8, d), F)],
        [b0, g0, mixed, cotangent, branch] + atts + list(wos) + [gain2, mod, db],
        4 * rows * d * 4 * width,
        grid=(rows // tile,),
        in_specs=[tiled(d)] * 5 + [tiled(width)] * 4 + [fixed(w) for w in wos] + [fixed(gain2), fixed(mod), fixed(db)],
        out_specs=[tiled(d)] * 2 + [tiled(width)] * 4 + [pl.BlockSpec((4 * width, d), lambda i: (0, 0)), pl.BlockSpec((8, d), lambda i: (0, 0))],
        name="post",
    )
    output, grad_mixed = post[0], post[1]
    g_att = post[2:6]
    dwo, sums_two = post[6], post[7]
    part = lambda r: dwo[r * width : (r + 1) * width]
    o1 = swap(part(1).astype(BF), "tensor", 1)
    o3 = swap(part(3).astype(BF), "tensor", 1)
    o2 = swap((part(2) + o3.astype(F)).astype(BF), "tensor", 2)
    grad_out = reduce_dp(part(0) + o1.astype(F) + o2.astype(F), dp, n_dp)

    gh1 = None
    dws = {}
    for pair in ((3, 2), (1, 0)):
        backs = {}
        for r in pair:
            q, k, v, _, st = fwd[r]
            backs[r] = call(
                back_kernel,
                [sds((rows, width), BF), sds((rows, 2 * width), F), sds((rows, 2 * width), F)],
                [q, k, v, g_att[r], st, cs_own],
                10 * rows * 2 * rows * 256 * 3,
                scratch=[pltpu.VMEM((2 * rows, width), F), pltpu.VMEM((2 * rows, width), F), pltpu.VMEM((width // HD, 2 * rows, width), BF), pltpu.VMEM((rows, width), F)],
                name=f"back{r}",
            )
        for r in pair:
            dq, own_kv, _ = backs[r]
            rcv_kv = swap(backs[r ^ 1][2], "tensor", 1)
            args = [dq, own_kv, rcv_kv, cs_own, h1, wts[r]]
            aliases = {}
            if gh1 is not None:
                aliases = {len(args): 0}
                args.append(gh1)
            add = {2: 3, 0: 1}.get(r)
            if add is not None:
                args.append(swap(dws[add], "tensor", 1))
            gh1, dws[r] = call(
                functools.partial(proj_kernel, gh1 is not None, add is not None),
                [sds((rows, d), F), sds((3 * width, d), F if r == 0 else BF)],
                args,
                4 * rows * d * 3 * width,
                aliases=aliases,
                name=f"proj{r}",
            )
    qkv_total = dws[0] + swap(dws[2], "tensor", 2).astype(F)
    grad_qkv = reduce_dp(qkv_total, dp, n_dp).reshape(3, width, d).transpose(2, 0, 1)

    grad_tokens, sums_one = call(
        tail_kernel,
        [sds((rows, d), F), sds((8, d), F)],
        [gh1, grad_mixed, tokens, noised, mask, gain1, mod],
        10 * rows * d,
        name="tail",
    )

    hid = jnp.concatenate([gub0, gub1, gub2, gub3], axis=0)
    mods = jnp.concatenate([sums_one[2:4], sums_two[1:5]], axis=0)
    shared = jnp.concatenate([sums_one[0:2], sums_two[0:1], g_db], axis=0)
    got = swap(jnp.concatenate([hid[1:2], hid[3:4], shared, mods], axis=0), "tensor", 1)
    hid = hid[0::2] + got[0:2]
    shared = shared + got[2:6]
    mods = mods + got[6:]
    got = swap(jnp.concatenate([hid[1:2], shared, mods], axis=0), "tensor", 2)
    shared = jnp.concatenate([hid[0:1] + got[0:1], shared + got[1:5]], axis=0)
    mods = joined(mods[None], got[5:][None], xb)
    pair_mods = mods.reshape(2, 6 * d)
    times = time_emb
    step = 1
    while step < n_dp:
        got = swap(jnp.concatenate([shared, mods.reshape(-1, d)], axis=0), "dp", step)
        shared = shared + got[0:5]
        mods = joined(mods, got[5:].reshape(mods.shape), bit_of(dp, step))
        times = joined(times, swap(times, "dp", step), bit_of(dp, step))
        step *= 2
    mods = mods.reshape(-1, 6 * d)
    ada_full = ada_weight.astype(F)
    tv = time_emb.astype(F)
    sig = jax.nn.sigmoid(tv)
    grad_time = matmul_high(pair_mods, ada_full.T) * sig * (1.0 + tv * (1.0 - sig))
    silu = jax.nn.silu(times.astype(F))
    grad_ada_weight = lax.dot_general(silu, mods, (((0,), (0,)), ((), ())), precision=lax.Precision.HIGHEST, preferred_element_type=F)
    grad_ada_bias = jnp.sum(mods, axis=0)
    return (
        output,
        grad_tokens,
        grad_time,
        shared[2],
        shared[1],
        shared[3],
        grad_ada_weight,
        grad_ada_bias,
        grad_qkv,
        grad_out,
        grad_up,
        shared[0],
        grad_down,
        shared[4],
    )


def solution(mesh):
    group = ("dp", "tensor")
    in_specs = (P(group, None), P("dp", None), P("dp"), P(group), P(), P(), P(), P(), P(), P(None, None, "tensor"), P("tensor", None), P(None, "tensor"), P("tensor"), P("tensor", None), P(), P(group, None))
    out_specs = (P(group, None), P(group, None), P("dp", None), P(), P(), P(), P(), P(), P(None, None, "tensor"), P("tensor", None), P(None, "tensor"), P("tensor"), P("tensor", None), P())
    return jax.shard_map(per_device, mesh=mesh, in_specs=in_specs, out_specs=out_specs, check_vma=False)
```

```python
import functools

import jax
import jax.numpy as jnp
import numpy as np
from jax import lax
from jax.experimental import pallas as pl
from jax.experimental.pallas import tpu as pltpu
from jax.sharding import PartitionSpec as P

BF = jnp.bfloat16
F = jnp.float32
HD = 64
LEN = 1024
EPS = 1e-05
GELU_COEF = 0.7978845608028654
CUBIC_COEF = 0.044715
SCALE = 0.125
LOG2E = 1.4426950408889634
EXP_SCALE = SCALE * LOG2E
MIB = 1 << 20


def nn(a, b):
    return lax.dot_general(a, b, (((1,), (0,)), ((), ())), preferred_element_type=F)


def nt(a, b):
    return lax.dot_general(a, b, (((1,), (1,)), ((), ())), preferred_element_type=F)


def tn(a, b):
    return lax.dot_general(a, b, (((0,), (0,)), ((), ())), preferred_element_type=F)


def normalize(values):
    centered = values - jnp.mean(values, axis=-1, keepdims=True)
    inv = lax.rsqrt(jnp.mean(centered * centered, axis=-1, keepdims=True) + EPS)
    return centered * inv, inv


def layer_back(grad_norm, normed, inv):
    mean_grad = jnp.mean(grad_norm, axis=-1, keepdims=True)
    mean_cross = jnp.mean(grad_norm * normed, axis=-1, keepdims=True)
    return inv * (grad_norm - mean_grad - normed * mean_cross)


def halves_turned(v):
    parts = []
    for h in range(v.shape[1] // HD):
        lo = v[:, h * HD : h * HD + HD // 2]
        hi = v[:, h * HD + HD // 2 : (h + 1) * HD]
        parts += [-hi, lo]
    return jnp.concatenate(parts, axis=1)


def halves_back(v):
    parts = []
    for h in range(v.shape[1] // HD):
        lo = v[:, h * HD : h * HD + HD // 2]
        hi = v[:, h * HD + HD // 2 : (h + 1) * HD]
        parts += [hi, -lo]
    return jnp.concatenate(parts, axis=1)


def tables(block, heads):
    cos, sin = block[:, :HD], block[:, HD:]
    return jnp.concatenate([cos] * heads, axis=1), jnp.concatenate([sin] * heads, axis=1)


MESH = pl.DeviceIdType.MESH
PIECE = 256
HALVED = 3


def sds(shape, dtype):
    return jax.ShapeDtypeStruct(shape, dtype)


def split3(v):
    hi = v.astype(BF).astype(F)
    mid = (v - hi).astype(BF).astype(F)
    return hi, mid, v - hi - mid


def pick(index, values):
    out = jnp.int32(values[0])
    for i, v in enumerate(values[1:], 1):
        out = jnp.where(index == i, jnp.int32(v), out)
    return out


MLP_ORDER = [(1, 0), (1, 1), (1, 2), (3, 0), (2, 0), (0, 0), (0, 1), (3, 1), (2, 1), (0, 2), (3, 2), (2, 2)]
CROSS = [3, 6, 4, 7, 5, 8, 0, 1, 2]
SMALL_INPUTS = ("mask", "gain1", "gain2", "dbias", "upb", "adab", "time", "noise")


def block_kernel(n_dp, names, *args):
    ref = dict(zip(names, args))
    g = lambda *keys: [ref[key] for key in keys]
    tok_h, cot_h, prefix, ada_h, table_h, wt_h, wo_h, wu_h, wd_h = g("tok_h", "cot_h", "prefix", "ada_h", "table_h", "wt_h", "wo_h", "wu_h", "wd_h")
    out_o, gtok_o, grads_o, mods_o, small_o, wmu, wmd = g("out_o", "gtok_o", "grads_o", "mods_o", "small_o", "wmu", "wmd")
    w, wsu, wsd, rb, rx, sx, g0, sb, ry, rz1, rz2, exv = g("w", "wsu", "wsd", "rb", "rx", "sx", "g0", "sb", "ry", "rz1", "rz2", "exv")
    tok, cs, h1o, h1p, q, k, v, att, st, km = g("tok", "cs", "h1o", "h1p", "q", "k", "v", "att", "st", "km")
    branch, mixed, h2, gm, bm, gh, dk, dv, dq, parr, dwo2 = g(
        "branch", "mixed", "h2", "gm", "bm", "gh", "dk", "dv", "dq", "parr", "dwo2"
    )
    vecs, mod, nz, bus, gub, sums, mods, cse, cre, xse, xre, bse, bre = g(
        "vecs", "mod", "nz", "bus", "gub", "sums", "mods", "cse", "cre", "xse", "xre", "bse", "bre"
    )
    rows, d = tok.shape
    width = q.shape[2]
    heads = width // HD
    cond = ada_h.shape[0]
    tile = 256
    dp = lax.axis_index("dp")
    t = lax.axis_index("tensor")
    xb, cb = t // 2, t % 2
    bits = [1 << i for i in range(n_dp.bit_length() - 1)]
    bit = [(dp // b) % 2 for b in bits]
    core = (dp, t + 1 - 2 * cb)
    chip = (dp, t + 2 - 4 * xb)
    peer = [(dp + b - 2 * b * v_, t) for b, v_ in zip(bits, bit)]
    yb = bit[0]

    barrier = pltpu.get_barrier_semaphore()
    for other in [core, chip] + peer:
        pl.semaphore_signal(barrier, inc=1, device_id=other, device_id_type=MESH)
    pl.semaphore_wait(barrier, 2 + len(peer))

    def remote(src, dst, name, index, to):
        return pltpu.make_async_remote_copy(
            src_ref=src, dst_ref=dst, send_sem=ref[name + "_s"].at[index], recv_sem=ref[name + "_r"].at[index], device_id=to, device_id_type=MESH
        )

    def local(src, dst, index):
        return pltpu.make_async_copy(src, dst, ref["loc"].at[index])

    def at(start, size, mult=8):
        return pl.ds(start if isinstance(start, int) else pl.multiple_of(start, mult), size)

    att_src = [(wt_h, 0), (wt_h, width), (wt_h, 2 * width), (wo_h, 0)]
    hw = width // 2

    def part(r, j, which):
        if j < 4:
            return w.at[r, at(j * width + which * hw, hw, 32)]
        c, kind = (j - 4) // 2, (j - 4) % 2
        span = at(c * PIECE + which * 128, 128, 128)
        return wmd.at[r, span] if kind else wmu.at[r, :, span]

    def own_part(j, which):
        if j < 4:
            src, base = att_src[j]
            return src.at[at(base + which * hw, hw, 32)]
        c, kind = (j - 4) // 2, (j - 4) % 2
        span = at(c * PIECE + which * 128, 128, 128)
        return wd_h.at[span] if kind else wu_h.at[:, span]

    def far(j):
        return remote(own_part(j, yb), part(2, j, yb), "far", j, chip)

    def side(j):
        return remote(part(2, j, yb), part(2, j, yb), "side", j, peer[0])

    def cross(j, which):
        p = part(2, j, (yb + which) % 2)
        return remote(p, part(3, j, (yb + which) % 2), "cross", 2 * j + which, core)

    near = [
        remote(wt_h, w.at[1, pl.ds(0, 3 * width)], "near", 0, core),
        remote(wo_h, w.at[1, pl.ds(3 * width, width)], "near", 1, core),
        remote(wu_h, wmu.at[1], "near", 2, core),
        remote(wd_h, wmd.at[1], "near", 3, core),
    ]
    n_parts = 10

    def arrived(j):
        far(j).wait_recv()
        side(j).start()
        cross(j, 0).start()

    def passed(j):
        side(j).wait_recv()
        cross(j, 1).start()

    ada = sb
    loads = [local(ada_h.at[:, pl.ds(i * d, d)], ada.at[pl.ds(i * cond, cond)], i) for i in range(6)]
    load_tok, load_cot = local(tok_h, tok, 6), local(cot_h, h2, 7)
    load_cs = [local(table_h.at[at(cb * rows, rows)], cs.at[pl.ds(0, rows)], 8), local(table_h.at[at((1 - cb) * rows, rows)], cs.at[pl.ds(rows, rows)], 9)]
    load_w = [local(wt_h, w.at[0, pl.ds(0, 3 * width)], 10), local(wo_h, w.at[0, pl.ds(3 * width, width)], 11)]
    load_small = [local(ref[name], ref[name + "_v"], 52 + i) for i, name in enumerate(SMALL_INPUTS)]
    mask_v, gain1_v, gain2_v, dbias_v, upb_v, adab_v, time_v, noise_v = [ref[name + "_v"] for name in SMALL_INPUTS]
    for c in load_small + loads + [load_tok]:
        c.start()
    for c in load_small:
        c.wait()
    bus[0] = jnp.broadcast_to(upb_v[...].astype(F).reshape(1, -1), bus.shape[1:])
    bias_near, bias_far = remote(bus.at[0], bus.at[1], "bias", 0, core), remote(bus.at[0], bus.at[2], "bias", 1, chip)
    bias_cross = remote(bus.at[2], bus.at[3], "bias", 2, core)
    bias_near.start()
    bias_far.start()
    for j in range(n_parts):
        far(j).start()
    near[0].start()
    for c in load_w + load_cs + [load_cot]:
        c.start()

    for i, one in enumerate((mask_v, gain1_v, gain2_v, dbias_v)):
        vecs[i : i + 1, :] = one[...].astype(F).reshape(1, d)
    tv = jnp.where(xb == 0, time_v[0:1, :].astype(F), time_v[1:2, :].astype(F))
    s = jnp.broadcast_to(tv, (16, cond))
    s = s / (1.0 + jnp.exp(-s))
    stacked = jnp.concatenate(split3(s), axis=0).astype(BF)
    for i in range(6):
        loads[i].wait()
        m = nn(stacked, ada[pl.ds(i * cond, cond), :])
        mod[i : i + 1, :] = m[0:1] + m[16:17] + m[32:33] + adab_v[pl.ds(i * d, d)].astype(F).reshape(1, d)
    place = lax.broadcasted_iota(jnp.int32, (4, 128), 0) * 128 + lax.broadcasted_iota(jnp.int32, (4, 128), 1) + cb * rows
    limit = jnp.where(xb == 0, prefix[0], prefix[1])
    on = jnp.where((noise_v[...] == 1) & (place >= limit), 1.0, 0.0)
    on = jnp.concatenate([on, jnp.zeros((12, 128), F)], axis=0).astype(BF)
    eye = jnp.where(lax.broadcasted_iota(jnp.int32, (128, 128), 0) == lax.broadcasted_iota(jnp.int32, (128, 128), 1), 1.0, 0.0).astype(BF)
    cols = nt(eye, on)
    for i in range(4):
        nz[i * 128 : (i + 1) * 128, :] = cols[:, i : i + 1]
    load_tok.wait()

    def inputs_at(rs):
        return jnp.where(nz[rs, :] > 0.5, vecs[0:1, :], tok[rs, :].astype(F))

    every = pl.ds(0, rows)
    n1, _ = normalize(inputs_at(every))
    h1o[...] = (n1 * vecs[1:2, :] * (1.0 + mod[1:2, :]) + mod[0:1, :]).astype(BF)
    h1_copy = remote(h1o, h1p, "h1", 0, core)
    h1_copy.start()
    load_cot.wait()
    gmv = (mod[5:6, :] * h2[...].astype(F)).astype(BF)
    gm[...] = gmv
    sums[4:5, :] = jnp.sum(gmv.astype(F), axis=0, keepdims=True)
    for c in load_cs + load_w[:1]:
        c.wait()
    h1_copy.wait()
    for c in near[1:]:
        c.start()

    lane_q = lax.broadcasted_iota(jnp.int32, (rows, width), 1) // HD
    lane = lax.broadcasted_iota(jnp.int32, (tile, width), 1) // HD
    lane_s = lax.broadcasted_iota(jnp.int32, (tile, 128), 1)

    def project(r):
        cos, sin = tables(cs[0:rows, :], heads)
        qv = nt(h1o[...], w[r, 0:width, :])
        qv = (qv * cos + halves_turned(qv) * sin).astype(BF)
        q[r] = qv
        qf = qv.astype(F)
        for h in range(heads):
            km[h, 0:rows, :] = jnp.where(lane_q == h, qf, 0.0).astype(BF)
        kv = nt(h1o[...], w[r, width : 2 * width, :])
        k[r, 0:rows, :] = (kv * cos + halves_turned(kv) * sin).astype(BF)
        v[r, 0:rows, :] = nt(h1o[...], w[r, 2 * width : 3 * width, :]).astype(BF)
        cos, sin = tables(cs[rows : 2 * rows, :], heads)
        kv = nt(h1p[...], w[r, width : 2 * width, :])
        k[r, rows : 2 * rows, :] = (kv * cos + halves_turned(kv) * sin).astype(BF)
        v[r, rows : 2 * rows, :] = nt(h1p[...], w[r, 2 * width : 3 * width, :]).astype(BF)

    def attend(r, i):
        rs = at(i * tile, tile, tile)
        acc = jnp.zeros((tile, width), F)
        stats = jnp.zeros((tile, 128), F)
        for h in range(heads):
            s = nt(km[h, rs, :], k[r])
            m = jnp.max(s, axis=1, keepdims=True)
            e = jnp.exp2((s - m) * EXP_SCALE)
            total = jnp.sum(e, axis=1, keepdims=True)
            p = (e * (1.0 / total)).astype(BF)
            acc = jnp.where(lane == h, nn(p, v[r]), acc)
            stats = jnp.where(lane_s == h, m * EXP_SCALE + jnp.log2(total), stats)
        att[r, rs, :] = acc.astype(BF)
        dq[rs, 0:128] = stats

    def at_step(step, todo):
        for key, fns in todo.items():

            @pl.when(step == key)
            def _():
                for fn in fns:
                    fn()

    def wait_near(i):
        return near[i].wait_recv

    def wait_cross(j):
        def go():
            cross(j, 0).wait_recv()
            cross(j, 1).wait_recv()

        return go

    arrive = lambda j: functools.partial(arrived, j)
    go_on = lambda j: functools.partial(passed, j)
    per_r = rows // tile

    def bias_on():
        bias_far.wait_recv()
        bias_cross.start()

    fwd_plan = {
        0: [arrive(0)],
        1: [arrive(1), bias_on],
        2: [wait_near(0), arrive(2), go_on(0)],
        3: [arrive(3), go_on(1)],
        4: [go_on(2)],
        5: [arrive(4), go_on(3)],
        6: [wait_cross(0), wait_cross(1), wait_cross(2)],
        7: [arrive(5), go_on(4)],
    }

    def fwd_body(it, carry):
        r, i = it // per_r, it % per_r
        at_step(it, fwd_plan)

        @pl.when(i == 0)
        def _():
            project(r)

        attend(r, i)

        @pl.when(i == per_r - 1)
        def _():
            st[r] = dq[:, 0:128].T[0:8, :]

        return carry

    lax.fori_loop(0, 4 * per_r, fwd_body, 0)
    arrived(6)
    load_w[1].wait()
    wait_near(1)()
    wait_cross(3)()

    def mid_body(i, carry):
        rs = at(i * tile, tile, tile)
        b = nn(att[0, rs, :], w[0, 3 * width : 4 * width, :])
        for r in range(1, 4):
            b = b + nn(att[r, rs, :], w[r, 3 * width : 4 * width, :])
        x = inputs_at(rs) + mod[2:3, :] * b
        n2, _ = normalize(x)
        branch[rs, :] = b
        mixed[rs, :] = x
        h2[rs, :] = (n2 * vecs[2:3, :] * (1.0 + mod[4:5, :]) + mod[3:4, :]).astype(BF)
        bm[rs, :] = jnp.zeros((tile, d), F)
        gh[rs, :] = jnp.zeros((tile, d), F)
        return carry

    lax.fori_loop(0, per_r, mid_body, 0)
    load_cot = local(cot_h, tok, 7)
    load_cot.start()

    def piece(buf, p, start=0, size=PIECE):
        return buf.at[at(p * PIECE + start, size)]

    def cross_send(n):
        p = CROSS[n]
        return remote(piece(sx, p), piece(rx, p), "gx", p, chip)

    off1 = yb * 128
    off2 = off1 + bit[1] * 64
    off3 = off2 + bit[2] * 32
    anti1 = (1 - yb) * 128
    anti2 = off1 + (1 - bit[1]) * 64
    anti3 = off2 + (1 - bit[2]) * 32

    def sl(p, start, size):
        return at(p * PIECE + start, size, 32)

    def send_y(p):
        return remote(rx.at[pl.ds(p * PIECE, 128)], ry.at[p], "gy", p, peer[0])

    def send_z1(p):
        return remote(rx.at[pl.ds(p * PIECE + 128, 64)], rz1.at[p], "gz", p, peer[1])

    def send_z2(p):
        return remote(rx.at[pl.ds(p * PIECE + 192, 32)], rz2.at[p], "gw", p, peer[2])

    def back_z2(p):
        return remote(sx.at[sl(p, off3, 32)], sx.at[sl(p, off3, 32)], "aw", p, peer[2])

    def back_z1(p):
        return remote(sx.at[sl(p, off2, 64)], sx.at[sl(p, off2, 64)], "az", p, peer[1])

    def back_y(p):
        return remote(sx.at[sl(p, off1, 128)], sx.at[sl(p, off1, 128)], "ay", p, peer[0])

    def more(e, p):
        return remote(g0.at[sl(p, off3, 32)], ref["ex"].at[e, p], "ge", e * 9 + p, peer[HALVED + e])

    def stage_x(n):
        p = CROSS[n]
        cross_send(n).wait()
        g0[piece_ds(p), :] = g0[piece_ds(p), :] + rx[piece_ds(p), :].astype(F)
        rx[pl.ds(p * PIECE, 128), :] = g0[sl(p, anti1, 128), :].astype(BF)
        send_y(p).start()

    def piece_ds(p):
        return pl.ds(p * PIECE, PIECE)

    def stage_y(n):
        p = CROSS[n]
        send_y(p).wait_recv()
        g0[sl(p, off1, 128), :] = g0[sl(p, off1, 128), :] + ry[p].astype(F)
        rx[pl.ds(p * PIECE + 128, 64), :] = g0[sl(p, anti2, 64), :].astype(BF)
        send_z1(p).start()

    def stage_z1(n):
        p = CROSS[n]
        send_z1(p).wait_recv()
        g0[sl(p, off2, 64), :] = g0[sl(p, off2, 64), :] + rz1[p].astype(F)
        rx[pl.ds(p * PIECE + 192, 32), :] = g0[sl(p, anti3, 32), :].astype(BF)
        send_z2(p).start()

    def stage_z2(n):
        p = CROSS[n]
        send_z2(p).wait_recv()
        total = g0[sl(p, off3, 32), :] + rz2[p].astype(F)
        for e in range(len(bits) - HALVED):
            g0[sl(p, off3, 32), :] = total
            more(e, p).start()
            more(e, p).wait()
            fill = local(ref["ex"].at[e, p], exv, 36)
            fill.start()
            fill.wait()
            total = total + exv[...]
        sx[sl(p, off3, 32), :] = total.astype(BF)
        back_z2(p).start()

    def stage_a1(n):
        p = CROSS[n]
        back_z2(p).wait_recv()
        back_z1(p).start()

    def stage_a2(n):
        p = CROSS[n]
        back_z1(p).wait_recv()
        back_y(p).start()

    def result(p):
        return local(sx.at[piece_ds(p)], grads_o.at[piece_ds(p)], 14 + p)

    def stage_a3(n):
        p = CROSS[n]
        back_y(p).wait_recv()
        result(p).start()

    def stage_end(n):
        p = CROSS[n]
        send_y(p).wait_send()
        send_z1(p).wait_send()
        send_z2(p).wait_send()
        back_z2(p).wait_send()
        back_z1(p).wait_send()
        back_y(p).wait_send()
        result(p).wait()

    stages = dict(X=stage_x, Y=stage_y, Z=stage_z1, W=stage_z2, A=stage_a1, B=stage_a2, C=stage_a3, E=stage_end)

    def run(text):
        for i in range(0, len(text), 2):
            stages[text[i]](int(text[i + 1]))

    steps = len(MLP_ORDER)

    def core_slot(step):
        return 2 * (sum(1 for r, _ in MLP_ORDER[:step] if r % 2) % 3)

    def give(step, kind):
        r, c = MLP_ORDER[step]
        slot = core_slot(step) + kind
        row = (3 * kind + c) * PIECE
        return remote(sb.at[pl.ds(slot * PIECE, PIECE)], rb.at[r // 2, pl.ds(row, PIECE)], "give", 2 * step + kind, core)

    def fetch(step, slot, own):
        r = pick(step, [r for r, _ in MLP_ORDER])
        c = pick(step, [c for _, c in MLP_ORDER])
        span = at(c * PIECE, PIECE, PIECE)
        up, down = (wu_h, wd_h) if own else (wmu.at[r], wmd.at[r])
        return [
            pltpu.make_async_copy(up.at[:, span], wsu.at[slot], ref["wst"].at[slot, 0]),
            pltpu.make_async_copy(down.at[span], wsd.at[slot], ref["wst"].at[slot, 1]),
        ]

    bias_near.wait_recv()
    for i in (2, 3):
        near[i].wait_recv()
    for c in fetch(0, 0, False):
        c.start()

    mlp_plan = {
        1: [go_on(5), arrive(7)],
        2: [wait_cross(4), wait_cross(5), go_on(6)],
        4: [arrive(8), go_on(7)],
        6: [wait_cross(6), wait_cross(7), arrive(9)],
        8: [go_on(8)],
        9: [go_on(9), wait_cross(8), wait_cross(9)],
    }

    def mlp_body(step, carry):
        slot = step % 2
        r = pick(step, [r for r, _ in MLP_ORDER])
        c = pick(step, [c for _, c in MLP_ORDER])
        at_step(step, mlp_plan)
        for cp in fetch(step, slot, False):
            cp.wait()

        nxt = pick(step, [r for r, _ in MLP_ORDER[1:]] + [4])

        @pl.when((nxt > 0) & (nxt < 4))
        def _():
            for cp in fetch(step + 1, 1 - slot, False):
                cp.start()

        @pl.when(nxt == 0)
        def _():
            for cp in fetch(step + 1, 1 - slot, True):
                cp.start()

        @pl.when(step == 0)
        def _():
            bias_cross.wait_recv()

        cols = at(c * PIECE, PIECE, PIECE)
        u = nn(h2[...], wsu[slot]) + bus[r, 0:1, cols]
        th = jnp.tanh(GELU_COEF * (u + CUBIC_COEF * u * u * u))
        act = (0.5 * u * (1.0 + th)).astype(BF)
        slope = 0.5 * (1.0 + th) + 0.5 * u * (1.0 - th * th) * GELU_COEF * (1.0 + 3.0 * CUBIC_COEF * u * u)
        gu_f = (nt(gm[...], wsd[slot]) * slope).astype(BF).astype(F)
        gu = gu_f.astype(BF)
        gub[r, 0:1, cols] = jnp.sum(gu_f, axis=0, keepdims=True)
        bm[...] += nn(act, wsd[slot])
        gh[...] += nt(gu, wsu[slot])
        ds_ = (tn(gu, h2[...]), tn(act, gm[...]))
        for i, (r_, c_) in enumerate(MLP_ORDER):

            @pl.when(step == i)
            def _():
                rows_ = [pl.ds((3 + 3 * kind + c_) * PIECE, PIECE) for kind in range(2)]
                inbox = [pl.ds((3 * kind + c_) * PIECE, PIECE) for kind in range(2)]
                if r_ % 2:
                    before = [j for j in range(i) if MLP_ORDER[j][0] % 2 and core_slot(j) == core_slot(i)]
                    for kind in range(2):
                        if before:
                            give(before[-1], kind).wait_send()
                        sb[pl.ds((core_slot(i) + kind) * PIECE, PIECE), :] = ds_[kind].astype(BF)
                        give(i, kind).start()
                else:
                    origin = MLP_ORDER.index((r_ + 1, c_))
                    for kind in range(2):
                        give(origin, kind).wait_recv()
                        total = ds_[kind] + rb[r_ // 2, inbox[kind], :].astype(F)
                        if r_ == 2:
                            sx[rows_[kind], :] = total.astype(BF)
                            cross_send(CROSS.index(3 + 3 * kind + c_)).start()
                        else:
                            g0[rows_[kind], :] = total

        return carry

    lax.fori_loop(0, steps, mlp_body, 0)
    odd = [i for i, (r, _) in enumerate(MLP_ORDER) if r % 2]
    for i in odd[-3:]:
        for kind in range(2):
            give(i, kind).wait_send()

    load_cot.wait()
    run("X0")
    gba = h1p

    def post_body(i, carry):
        rs = at(i * tile, tile, tile)
        x = mixed[rs, :]
        n2, inv = normalize(x)
        c = tok[rs, :].astype(F)
        bmlp = bm[rs, :] + vecs[3:4, :]
        h2[rs, :] = (x + mod[5:6, :] * bmlp).astype(BF)
        gr = gh[rs, :]
        gs = gr * (1.0 + mod[4:5, :])
        gmix = c + layer_back(gs * vecs[2:3, :], n2, inv)
        mixed[rs, :] = gmix
        gba[rs, :] = (mod[2:3, :] * gmix).astype(BF)
        part_sums = [gs * n2, gmix * branch[rs, :], gr, gr * n2 * vecs[2:3, :], c * bmlp]
        for row, val in zip((3, 10, 11, 12, 13), part_sums):
            got = jnp.sum(val, axis=0, keepdims=True)

            @pl.when(i == 0)
            def _():
                sums[row : row + 1, :] = got

            @pl.when(i > 0)
            def _():
                sums[row : row + 1, :] += got

        return carry

    lax.fori_loop(0, per_r, post_body, 0)
    store_out = local(h2, out_o, 26)
    store_out.start()
    load_tok = local(tok_h, tok, 6)
    load_tok.start()
    run("")
    for r in range(4):
        wo = w[r, 3 * width : 4 * width, :]
        dw = tn(att[r], gba[...])
        att[r] = nt(gba[...], wo).astype(BF)
        if r == 0:
            g0[pl.ds(3 * width, width), :] = dw
        elif r == 2:
            dwo2[...] = dw
        else:
            sb[pl.ds((3 - r) // 2 * 4 * width + 3 * width, width), :] = dw.astype(BF)

    lane_k = lax.broadcasted_iota(jnp.int32, (2 * rows, width), 1) // HD

    def back_tile(r, i, it):
        @pl.when(i == 0)
        def _():
            kf = k[r].astype(F)
            for h in range(heads):
                km[h] = jnp.where(lane_k == h, kf, 0.0).astype(BF)
            dk[...] = jnp.zeros_like(dk)
            dv[...] = jnp.zeros_like(dv)

        rs = at(i * tile, tile, tile)
        qt = q[r, rs, :].astype(F)
        gt = att[r, rs, :].astype(F)
        acc = jnp.zeros((tile, width), F)
        for h in range(heads):
            back_events(it, h)
            qm = jnp.where(lane == h, qt, 0.0).astype(BF)
            gmh = jnp.where(lane == h, gt, 0.0).astype(BF)
            p = jnp.exp2(nt(k[r], qm) * EXP_SCALE - st[r, h : h + 1, rs])
            dpr = nt(v[r], gmh)
            inner = jnp.sum(p * dpr, axis=0, keepdims=True)
            ds_ = (p * (dpr - inner)).astype(BF)
            dv[...] += nn(p.astype(BF), gmh)
            dk[...] += nn(ds_, qm)
            acc = acc + tn(ds_, km[h])
        dq[rs, :] = acc

    def par_copy(r):
        lanes = pl.ds((r % 2) * 2 * width, 2 * width)
        return remote(branch.at[:, lanes], parr.at[r % 2], "par", r, core)

    def finish_back(r):
        cos, sin = tables(cs[0:rows, :], heads)
        gq = dq[...] * SCALE
        q[r] = (gq * cos + halves_back(gq * sin)).astype(BF)
        lanes = slice((r % 2) * 2 * width, (r % 2) * 2 * width + 2 * width)
        bm[:, lanes] = jnp.concatenate([dk[0:rows, :] * SCALE, dv[0:rows, :]], axis=1)
        if r < 2:
            par_copy(r + 2).wait_send()
            if r == 1:
                pl.semaphore_wait(ref["credit"], 1)
        branch[:, lanes] = jnp.concatenate([dk[rows : 2 * rows, :] * SCALE, dv[rows : 2 * rows, :]], axis=1)
        par_copy(r).start()

    def hand(r):
        base = (3 - r) // 2 * 4 * width
        return remote(sb.at[pl.ds(base, 4 * width)], rb.at[r // 2, pl.ds(0, 4 * width)], "hand", r // 2, core)

    def weight_grads(r):
        par_copy(r ^ 1).wait_recv()
        cos, sin = tables(cs[0:rows, :], heads)
        lanes = slice((r % 2) * 2 * width, (r % 2) * 2 * width + 2 * width)
        gkv = bm[:, lanes] + parr[(r ^ 1) % 2]
        gk = gkv[:, :width]
        gk = (gk * cos + halves_back(gk * sin)).astype(BF)
        gv = gkv[:, width:].astype(BF)
        parts = (q[r], gk, gv)
        if r % 2 == 0:
            hand(r + 1).wait_recv()
        back = 0.0 if r == 3 else gh[...]
        for i, p_ in enumerate(parts):
            place_ = pl.ds(i * width, width)
            back = back + nn(p_, w[r, i * width : (i + 1) * width, :])
            dw = tn(p_, h1o[...])
            if r % 2:
                sb[pl.ds((3 - r) // 2 * 4 * width + i * width, width), :] = dw.astype(BF)
            else:
                dw = dw + rb[r // 2, place_, :].astype(F)
                if r == 2:
                    sx[place_, :] = dw.astype(BF)
                else:
                    g0[place_, :] = dw
        gh[...] = back
        place_ = pl.ds(3 * width, width)
        if r % 2:
            hand(r).start()
        elif r == 2:
            sx[place_, :] = (dwo2[...] + rb[1, place_, :].astype(F)).astype(BF)
            for n in (6, 7, 8):
                cross_send(n).start()
        else:
            g0[place_, :] = g0[place_, :] + rb[0, place_, :].astype(F)

    def give_credit():
        pl.semaphore_signal(ref["credit"], inc=1, device_id=core, device_id_type=MESH)

    back_plan = [
        {0: "X1Y0", 2: "X2", 4: "W1X3", 5: "Z2A1Y3X4", 6: "W2"},
        {1: "Z0", 2: "W0", 3: "A0", 4: "B0", 5: "C0", 6: "B1", 7: "A2"},
        {1: "Y1", 2: "Z1", 3: "Y2", 6: "Y4X5Z3", 7: "C1Z4"},
    ]

    def back_events(it, h):
        at_step(it, {key: [functools.partial(run, text)] for key, text in back_plan[h].items()})

    def back_body(it, carry):
        i = it % per_r
        back_tile(3 - it // per_r, i, it)
        for r in range(4):

            @pl.when(it == (3 - r) * per_r + per_r - 1)
            def _():
                finish_back(r)

        @pl.when(it == 2 * per_r)
        def _():
            weight_grads(3)
            weight_grads(2)
            give_credit()

        return carry

    lax.fori_loop(0, 4 * per_r, back_body, 0)
    run("")
    weight_grads(1)
    run("W3Y5B2")
    weight_grads(0)

    hand(1).wait_send()
    hand(3).wait_send()
    store_out.wait()
    load_tok.wait()
    run("X6W4")

    def tail_body(i, carry):
        rs = at(i * tile, tile, tile)
        on_ = nz[rs, :] > 0.5
        n1_, inv = normalize(inputs_at(rs))
        gr = gh[rs, :]
        gs = gr * (1.0 + mod[1:2, :])
        gi = mixed[rs, :] + layer_back(gs * vecs[1:2, :], n1_, inv)
        mixed[rs, :] = jnp.where(on_, 0.0, gi)
        part_sums = [gs * n1_, jnp.where(on_, gi, 0.0), gr, gr * n1_ * vecs[1:2, :]]
        for row, val in zip((1, 2, 8, 9), part_sums):
            got = jnp.sum(val, axis=0, keepdims=True)

            @pl.when(i == 0)
            def _():
                sums[row : row + 1, :] = got

            @pl.when(i > 0)
            def _():
                sums[row : row + 1, :] += got

        return carry

    lax.fori_loop(0, per_r, tail_body, 0)
    store_tok = local(mixed, gtok_o, 27)
    store_tok.start()
    run("A3C2Z5")

    none = jnp.zeros((2, d), F)
    cse[0:8, :] = jnp.concatenate([sums[8:14, :], none], axis=0)
    cse[8:16, :] = jnp.concatenate([gub[1, 0:1, :], gub[3, 0:1, :], sums[1:5, :], none], axis=0)
    core_sum = remote(cse, cre, "sc", 0, core)
    core_sum.start()
    run("")
    core_sum.wait_recv()
    own_mods = cse[0:6, :] + cre[0:6, :]
    tv_row = jnp.concatenate([tv, jnp.zeros((1, d - cond), F)], axis=1)
    me = 2 * dp + xb
    mods[me] = jnp.concatenate([own_mods, tv_row, jnp.zeros((1, d), F)], axis=0)
    xse[...] = jnp.concatenate([gub[2, 0:1, :] + cre[9:10, :], cse[10:14, :] + cre[10:14, :], jnp.zeros((3, d), F)], axis=0)
    chip_sum = remote(xse, xre, "sx", 0, chip)
    chip_mods = remote(mods.at[me], mods.at[me], "sx", 1, chip)
    chip_sum.start()
    chip_mods.start()
    run("X7A4Y6B3")
    chip_sum.wait_recv()
    cur = jnp.concatenate([gub[0, 0:1, :] + cre[8:9, :] + xre[0:1, :], xse[1:8, :] + xre[1:8, :]], axis=0)
    chip_mods.wait()
    pending = [core_sum, chip_sum]
    drain = ["W5", "B4", "Y7X8Z6"]
    for i, b in enumerate(bits):
        bse[i] = cur
        base = (dp // b) * b * 2
        one = remote(bse.at[i], bre.at[i], "sd", 2 * i, peer[i])
        two = remote(mods.at[pl.ds(base, 2 * b)], mods.at[pl.ds(base, 2 * b)], "sd", 2 * i + 1, peer[i])
        one.start()
        two.start()
        if drain:
            run(drain.pop(0))
        one.wait_recv()
        two.wait()
        pending.append(one)
        cur = cur + bre[i]
    small_o[...] = cur
    for text in drain:
        run(text)
    store_mods = local(mods, mods_o, 28)
    store_mods.start()
    run("A5C3Z7W6")
    run("C4B5W7Y8")
    run("A6A7C5Z8")
    run("B6B7W8C6")
    run("A8C7B8C8")
    for n in range(9):
        stage_end(n)
    for c in [store_mods, store_tok]:
        c.wait()
    for c in pending:
        c.wait_send()
    for c in near + [bias_near, bias_far, bias_cross]:
        c.wait_send()
    for j in range(n_parts):
        far(j).wait_send()
        side(j).wait_send()
        cross(j, 0).wait_send()
        cross(j, 1).wait_send()
    for r in range(2):
        par_copy(r).wait_send()


def finish_kernel(n_dp, grads_h, out_h, tok_h, mods_h, small, ada_h, time, out_o, gtok_o, gqkv_o, gout_o, gup_o, gdown_o, gada_o, gtime_o, gadab_o, gmask_o, ga_o, gm_o, gub_o, gdb_o, grads, wide, outv, tokv, mods, ada, adag, sem):
    d = grads.shape[1]
    width = gout_o.shape[0]
    cond = ada.shape[0]
    seqs = mods.shape[0]
    dp = lax.axis_index("dp")

    def copy(src, dst, index):
        return pltpu.make_async_copy(src, dst, sem.at[index])

    span = lambda p: pl.ds(p * PIECE, PIECE)
    load_mods, load_ada = copy(mods_h, mods, 0), copy(ada_h, ada, 1)
    load_tok, load_out = copy(tok_h, tokv, 2), copy(out_h, outv, 3)
    pieces = [copy(grads_h.at[span(p)], grads.at[span(p)], 4 + p) for p in range(9)]
    for c in [load_mods] + pieces + [load_tok, load_out, load_ada]:
        c.start()
    stores = []

    def store(src, dst):
        stores.append(copy(src, dst, 13 + len(stores)))
        stores[-1].start()

    head = 3 * width
    for p in range(9):
        pieces[p].wait()
        if 3 <= p < 6:
            for b in range(3):
                wide[span(p), span(b)] = grads[span(p), span(b)].astype(F).T
                store(wide.at[span(p), span(b)], gup_o.at[span(b), span(p - 3)])
        else:
            wide[span(p), :] = grads[span(p), :].astype(F)
            if p >= 6:
                store(wide.at[span(p)], gdown_o.at[span(p - 6)])
            elif p == 2:
                store(wide.at[pl.ds(0, head)], gqkv_o)
                store(wide.at[pl.ds(head, width)], gout_o)
    load_tok.wait()
    store(tokv, gtok_o)
    load_out.wait()
    store(outv, out_o)
    load_mods.wait()
    total = mods[0]
    for s_ in range(1, seqs):
        total = total + mods[s_]
    tall = jnp.concatenate([mods[s_, 6:7, 0:cond] for s_ in range(seqs)], axis=0)
    left = split3(tall / (1.0 + jnp.exp(-tall)))
    lhs = jnp.concatenate([left[0], left[0], left[1], left[0], left[2], left[1]], axis=0).astype(BF)
    for j in range(6):
        gadab_o[pl.ds(j * d, d)] = total[j : j + 1, :].reshape(d)
        right = split3(jnp.concatenate([mods[s_, j : j + 1, :] for s_ in range(seqs)], axis=0))
        rhs = jnp.concatenate([right[0], right[1], right[0], right[2], right[0], right[1]], axis=0).astype(BF)
        adag[j] = tn(lhs, rhs)
        store(adag.at[j], gada_o.at[:, pl.ds(j * d, d)])
    load_ada.wait()
    acc = jnp.zeros((48, cond), F)
    for j in range(6):
        pairs = jnp.concatenate([mods[2 * dp, j : j + 1, :], mods[2 * dp + 1, j : j + 1, :], jnp.zeros((14, d), F)], axis=0)
        acc = acc + nt(jnp.concatenate(split3(pairs), axis=0).astype(BF), ada[:, pl.ds(j * d, d)])
    te = time[...].astype(F)
    sig = 1.0 / (1.0 + jnp.exp(-te))
    gtime_o[...] = (acc[0:2] + acc[16:18] + acc[32:34]) * sig * (1.0 + te * (1.0 - sig))
    for row, o in enumerate((gub_o, ga_o, gmask_o, gm_o, gdb_o)):
        o[...] = small[row : row + 1, :].reshape(d)
    for c in stores:
        c.wait()


def rotary_block():
    freq = np.float32(10000.0) ** (np.float32(-2.0) * np.arange(HD // 2, dtype=np.float32) / np.float32(HD))
    angle = np.arange(LEN, dtype=np.float32)[:, None] * freq[None, :].astype(np.float32)
    angle = np.concatenate([angle, angle], axis=1)
    return np.concatenate([np.cos(angle), np.sin(angle)], axis=1).astype(np.float32)


def per_device(tokens, time_emb, prefix_len, noise_mask, mask_embed, gain_attn, gain_mlp, ada_weight, ada_bias, qkv_weight, out_weight, up_weight, up_bias, down_weight, down_bias, cotangent):
    rows, d = tokens.shape
    n_dp = lax.axis_size("dp")
    width = qkv_weight.shape[2]
    cond = time_emb.shape[1]
    hidden = up_weight.shape[1]
    n_bits = n_dp.bit_length() - 1
    assert lax.axis_size("tensor") == 4 and time_emb.shape[0] == 2 and 2 * rows == LEN
    assert n_dp == 1 << n_bits and n_bits >= HALVED and 4 * width == hidden == 3 * PIECE == d
    wt = qkv_weight.transpose(1, 2, 0).reshape(3 * width, d)
    table = jnp.asarray(rotary_block())
    a = pl.BlockSpec(memory_space=pl.ANY)
    m = pl.BlockSpec(memory_space=pltpu.VMEM)
    smem = pl.BlockSpec(memory_space=pltpu.SMEM)
    total = 4 * width + 2 * hidden
    noise = noise_mask.reshape(4, rows // 4)
    small_in = (mask_embed, gain_attn, gain_mlp, down_bias, up_bias, ada_bias, time_emb, noise)
    ins = [("tok_h", tokens, a), ("cot_h", cotangent, a), ("prefix", prefix_len, smem)]
    ins += [(name, value, a) for name, value in zip(SMALL_INPUTS, small_in)]
    ins += [("ada_h", ada_weight, a), ("table_h", table, a), ("wt_h", wt, a), ("wo_h", out_weight, a), ("wu_h", up_weight, a), ("wd_h", down_weight, a)]
    outs = [
        ("out_o", (rows, d), BF, a), ("gtok_o", (rows, d), F, a), ("grads_o", (total, d), BF, a), ("mods_o", (2 * n_dp, 8, d), F, a), ("small_o", (8, d), F, m),
        ("wmu", (4, d, hidden), BF, a), ("wmd", (4, hidden, d), BF, a),
    ]
    extra = max(n_bits - HALVED, 1)
    if n_bits > HALVED:
        outs.append(("ex", (extra, 9, 32, d), F, a))
    vmem = [
        ("w", (4, 4 * width, d), BF), ("wsu", (2, d, PIECE), BF), ("wsd", (2, PIECE, d), BF), ("rb", (2, 2 * hidden, d), BF), ("rx", (total, d), BF), ("sx", (total, d), BF),
        ("g0", (total, d), F), ("sb", (6 * PIECE, d), BF), ("ry", (9, 128, d), BF), ("rz1", (9, 64, d), BF), ("rz2", (9, 32, d), BF), ("exv", (32, d), F),
        ("tok", (rows, d), BF), ("cs", (2 * rows, 2 * HD), F), ("h1o", (rows, d), BF), ("h1p", (rows, d), BF),
        ("q", (4, rows, width), BF), ("k", (4, 2 * rows, width), BF), ("v", (4, 2 * rows, width), BF), ("att", (4, rows, width), BF), ("st", (4, 8, rows), F),
        ("km", (width // HD, 2 * rows, width), BF), ("branch", (rows, d), F), ("mixed", (rows, d), F), ("h2", (rows, d), BF), ("gm", (rows, d), BF),
        ("bm", (rows, d), F), ("gh", (rows, d), F), ("dk", (2 * rows, width), F), ("dv", (2 * rows, width), F), ("dq", (rows, width), F),
        ("parr", (2, rows, 2 * width), F), ("dwo2", (width, d), F), ("vecs", (8, d), F), ("mod", (8, d), F), ("nz", (rows, 1), F),
        ("bus", (4, 8, hidden), F), ("gub", (4, 8, hidden), F), ("sums", (16, d), F), ("mods", (2 * n_dp, 8, d), F), ("cse", (16, d), F), ("cre", (16, d), F),
        ("xse", (8, d), F), ("xre", (8, d), F), ("bse", (n_bits, 8, d), F), ("bre", (n_bits, 8, d), F),
    ]
    vmem += [(name + "_v", value.shape, value.dtype) for name, value in zip(SMALL_INPUTS, small_in)]
    pairs = [
        ("far", 10), ("side", 10), ("cross", 20), ("near", 4), ("bias", 3), ("h1", 1), ("give", 24), ("gx", 9), ("gy", 9), ("gz", 9), ("gw", 9), ("aw", 9), ("az", 9), ("ay", 9),
        ("ge", 9 * extra), ("par", 4), ("hand", 2), ("sc", 1), ("sx", 2), ("sd", 2 * n_bits),
    ]
    dma = pltpu.SemaphoreType.DMA
    sems = [("loc", dma((60,))), ("wst", dma((2, 2))), ("credit", pltpu.SemaphoreType.REGULAR)]
    for name, n in pairs:
        sems += [(name + "_s", dma((n,))), (name + "_r", dma((n,)))]
    names = [i[0] for i in ins] + [o[0] for o in outs] + [x[0] for x in vmem] + [x[0] for x in sems]
    res = pl.pallas_call(
        functools.partial(block_kernel, n_dp, names),
        out_shape=tuple(sds(shape, dtype) for _, shape, dtype, _ in outs),
        in_specs=[i[2] for i in ins],
        out_specs=tuple(o[3] for o in outs),
        scratch_shapes=[pltpu.VMEM(shape, dtype) for _, shape, dtype in vmem] + [x[1] for x in sems],
        compiler_params=pltpu.CompilerParams(vmem_limit_bytes=63 * MIB + 3 * MIB // 4, collective_id=0, has_side_effects=True),
        cost_estimate=pl.CostEstimate(flops=4 * 10**10, bytes_accessed=10**8, transcendentals=0),
        name="block",
    )(*[i[1] for i in ins])
    out16, gtok, grads, mods, small = res[:5]
    vecs = [sds((d,), F)] * 5
    finals = [sds((rows, d), BF), sds((rows, d), F), sds((3 * width, d), F), sds((width, d), F), sds((d, hidden), F), sds((hidden, d), F), sds((cond, 6 * d), F)]
    done = pl.pallas_call(
        functools.partial(finish_kernel, n_dp),
        out_shape=tuple(finals + [sds((2, cond), F), sds((6 * d,), F)] + vecs),
        in_specs=[a, a, a, a, m, a, m],
        out_specs=tuple([a] * len(finals) + [m] * 7),
        scratch_shapes=[
            pltpu.VMEM((total, d), BF), pltpu.VMEM((total, d), F), pltpu.VMEM((rows, d), BF), pltpu.VMEM((rows, d), F), pltpu.VMEM(mods.shape, F),
            pltpu.VMEM(ada_weight.shape, BF), pltpu.VMEM((6, cond, d), F), dma((40,)),
        ],
        compiler_params=pltpu.CompilerParams(vmem_limit_bytes=63 * MIB),
        cost_estimate=pl.CostEstimate(flops=10**8, bytes_accessed=2 * 10**7, transcendentals=0),
        name="finish",
    )(grads, out16, gtok, mods, small, ada_weight, time_emb)
    output, grad_tokens, gqkv, gout, gup, gdown, grad_ada, grad_time, grad_adab, g_mask, g_attn, g_mlp, g_upb, g_db = done
    return (output, grad_tokens, grad_time, g_mask, g_attn, g_mlp, grad_ada, grad_adab, gqkv.reshape(3, width, d).transpose(2, 0, 1), gout, gup, g_upb, gdown, g_db)


def solution(mesh):
    group = ("dp", "tensor")
    in_specs = (P(group, None), P("dp", None), P("dp"), P(group), P(), P(), P(), P(), P(), P(None, None, "tensor"), P("tensor", None), P(None, "tensor"), P("tensor"), P("tensor", None), P(), P(group, None))
    out_specs = (P(group, None), P(group, None), P("dp", None), P(), P(), P(), P(), P(), P(None, None, "tensor"), P("tensor", None), P(None, "tensor"), P("tensor"), P("tensor", None), P())
    return jax.shard_map(per_device, mesh=mesh, in_specs=in_specs, out_specs=out_specs, check_vma=False)
```

```python
import functools

import jax
import jax.numpy as jnp
import numpy as np
from jax import lax
from jax.experimental import pallas as pl
from jax.experimental.pallas import tpu as pltpu
from jax.sharding import PartitionSpec as P

BF = jnp.bfloat16
F = jnp.float32
HD = 64
LEN = 1024
EPS = 1e-05
GELU_COEF = 0.7978845608028654
CUBIC_COEF = 0.044715
SCALE = 0.125
LOG2E = 1.4426950408889634
EXP_SCALE = SCALE * LOG2E
MIB = 1 << 20


def nn(a, b):
    return lax.dot_general(a, b, (((1,), (0,)), ((), ())), preferred_element_type=F)


def nt(a, b):
    return lax.dot_general(a, b, (((1,), (1,)), ((), ())), preferred_element_type=F)


def tn(a, b):
    return lax.dot_general(a, b, (((0,), (0,)), ((), ())), preferred_element_type=F)


def normalize(values):
    centered = values - jnp.mean(values, axis=-1, keepdims=True)
    inv = lax.rsqrt(jnp.mean(centered * centered, axis=-1, keepdims=True) + EPS)
    return centered * inv, inv


def layer_back(grad_norm, normed, inv):
    mean_grad = jnp.mean(grad_norm, axis=-1, keepdims=True)
    mean_cross = jnp.mean(grad_norm * normed, axis=-1, keepdims=True)
    return inv * (grad_norm - mean_grad - normed * mean_cross)


def halves_turned(v):
    parts = []
    for h in range(v.shape[1] // HD):
        lo = v[:, h * HD : h * HD + HD // 2]
        hi = v[:, h * HD + HD // 2 : (h + 1) * HD]
        parts += [-hi, lo]
    return jnp.concatenate(parts, axis=1)


def halves_back(v):
    parts = []
    for h in range(v.shape[1] // HD):
        lo = v[:, h * HD : h * HD + HD // 2]
        hi = v[:, h * HD + HD // 2 : (h + 1) * HD]
        parts += [hi, -lo]
    return jnp.concatenate(parts, axis=1)


def tables(block, heads):
    cos, sin = block[:, :HD], block[:, HD:]
    return jnp.concatenate([cos] * heads, axis=1), jnp.concatenate([sin] * heads, axis=1)


MESH = pl.DeviceIdType.MESH
PIECE = 256
HALVED = 3


def sds(shape, dtype):
    return jax.ShapeDtypeStruct(shape, dtype)


def split3(v):
    hi = v.astype(BF).astype(F)
    mid = (v - hi).astype(BF).astype(F)
    return hi, mid, v - hi - mid


def pick(index, values):
    out = jnp.int32(values[0])
    for i, v in enumerate(values[1:], 1):
        out = jnp.where(index == i, jnp.int32(v), out)
    return out


MLP_ORDER = [(1, 0), (1, 1), (3, 0), (2, 0), (1, 2), (0, 0), (3, 1), (2, 1), (0, 1), (0, 2), (3, 2), (2, 2)]
CROSS = [(768, 256), (1536, 256), (1024, 256), (1792, 256), (1280, 256), (2048, 256), (0, 128), (128, 128), (256, 128), (384, 128), (512, 128), (640, 128)]
SMALL_INPUTS = ("mask", "gain1", "gain2", "dbias", "upb", "adab", "time", "noise")


def block_kernel(n_dp, names, *args):
    ref = dict(zip(names, args))
    g = lambda *keys: [ref[key] for key in keys]
    tok_h, cot_h, prefix, ada_h, table_h, wt_h, wo_h, wu_h, wd_h = g("tok_h", "cot_h", "prefix", "ada_h", "table_h", "wt_h", "wo_h", "wu_h", "wd_h")
    out_o, gtok_o, grads_o, mods_o, small_o, wmu, wmd = g("out_o", "gtok_o", "grads_o", "mods_o", "small_o", "wmu", "wmd")
    w, wsu, wsd, rb, rx, sx, g0, sb, ry, rz, exv = g("w", "wsu", "wsd", "rb", "rx", "sx", "g0", "sb", "ry", "rz", "exv")
    tok, cs, h1o, h1p, q, k, v, att, st, km = g("tok", "cs", "h1o", "h1p", "q", "k", "v", "att", "st", "km")
    branch, mixed, h2, gm, bm, gh, dk, dv, dq, parr, dwo2 = g(
        "branch", "mixed", "h2", "gm", "bm", "gh", "dk", "dv", "dq", "parr", "dwo2"
    )
    vecs, mod, nz, bus, gub, sums, mods, cse, cre, xse, xre, bse, bre = g(
        "vecs", "mod", "nz", "bus", "gub", "sums", "mods", "cse", "cre", "xse", "xre", "bse", "bre"
    )
    rows, d = tok.shape
    width = q.shape[2]
    heads = width // HD
    cond = ada_h.shape[0]
    tile = 256
    dp = lax.axis_index("dp")
    t = lax.axis_index("tensor")
    xb, cb = t // 2, t % 2
    bits = [1 << i for i in range(n_dp.bit_length() - 1)]
    bit = [(dp // b) % 2 for b in bits]
    core = (dp, t + 1 - 2 * cb)
    chip = (dp, t + 2 - 4 * xb)
    peer = [(dp + b - 2 * b * v_, t) for b, v_ in zip(bits, bit)]
    yb = bit[0]

    corner = (dp + 2 - 4 * bit[1] + 4 - 8 * bit[2], t)
    barrier = pltpu.get_barrier_semaphore()
    for other in [core, chip, corner] + peer:
        pl.semaphore_signal(barrier, inc=1, device_id=other, device_id_type=MESH)
    pl.semaphore_wait(barrier, 3 + len(peer))

    def remote(src, dst, name, index, to):
        return pltpu.make_async_remote_copy(
            src_ref=src, dst_ref=dst, send_sem=ref[name + "_s"].at[index], recv_sem=ref[name + "_r"].at[index], device_id=to, device_id_type=MESH
        )

    def local(src, dst, index):
        return pltpu.make_async_copy(src, dst, ref["loc"].at[index])

    def at(start, size, mult=8):
        return pl.ds(start if isinstance(start, int) else pl.multiple_of(start, mult), size)

    att_src = [(wt_h, 0), (wt_h, width), (wt_h, 2 * width), (wo_h, 0)]
    hw = width // 2

    def part(r, j, which):
        if j < 4:
            return w.at[r, at(j * width + which * hw, hw, 32)]
        c, kind = (j - 4) // 2, (j - 4) % 2
        span = at(c * PIECE + which * 128, 128, 128)
        return wmd.at[r, span] if kind else wmu.at[r, :, span]

    def own_part(j, which):
        if j < 4:
            src, base = att_src[j]
            return src.at[at(base + which * hw, hw, 32)]
        c, kind = (j - 4) // 2, (j - 4) % 2
        span = at(c * PIECE + which * 128, 128, 128)
        return wd_h.at[span] if kind else wu_h.at[:, span]

    def far(j):
        return remote(own_part(j, yb), part(2, j, yb), "far", j, chip)

    def side(j):
        return remote(part(2, j, yb), part(2, j, yb), "side", j, peer[0])

    def cross(j, which):
        p = part(2, j, (yb + which) % 2)
        return remote(p, part(3, j, (yb + which) % 2), "cross", 2 * j + which, core)

    near = [
        remote(wt_h, w.at[1, pl.ds(0, 3 * width)], "near", 0, core),
        remote(wo_h, w.at[1, pl.ds(3 * width, width)], "near", 1, core),
        remote(wu_h, wmu.at[1], "near", 2, core),
        remote(wd_h, wmd.at[1], "near", 3, core),
    ]
    n_parts = 10

    def arrived(j):
        far(j).wait_recv()
        side(j).start()
        cross(j, 0).start()

    def passed(j):
        side(j).wait_recv()
        cross(j, 1).start()

    ada = sb
    loads = [local(ada_h.at[:, pl.ds(i * d, d)], ada.at[pl.ds(i * cond, cond)], i) for i in range(6)]
    load_tok, load_cot = local(tok_h, tok, 6), local(cot_h, h2, 7)
    load_cs = [local(table_h.at[at(cb * rows, rows)], cs.at[pl.ds(0, rows)], 8), local(table_h.at[at((1 - cb) * rows, rows)], cs.at[pl.ds(rows, rows)], 9)]
    load_w = [local(wt_h, w.at[0, pl.ds(0, 3 * width)], 10), local(wo_h, w.at[0, pl.ds(3 * width, width)], 11)]
    load_small = [local(ref[name], ref[name + "_v"], 52 + i) for i, name in enumerate(SMALL_INPUTS)]
    mask_v, gain1_v, gain2_v, dbias_v, upb_v, adab_v, time_v, noise_v = [ref[name + "_v"] for name in SMALL_INPUTS]
    for c in load_small + loads + [load_tok]:
        c.start()
    for c in load_small:
        c.wait()
    bus[0] = jnp.broadcast_to(upb_v[...].astype(F).reshape(1, -1), bus.shape[1:])
    bias_near, bias_far = remote(bus.at[0], bus.at[1], "bias", 0, core), remote(bus.at[0], bus.at[2], "bias", 1, chip)
    bias_cross = remote(bus.at[2], bus.at[3], "bias", 2, core)
    bias_near.start()
    bias_far.start()
    for j in range(n_parts):
        far(j).start()
    near[0].start()
    for c in load_w + load_cs + [load_cot]:
        c.start()

    for i, one in enumerate((mask_v, gain1_v, gain2_v, dbias_v)):
        vecs[i : i + 1, :] = one[...].astype(F).reshape(1, d)
    tv = jnp.where(xb == 0, time_v[0:1, :].astype(F), time_v[1:2, :].astype(F))
    s = jnp.broadcast_to(tv, (16, cond))
    s = s / (1.0 + jnp.exp(-s))
    stacked = jnp.concatenate(split3(s), axis=0).astype(BF)
    for i in range(6):
        loads[i].wait()
        m = nn(stacked, ada[pl.ds(i * cond, cond), :])
        mod[i : i + 1, :] = m[0:1] + m[16:17] + m[32:33] + adab_v[pl.ds(i * d, d)].astype(F).reshape(1, d)
    place = lax.broadcasted_iota(jnp.int32, (4, 128), 0) * 128 + lax.broadcasted_iota(jnp.int32, (4, 128), 1) + cb * rows
    limit = jnp.where(xb == 0, prefix[0], prefix[1])
    on = jnp.where((noise_v[...] == 1) & (place >= limit), 1.0, 0.0)
    on = jnp.concatenate([on, jnp.zeros((12, 128), F)], axis=0).astype(BF)
    eye = jnp.where(lax.broadcasted_iota(jnp.int32, (128, 128), 0) == lax.broadcasted_iota(jnp.int32, (128, 128), 1), 1.0, 0.0).astype(BF)
    cols = nt(eye, on)
    for i in range(4):
        nz[i * 128 : (i + 1) * 128, :] = cols[:, i : i + 1]
    load_tok.wait()

    def inputs_at(rs):
        return jnp.where(nz[rs, :] > 0.5, vecs[0:1, :], tok[rs, :].astype(F))

    every = pl.ds(0, rows)
    n1, _ = normalize(inputs_at(every))
    h1o[...] = (n1 * vecs[1:2, :] * (1.0 + mod[1:2, :]) + mod[0:1, :]).astype(BF)
    h1_copy = remote(h1o, h1p, "h1", 0, core)
    h1_copy.start()
    load_cot.wait()
    gmv = (mod[5:6, :] * h2[...].astype(F)).astype(BF)
    gm[...] = gmv
    sums[4:5, :] = jnp.sum(gmv.astype(F), axis=0, keepdims=True)
    for c in load_cs + load_w[:1]:
        c.wait()
    h1_copy.wait()
    for c in near[1:]:
        c.start()

    lane_q = lax.broadcasted_iota(jnp.int32, (rows, width), 1) // HD
    lane = lax.broadcasted_iota(jnp.int32, (tile, width), 1) // HD
    lane_s = lax.broadcasted_iota(jnp.int32, (tile, 128), 1)

    def project(r):
        cos, sin = tables(cs[0:rows, :], heads)
        qv = nt(h1o[...], w[r, 0:width, :])
        qv = (qv * cos + halves_turned(qv) * sin).astype(BF)
        q[r] = qv
        qf = qv.astype(F)
        for h in range(heads):
            km[h, 0:rows, :] = jnp.where(lane_q == h, qf, 0.0).astype(BF)
        kv = nt(h1o[...], w[r, width : 2 * width, :])
        k[r, 0:rows, :] = (kv * cos + halves_turned(kv) * sin).astype(BF)
        v[r, 0:rows, :] = nt(h1o[...], w[r, 2 * width : 3 * width, :]).astype(BF)
        cos, sin = tables(cs[rows : 2 * rows, :], heads)
        kv = nt(h1p[...], w[r, width : 2 * width, :])
        k[r, rows : 2 * rows, :] = (kv * cos + halves_turned(kv) * sin).astype(BF)
        v[r, rows : 2 * rows, :] = nt(h1p[...], w[r, 2 * width : 3 * width, :]).astype(BF)

    def attend(r, i):
        rs = at(i * tile, tile, tile)
        acc = jnp.zeros((tile, width), F)
        stats = jnp.zeros((tile, 128), F)
        for h in range(heads):
            s = nt(km[h, rs, :], k[r])
            m = jnp.max(s, axis=1, keepdims=True)
            e = jnp.exp2((s - m) * EXP_SCALE)
            total = jnp.sum(e, axis=1, keepdims=True)
            p = (e * (1.0 / total)).astype(BF)
            acc = jnp.where(lane == h, nn(p, v[r]), acc)
            stats = jnp.where(lane_s == h, m * EXP_SCALE + jnp.log2(total), stats)
        att[r, rs, :] = acc.astype(BF)
        dq[rs, 0:128] = stats

    def at_step(step, todo):
        for key, fns in todo.items():

            @pl.when(step == key)
            def _():
                for fn in fns:
                    fn()

    def wait_near(i):
        return near[i].wait_recv

    def wait_cross(j):
        def go():
            cross(j, 0).wait_recv()
            cross(j, 1).wait_recv()

        return go

    arrive = lambda j: functools.partial(arrived, j)
    go_on = lambda j: functools.partial(passed, j)
    per_r = rows // tile

    def bias_on():
        bias_far.wait_recv()
        bias_cross.start()

    fwd_plan = {
        0: [arrive(0)],
        1: [arrive(1), bias_on],
        2: [wait_near(0), arrive(2), go_on(0)],
        3: [arrive(3), go_on(1)],
        4: [go_on(2)],
        5: [arrive(4), go_on(3)],
        6: [wait_cross(0), wait_cross(1), wait_cross(2)],
        7: [arrive(5), go_on(4)],
    }

    def fwd_body(it, carry):
        r, i = it // per_r, it % per_r
        at_step(it, fwd_plan)

        @pl.when(i == 0)
        def _():
            project(r)

        attend(r, i)

        @pl.when(i == per_r - 1)
        def _():
            st[r] = dq[:, 0:128].T[0:8, :]

        return carry

    lax.fori_loop(0, 4 * per_r, fwd_body, 0)
    arrived(6)
    load_w[1].wait()
    wait_near(1)()
    wait_cross(3)()

    def mid_body(i, carry):
        rs = at(i * tile, tile, tile)
        b = nn(att[0, rs, :], w[0, 3 * width : 4 * width, :])
        for r in range(1, 4):
            b = b + nn(att[r, rs, :], w[r, 3 * width : 4 * width, :])
        x = inputs_at(rs) + mod[2:3, :] * b
        n2, _ = normalize(x)
        branch[rs, :] = b
        mixed[rs, :] = x
        h2[rs, :] = (n2 * vecs[2:3, :] * (1.0 + mod[4:5, :]) + mod[3:4, :]).astype(BF)
        bm[rs, :] = jnp.zeros((tile, d), F)
        gh[rs, :] = jnp.zeros((tile, d), F)
        return carry

    lax.fori_loop(0, per_r, mid_body, 0)
    load_cot = local(cot_h, tok, 7)
    load_cot.start()

    def cross_send(n):
        base, size = CROSS[n]
        return remote(sx.at[pl.ds(base, size)], rx.at[pl.ds(base, size)], "gx", n, chip)

    def line_peer(m):
        return (dp + (2 - 4 * bit[1] if m & 2 else 0) + (4 - 8 * bit[2] if m & 1 else 0), t)

    def half_at(n, other=False):
        base, size = CROSS[n]
        return at(base + ((1 - yb) if other else yb) * (size // 2), size // 2, 16)

    def line_at(n, m=0):
        base, size = CROSS[n]
        rank = 2 * (1 - bit[1] if m & 2 else bit[1]) + (1 - bit[2] if m & 1 else bit[2])
        return at(base + yb * (size // 2) + rank * (size // 8), size // 8, 16)

    def out_half(n):
        base, size = CROSS[n]
        return pl.ds(base, size // 2)

    def out_line(n, m):
        base, size = CROSS[n]
        return pl.ds(base + size // 2 + (m - 1) * (size // 8), size // 8)

    def in_half(n):
        base, size = CROSS[n]
        return pl.ds(base // 2, size // 2)

    def in_line(n, m):
        base, size = CROSS[n]
        return pl.ds(base * 3 // 8 + (m - 1) * (size // 8), size // 8)

    def send_y(n):
        return remote(rx.at[out_half(n)], ry.at[in_half(n)], "gy", n, peer[0])

    def send_line(n, m):
        return remote(rx.at[out_line(n, m)], rz.at[in_line(n, m)], "gz", 3 * n + m - 1, line_peer(m))

    def back_far(n):
        return remote(sx.at[line_at(n)], sx.at[line_at(n)], "aw", n, peer[2])

    def back_near(n):
        base, size = CROSS[n]
        two = at(base + yb * (size // 2) + bit[1] * (size // 4), size // 4, 16)
        return remote(sx.at[two], sx.at[two], "az", n, peer[1])

    def back_y(n):
        return remote(sx.at[half_at(n)], sx.at[half_at(n)], "ay", n, peer[0])

    def more(e, n):
        return remote(g0.at[line_at(n)], ref["ex"].at[e, n, pl.ds(0, CROSS[n][1] // 8)], "ge", e * len(CROSS) + n, peer[HALVED + e])

    def stage_x(n):
        base, size = CROSS[n]
        cross_send(n).wait()
        g0[pl.ds(base, size), :] = g0[pl.ds(base, size), :] + rx[pl.ds(base, size), :].astype(F)
        rx[out_half(n), :] = g0[half_at(n, True), :].astype(BF)
        send_y(n).start()

    def stage_y(n):
        send_y(n).wait_recv()
        g0[half_at(n), :] = g0[half_at(n), :] + ry[in_half(n), :].astype(F)
        for m in (1, 2, 3):
            rx[out_line(n, m), :] = g0[line_at(n, m), :].astype(BF)
            send_line(n, m).start()

    def stage_z(n):
        for m in (1, 2, 3):
            send_line(n, m).wait_recv()
        got = [rz[in_line(n, m), :].astype(F) for m in (1, 2, 3)]
        total = g0[line_at(n), :] + ((got[0] + got[1]) + got[2])
        for e in range(len(bits) - HALVED):
            g0[line_at(n), :] = total
            more(e, n).start()
            more(e, n).wait()
            room = pl.ds(0, CROSS[n][1] // 8)
            fill = local(ref["ex"].at[e, n, room], exv.at[room], 36)
            fill.start()
            fill.wait()
            total = total + exv[room, :]
        sx[line_at(n), :] = total.astype(BF)
        back_far(n).start()

    def stage_a(n):
        back_far(n).wait_recv()
        back_near(n).start()

    def stage_b(n):
        back_near(n).wait_recv()
        back_y(n).start()

    def result(n):
        base, size = CROSS[n]
        return local(sx.at[pl.ds(base, size)], grads_o.at[pl.ds(base, size)], 14 + n)

    def stage_c(n):
        back_y(n).wait_recv()
        result(n).start()

    def stage_end(n):
        send_y(n).wait_send()
        for m in (1, 2, 3):
            send_line(n, m).wait_send()
        back_far(n).wait_send()
        back_near(n).wait_send()
        back_y(n).wait_send()
        result(n).wait()

    stages = dict(X=stage_x, Y=stage_y, Z=stage_z, A=stage_a, B=stage_b, C=stage_c)

    def run(text):
        for i in range(0, len(text), 2):
            stages[text[i]](int(text[i + 1], 16))

    steps = len(MLP_ORDER)

    def core_slot(step):
        return 2 * (sum(1 for r, _ in MLP_ORDER[:step] if r % 2) % 3)

    def give(step, kind):
        r, c = MLP_ORDER[step]
        slot = core_slot(step) + kind
        row = (3 * kind + c) * PIECE
        return remote(sb.at[pl.ds(slot * PIECE, PIECE)], rb.at[r // 2, pl.ds(row, PIECE)], "give", 2 * step + kind, core)

    def fetch(step, slot, own):
        r = pick(step, [r for r, _ in MLP_ORDER])
        c = pick(step, [c for _, c in MLP_ORDER])
        span = at(c * PIECE, PIECE, PIECE)
        up, down = (wu_h, wd_h) if own else (wmu.at[r], wmd.at[r])
        return [
            pltpu.make_async_copy(up.at[:, span], wsu.at[slot], ref["wst"].at[slot, 0]),
            pltpu.make_async_copy(down.at[span], wsd.at[slot], ref["wst"].at[slot, 1]),
        ]

    bias_near.wait_recv()
    for i in (2, 3):
        near[i].wait_recv()
    for c in fetch(0, 0, False):
        c.start()

    mlp_plan = {
        0: [go_on(5)],
        1: [wait_cross(4), wait_cross(5), arrive(7), go_on(6)],
        3: [arrive(8), go_on(7)],
        5: [wait_cross(6), wait_cross(7), arrive(9)],
        7: [go_on(8)],
        9: [go_on(9), wait_cross(8), wait_cross(9)],
    }

    def mlp_body(step, carry):
        slot = step % 2
        r = pick(step, [r for r, _ in MLP_ORDER])
        c = pick(step, [c for _, c in MLP_ORDER])
        at_step(step, mlp_plan)
        for cp in fetch(step, slot, False):
            cp.wait()

        nxt = pick(step, [r for r, _ in MLP_ORDER[1:]] + [4])

        @pl.when((nxt > 0) & (nxt < 4))
        def _():
            for cp in fetch(step + 1, 1 - slot, False):
                cp.start()

        @pl.when(nxt == 0)
        def _():
            for cp in fetch(step + 1, 1 - slot, True):
                cp.start()

        @pl.when(step == 0)
        def _():
            bias_cross.wait_recv()

        cols = at(c * PIECE, PIECE, PIECE)
        u = nn(h2[...], wsu[slot]) + bus[r, 0:1, cols]
        th = jnp.tanh(GELU_COEF * (u + CUBIC_COEF * u * u * u))
        act = (0.5 * u * (1.0 + th)).astype(BF)
        slope = 0.5 * (1.0 + th) + 0.5 * u * (1.0 - th * th) * GELU_COEF * (1.0 + 3.0 * CUBIC_COEF * u * u)
        gu_f = (nt(gm[...], wsd[slot]) * slope).astype(BF).astype(F)
        gu = gu_f.astype(BF)
        gub[r, 0:1, cols] = jnp.sum(gu_f, axis=0, keepdims=True)
        bm[...] += nn(act, wsd[slot])
        gh[...] += nt(gu, wsu[slot])
        ds_ = (tn(gu, h2[...]), tn(act, gm[...]))
        for i, (r_, c_) in enumerate(MLP_ORDER):

            @pl.when(step == i)
            def _():
                rows_ = [pl.ds((3 + 3 * kind + c_) * PIECE, PIECE) for kind in range(2)]
                inbox = [pl.ds((3 * kind + c_) * PIECE, PIECE) for kind in range(2)]
                if r_ % 2:
                    before = [j for j in range(i) if MLP_ORDER[j][0] % 2 and core_slot(j) == core_slot(i)]
                    for kind in range(2):
                        if before:
                            give(before[-1], kind).wait_send()
                        sb[pl.ds((core_slot(i) + kind) * PIECE, PIECE), :] = ds_[kind].astype(BF)
                        give(i, kind).start()
                else:
                    origin = MLP_ORDER.index((r_ + 1, c_))
                    for kind in range(2):
                        give(origin, kind).wait_recv()
                        total = ds_[kind] + rb[r_ // 2, inbox[kind], :].astype(F)
                        if r_ == 2:
                            sx[rows_[kind], :] = total.astype(BF)
                            cross_send(CROSS.index(((3 + 3 * kind + c_) * PIECE, PIECE))).start()
                        else:
                            g0[rows_[kind], :] = total

        return carry

    lax.fori_loop(0, steps, mlp_body, 0)
    odd = [i for i, (r, _) in enumerate(MLP_ORDER) if r % 2]
    for i in odd[-3:]:
        for kind in range(2):
            give(i, kind).wait_send()

    load_cot.wait()
    run("X0")
    gba = h1p

    def post_body(i, carry):
        rs = at(i * tile, tile, tile)
        x = mixed[rs, :]
        n2, inv = normalize(x)
        c = tok[rs, :].astype(F)
        bmlp = bm[rs, :] + vecs[3:4, :]
        h2[rs, :] = (x + mod[5:6, :] * bmlp).astype(BF)
        gr = gh[rs, :]
        gs = gr * (1.0 + mod[4:5, :])
        gmix = c + layer_back(gs * vecs[2:3, :], n2, inv)
        mixed[rs, :] = gmix
        gba[rs, :] = (mod[2:3, :] * gmix).astype(BF)
        part_sums = [gs * n2, gmix * branch[rs, :], gr, gr * n2 * vecs[2:3, :], c * bmlp]
        for row, val in zip((3, 10, 11, 12, 13), part_sums):
            got = jnp.sum(val, axis=0, keepdims=True)

            @pl.when(i == 0)
            def _():
                sums[row : row + 1, :] = got

            @pl.when(i > 0)
            def _():
                sums[row : row + 1, :] += got

        return carry

    lax.fori_loop(0, per_r, post_body, 0)
    store_out = local(h2, out_o, 26)
    store_out.start()
    load_tok = local(tok_h, tok, 6)
    load_tok.start()
    for r in range(4):
        wo = w[r, 3 * width : 4 * width, :]
        dw = tn(att[r], gba[...])
        att[r] = nt(gba[...], wo).astype(BF)
        if r == 0:
            g0[pl.ds(3 * width, width), :] = dw
        elif r == 2:
            dwo2[...] = dw
        else:
            sb[pl.ds((3 - r) // 2 * 4 * width + 3 * width, width), :] = dw.astype(BF)

    lane_k = lax.broadcasted_iota(jnp.int32, (2 * rows, width), 1) // HD

    def back_tile(r, i, it):
        @pl.when(i == 0)
        def _():
            kf = k[r].astype(F)
            for h in range(heads):
                km[h] = jnp.where(lane_k == h, kf, 0.0).astype(BF)
            dk[...] = jnp.zeros_like(dk)
            dv[...] = jnp.zeros_like(dv)

        rs = at(i * tile, tile, tile)
        qt = q[r, rs, :].astype(F)
        gt = att[r, rs, :].astype(F)
        acc = jnp.zeros((tile, width), F)
        for h in range(heads):
            back_events(it, h)
            qm = jnp.where(lane == h, qt, 0.0).astype(BF)
            gmh = jnp.where(lane == h, gt, 0.0).astype(BF)
            p = jnp.exp2(nt(k[r], qm) * EXP_SCALE - st[r, h : h + 1, rs])
            dpr = nt(v[r], gmh)
            inner = jnp.sum(p * dpr, axis=0, keepdims=True)
            ds_ = (p * (dpr - inner)).astype(BF)
            dv[...] += nn(p.astype(BF), gmh)
            dk[...] += nn(ds_, qm)
            acc = acc + tn(ds_, km[h])
        dq[rs, :] = acc

    def par_copy(r):
        lanes = pl.ds((r % 2) * 2 * width, 2 * width)
        return remote(branch.at[:, lanes], parr.at[r % 2], "par", r, core)

    def finish_back(r):
        cos, sin = tables(cs[0:rows, :], heads)
        gq = dq[...] * SCALE
        q[r] = (gq * cos + halves_back(gq * sin)).astype(BF)
        lanes = slice((r % 2) * 2 * width, (r % 2) * 2 * width + 2 * width)
        bm[:, lanes] = jnp.concatenate([dk[0:rows, :] * SCALE, dv[0:rows, :]], axis=1)
        if r < 2:
            par_copy(r + 2).wait_send()
            if r == 1:
                pl.semaphore_wait(ref["credit"], 1)
        branch[:, lanes] = jnp.concatenate([dk[rows : 2 * rows, :] * SCALE, dv[rows : 2 * rows, :]], axis=1)
        par_copy(r).start()

    def hand(r):
        base = (3 - r) // 2 * 4 * width
        return remote(sb.at[pl.ds(base, 4 * width)], rb.at[r // 2, pl.ds(0, 4 * width)], "hand", r // 2, core)

    def weight_grads(r):
        par_copy(r ^ 1).wait_recv()
        cos, sin = tables(cs[0:rows, :], heads)
        lanes = slice((r % 2) * 2 * width, (r % 2) * 2 * width + 2 * width)
        gkv = bm[:, lanes] + parr[(r ^ 1) % 2]
        gk = gkv[:, :width]
        gk = (gk * cos + halves_back(gk * sin)).astype(BF)
        gv = gkv[:, width:].astype(BF)
        parts = (q[r], gk, gv)
        if r % 2 == 0:
            hand(r + 1).wait_recv()
        back = 0.0 if r == 3 else gh[...]
        for i, p_ in enumerate(parts):
            place_ = pl.ds(i * width, width)
            back = back + nn(p_, w[r, i * width : (i + 1) * width, :])
            dw = tn(p_, h1o[...])
            if r % 2:
                sb[pl.ds((3 - r) // 2 * 4 * width + i * width, width), :] = dw.astype(BF)
            else:
                dw = dw + rb[r // 2, place_, :].astype(F)
                if r == 2:
                    sx[place_, :] = dw.astype(BF)
                else:
                    g0[place_, :] = dw
        gh[...] = back
        place_ = pl.ds(3 * width, width)
        if r % 2:
            hand(r).start()
        elif r == 2:
            sx[place_, :] = (dwo2[...] + rb[1, place_, :].astype(F)).astype(BF)
            for n in range(6, len(CROSS)):
                cross_send(n).start()
        else:
            g0[place_, :] = g0[place_, :] + rb[0, place_, :].astype(F)

    def give_credit():
        pl.semaphore_signal(ref["credit"], inc=1, device_id=core, device_id_type=MESH)

    back_plan = [
        {0: "X1", 2: "Y1X2", 4: "Z1Y2", 5: "A1Y3X4B0Z2", 7: "Y4Z3X5"},
        {4: "X3A0", 6: "B1", 7: "A2"},
        {0: "Y0", 2: "Z0"},
    ]

    def back_events(it, h):
        at_step(it, {key: [functools.partial(run, text)] for key, text in back_plan[h].items()})

    def back_body(it, carry):
        i = it % per_r
        back_tile(3 - it // per_r, i, it)
        for r in range(4):

            @pl.when(it == (3 - r) * per_r + per_r - 1)
            def _():
                finish_back(r)

        @pl.when(it == 2 * per_r)
        def _():
            weight_grads(3)
            weight_grads(2)
            give_credit()

        return carry

    lax.fori_loop(0, 4 * per_r, back_body, 0)
    run("C0")
    weight_grads(1)
    run("Z4C1")
    weight_grads(0)

    hand(1).wait_send()
    hand(3).wait_send()
    store_out.wait()
    load_tok.wait()
    run("X6X7B2A3Y5X8")

    def tail_body(i, carry):
        rs = at(i * tile, tile, tile)
        on_ = nz[rs, :] > 0.5
        n1_, inv = normalize(inputs_at(rs))
        gr = gh[rs, :]
        gs = gr * (1.0 + mod[1:2, :])
        gi = mixed[rs, :] + layer_back(gs * vecs[1:2, :], n1_, inv)
        mixed[rs, :] = jnp.where(on_, 0.0, gi)
        part_sums = [gs * n1_, jnp.where(on_, gi, 0.0), gr, gr * n1_ * vecs[1:2, :]]
        for row, val in zip((1, 2, 8, 9), part_sums):
            got = jnp.sum(val, axis=0, keepdims=True)

            @pl.when(i == 0)
            def _():
                sums[row : row + 1, :] = got

            @pl.when(i > 0)
            def _():
                sums[row : row + 1, :] += got

        return carry

    lax.fori_loop(0, per_r, tail_body, 0)
    store_tok = local(mixed, gtok_o, 27)
    store_tok.start()
    run("A4")

    none = jnp.zeros((2, d), F)
    cse[0:8, :] = jnp.concatenate([sums[8:14, :], none], axis=0)
    cse[8:16, :] = jnp.concatenate([gub[1, 0:1, :], gub[3, 0:1, :], sums[1:5, :], none], axis=0)
    core_sum = remote(cse, cre, "sc", 0, core)
    core_sum.start()
    me = 2 * dp + xb
    chip_sum = remote(xse, xre, "sx", 0, chip)
    chip_mods = remote(mods.at[me], mods.at[me], "sx", 1, chip)

    def peer_sums(i):
        block = pl.ds((dp // bits[i]) * bits[i] * 2, 2 * bits[i])
        return remote(bse.at[i], bre.at[i], "sd", 2 * i, peer[i]), remote(mods.at[block], mods.at[block], "sd", 2 * i + 1, peer[i])

    def sums_on(i):
        if i == 0:
            core_sum.wait_recv()
            tv_row = jnp.concatenate([tv, jnp.zeros((1, d - cond), F)], axis=1)
            mods[me] = jnp.concatenate([cse[0:6, :] + cre[0:6, :], tv_row, jnp.zeros((1, d), F)], axis=0)
            xse[...] = jnp.concatenate([gub[2, 0:1, :] + cre[9:10, :], cse[10:14, :] + cre[10:14, :], jnp.zeros((3, d), F)], axis=0)
            chip_sum.start()
            chip_mods.start()
            return
        if i == 1:
            chip_sum.wait_recv()
            cur = jnp.concatenate([gub[0, 0:1, :] + cre[8:9, :] + xre[0:1, :], xse[1:8, :] + xre[1:8, :]], axis=0)
            chip_mods.wait()
        else:
            one, two = peer_sums(i - 2)
            one.wait_recv()
            two.wait()
            cur = bse[i - 2] + bre[i - 2]
        if i - 1 < len(bits):
            bse[i - 1] = cur
            for c in peer_sums(i - 1):
                c.start()
        else:
            small_o[...] = cur

    run("Y6X9B3Y7")
    sums_on(0)
    run("Z5XaB4C2Z6Y8")
    sums_on(1)
    run("XbZ7A5Y9A6Z8C3A7")
    for i in range(2, len(bits) - 1):
        sums_on(i)
    run("B5YaZ9B6A8B7C4Za")
    sums_on(len(bits) - 1)
    run("YbA9B8AaC5ZbB9C6")
    sums_on(len(bits))
    run("BaC7AbC8C9Bb")
    sums_on(len(bits) + 1)
    store_mods = local(mods, mods_o, 28)
    store_mods.start()
    run("CaCb")
    for n in range(len(CROSS)):
        stage_end(n)
    for c in [store_mods, store_tok]:
        c.wait()
    for c in [core_sum, chip_sum] + [peer_sums(i)[0] for i in range(len(bits))]:
        c.wait_send()
    for c in near + [bias_near, bias_far, bias_cross]:
        c.wait_send()
    for j in range(n_parts):
        far(j).wait_send()
        side(j).wait_send()
        cross(j, 0).wait_send()
        cross(j, 1).wait_send()
    for r in range(2):
        par_copy(r).wait_send()


def finish_kernel(n_dp, grads_h, out_h, tok_h, mods_h, small, ada_h, time, out_o, gtok_o, gqkv_o, gout_o, gup_o, gdown_o, gada_o, gtime_o, gadab_o, gmask_o, ga_o, gm_o, gub_o, gdb_o, grads, wide, outv, tokv, mods, ada, adag, sem):
    d = grads.shape[1]
    width = gout_o.shape[0]
    cond = ada.shape[0]
    seqs = mods.shape[0]
    dp = lax.axis_index("dp")

    def copy(src, dst, index):
        return pltpu.make_async_copy(src, dst, sem.at[index])

    span = lambda p: pl.ds(p * PIECE, PIECE)
    load_mods, load_ada = copy(mods_h, mods, 0), copy(ada_h, ada, 1)
    load_tok, load_out = copy(tok_h, tokv, 2), copy(out_h, outv, 3)
    pieces = [copy(grads_h.at[span(p)], grads.at[span(p)], 4 + p) for p in range(9)]
    for c in [load_mods] + pieces + [load_tok, load_out, load_ada]:
        c.start()
    stores = []

    def store(src, dst):
        stores.append(copy(src, dst, 13 + len(stores)))
        stores[-1].start()

    head = 3 * width
    for p in range(9):
        pieces[p].wait()
        if 3 <= p < 6:
            for b in range(3):
                wide[span(p), span(b)] = grads[span(p), span(b)].astype(F).T
                store(wide.at[span(p), span(b)], gup_o.at[span(b), span(p - 3)])
        else:
            wide[span(p), :] = grads[span(p), :].astype(F)
            if p >= 6:
                store(wide.at[span(p)], gdown_o.at[span(p - 6)])
            elif p == 2:
                store(wide.at[pl.ds(0, head)], gqkv_o)
                store(wide.at[pl.ds(head, width)], gout_o)
    load_tok.wait()
    store(tokv, gtok_o)
    load_out.wait()
    store(outv, out_o)
    load_mods.wait()
    total = mods[0]
    for s_ in range(1, seqs):
        total = total + mods[s_]
    tall = jnp.concatenate([mods[s_, 6:7, 0:cond] for s_ in range(seqs)], axis=0)
    left = split3(tall / (1.0 + jnp.exp(-tall)))
    lhs = jnp.concatenate([left[0], left[0], left[1], left[0], left[2], left[1]], axis=0).astype(BF)
    for j in range(6):
        gadab_o[pl.ds(j * d, d)] = total[j : j + 1, :].reshape(d)
        right = split3(jnp.concatenate([mods[s_, j : j + 1, :] for s_ in range(seqs)], axis=0))
        rhs = jnp.concatenate([right[0], right[1], right[0], right[2], right[0], right[1]], axis=0).astype(BF)
        adag[j] = tn(lhs, rhs)
        store(adag.at[j], gada_o.at[:, pl.ds(j * d, d)])
    load_ada.wait()
    acc = jnp.zeros((48, cond), F)
    for j in range(6):
        pairs = jnp.concatenate([mods[2 * dp, j : j + 1, :], mods[2 * dp + 1, j : j + 1, :], jnp.zeros((14, d), F)], axis=0)
        acc = acc + nt(jnp.concatenate(split3(pairs), axis=0).astype(BF), ada[:, pl.ds(j * d, d)])
    te = time[...].astype(F)
    sig = 1.0 / (1.0 + jnp.exp(-te))
    gtime_o[...] = (acc[0:2] + acc[16:18] + acc[32:34]) * sig * (1.0 + te * (1.0 - sig))
    for row, o in enumerate((gub_o, ga_o, gmask_o, gm_o, gdb_o)):
        o[...] = small[row : row + 1, :].reshape(d)
    for c in stores:
        c.wait()


def rotary_block():
    freq = np.float32(10000.0) ** (np.float32(-2.0) * np.arange(HD // 2, dtype=np.float32) / np.float32(HD))
    angle = np.arange(LEN, dtype=np.float32)[:, None] * freq[None, :].astype(np.float32)
    angle = np.concatenate([angle, angle], axis=1)
    return np.concatenate([np.cos(angle), np.sin(angle)], axis=1).astype(np.float32)


def per_device(tokens, time_emb, prefix_len, noise_mask, mask_embed, gain_attn, gain_mlp, ada_weight, ada_bias, qkv_weight, out_weight, up_weight, up_bias, down_weight, down_bias, cotangent):
    rows, d = tokens.shape
    n_dp = lax.axis_size("dp")
    width = qkv_weight.shape[2]
    cond = time_emb.shape[1]
    hidden = up_weight.shape[1]
    n_bits = n_dp.bit_length() - 1
    assert lax.axis_size("tensor") == 4 and time_emb.shape[0] == 2 and 2 * rows == LEN
    assert n_dp == 1 << n_bits and n_bits >= HALVED and 4 * width == hidden == 3 * PIECE == d
    wt = qkv_weight.transpose(1, 2, 0).reshape(3 * width, d)
    table = jnp.asarray(rotary_block())
    a = pl.BlockSpec(memory_space=pl.ANY)
    m = pl.BlockSpec(memory_space=pltpu.VMEM)
    smem = pl.BlockSpec(memory_space=pltpu.SMEM)
    total = 4 * width + 2 * hidden
    noise = noise_mask.reshape(4, rows // 4)
    small_in = (mask_embed, gain_attn, gain_mlp, down_bias, up_bias, ada_bias, time_emb, noise)
    ins = [("tok_h", tokens, a), ("cot_h", cotangent, a), ("prefix", prefix_len, smem)]
    ins += [(name, value, a) for name, value in zip(SMALL_INPUTS, small_in)]
    ins += [("ada_h", ada_weight, a), ("table_h", table, a), ("wt_h", wt, a), ("wo_h", out_weight, a), ("wu_h", up_weight, a), ("wd_h", down_weight, a)]
    outs = [
        ("out_o", (rows, d), BF, a), ("gtok_o", (rows, d), F, a), ("grads_o", (total, d), BF, a), ("mods_o", (2 * n_dp, 8, d), F, a), ("small_o", (8, d), F, m),
        ("wmu", (4, d, hidden), BF, a), ("wmd", (4, hidden, d), BF, a),
    ]
    n_pieces = len(CROSS)
    extra = max(n_bits - HALVED, 1)
    if n_bits > HALVED:
        outs.append(("ex", (extra, n_pieces, 32, d), F, a))
    vmem = [
        ("w", (4, 4 * width, d), BF), ("wsu", (2, d, PIECE), BF), ("wsd", (2, PIECE, d), BF), ("rb", (2, 2 * hidden, d), BF), ("rx", (total, d), BF), ("sx", (total, d), BF),
        ("g0", (total, d), F), ("sb", (6 * PIECE, d), BF), ("ry", (total // 2, d), BF), ("rz", (total * 3 // 8, d), BF), ("exv", (32, d), F),
        ("tok", (rows, d), BF), ("cs", (2 * rows, 2 * HD), F), ("h1o", (rows, d), BF), ("h1p", (rows, d), BF),
        ("q", (4, rows, width), BF), ("k", (4, 2 * rows, width), BF), ("v", (4, 2 * rows, width), BF), ("att", (4, rows, width), BF), ("st", (4, 8, rows), F),
        ("km", (width // HD, 2 * rows, width), BF), ("branch", (rows, d), F), ("mixed", (rows, d), F), ("h2", (rows, d), BF), ("gm", (rows, d), BF),
        ("bm", (rows, d), F), ("gh", (rows, d), F), ("dk", (2 * rows, width), F), ("dv", (2 * rows, width), F), ("dq", (rows, width), F),
        ("parr", (2, rows, 2 * width), F), ("dwo2", (width, d), F), ("vecs", (8, d), F), ("mod", (8, d), F), ("nz", (rows, 1), F),
        ("bus", (4, 8, hidden), F), ("gub", (4, 8, hidden), F), ("sums", (16, d), F), ("mods", (2 * n_dp, 8, d), F), ("cse", (16, d), F), ("cre", (16, d), F),
        ("xse", (8, d), F), ("xre", (8, d), F), ("bse", (n_bits, 8, d), F), ("bre", (n_bits, 8, d), F),
    ]
    vmem += [(name + "_v", value.shape, value.dtype) for name, value in zip(SMALL_INPUTS, small_in)]
    pairs = [
        ("far", 10), ("side", 10), ("cross", 20), ("near", 4), ("bias", 3), ("h1", 1), ("give", 24), ("gx", n_pieces), ("gy", n_pieces), ("gz", 3 * n_pieces), ("aw", n_pieces), ("az", n_pieces), ("ay", n_pieces),
        ("ge", n_pieces * extra), ("par", 4), ("hand", 2), ("sc", 1), ("sx", 2), ("sd", 2 * n_bits),
    ]
    dma = pltpu.SemaphoreType.DMA
    sems = [("loc", dma((60,))), ("wst", dma((2, 2))), ("credit", pltpu.SemaphoreType.REGULAR)]
    for name, n in pairs:
        sems += [(name + "_s", dma((n,))), (name + "_r", dma((n,)))]
    names = [i[0] for i in ins] + [o[0] for o in outs] + [x[0] for x in vmem] + [x[0] for x in sems]
    res = pl.pallas_call(
        functools.partial(block_kernel, n_dp, names),
        out_shape=tuple(sds(shape, dtype) for _, shape, dtype, _ in outs),
        in_specs=[i[2] for i in ins],
        out_specs=tuple(o[3] for o in outs),
        scratch_shapes=[pltpu.VMEM(shape, dtype) for _, shape, dtype in vmem] + [x[1] for x in sems],
        compiler_params=pltpu.CompilerParams(vmem_limit_bytes=63 * MIB + 3 * MIB // 4, collective_id=0, has_side_effects=True),
        cost_estimate=pl.CostEstimate(flops=4 * 10**10, bytes_accessed=10**8, transcendentals=0),
        name="block",
    )(*[i[1] for i in ins])
    out16, gtok, grads, mods, small = res[:5]
    vecs = [sds((d,), F)] * 5
    finals = [sds((rows, d), BF), sds((rows, d), F), sds((3 * width, d), F), sds((width, d), F), sds((d, hidden), F), sds((hidden, d), F), sds((cond, 6 * d), F)]
    done = pl.pallas_call(
        functools.partial(finish_kernel, n_dp),
        out_shape=tuple(finals + [sds((2, cond), F), sds((6 * d,), F)] + vecs),
        in_specs=[a, a, a, a, m, a, m],
        out_specs=tuple([a] * len(finals) + [m] * 7),
        scratch_shapes=[
            pltpu.VMEM((total, d), BF), pltpu.VMEM((total, d), F), pltpu.VMEM((rows, d), BF), pltpu.VMEM((rows, d), F), pltpu.VMEM(mods.shape, F),
            pltpu.VMEM(ada_weight.shape, BF), pltpu.VMEM((6, cond, d), F), dma((40,)),
        ],
        compiler_params=pltpu.CompilerParams(vmem_limit_bytes=63 * MIB),
        cost_estimate=pl.CostEstimate(flops=10**8, bytes_accessed=2 * 10**7, transcendentals=0),
        name="finish",
    )(grads, out16, gtok, mods, small, ada_weight, time_emb)
    output, grad_tokens, gqkv, gout, gup, gdown, grad_ada, grad_time, grad_adab, g_mask, g_attn, g_mlp, g_upb, g_db = done
    return (output, grad_tokens, grad_time, g_mask, g_attn, g_mlp, grad_ada, grad_adab, gqkv.reshape(3, width, d).transpose(2, 0, 1), gout, gup, g_upb, gdown, g_db)


def solution(mesh):
    group = ("dp", "tensor")
    in_specs = (P(group, None), P("dp", None), P("dp"), P(group), P(), P(), P(), P(), P(), P(None, None, "tensor"), P("tensor", None), P(None, "tensor"), P("tensor"), P("tensor", None), P(), P(group, None))
    out_specs = (P(group, None), P(group, None), P("dp", None), P(), P(), P(), P(), P(), P(None, None, "tensor"), P("tensor", None), P(None, "tensor"), P("tensor"), P("tensor", None), P())
    return jax.shard_map(per_device, mesh=mesh, in_specs=in_specs, out_specs=out_specs, check_vma=False)
```

```python
import functools

import jax
import jax.numpy as jnp
import numpy as np
from jax import lax
from jax.experimental import pallas as pl
from jax.experimental.pallas import tpu as pltpu
from jax.sharding import PartitionSpec as P

BF = jnp.bfloat16
F = jnp.float32
HD = 64
LEN = 1024
EPS = 1e-05
GELU_COEF = 0.7978845608028654
CUBIC_COEF = 0.044715
SCALE = 0.125
LOG2E = 1.4426950408889634
EXP_SCALE = SCALE * LOG2E
MIB = 1 << 20


def nn(a, b):
    return lax.dot_general(a, b, (((1,), (0,)), ((), ())), preferred_element_type=F)


def nt(a, b):
    return lax.dot_general(a, b, (((1,), (1,)), ((), ())), preferred_element_type=F)


def tn(a, b):
    return lax.dot_general(a, b, (((0,), (0,)), ((), ())), preferred_element_type=F)


def normalize(values):
    centered = values - jnp.mean(values, axis=-1, keepdims=True)
    inv = lax.rsqrt(jnp.mean(centered * centered, axis=-1, keepdims=True) + EPS)
    return centered * inv, inv


def layer_back(grad_norm, normed, inv):
    mean_grad = jnp.mean(grad_norm, axis=-1, keepdims=True)
    mean_cross = jnp.mean(grad_norm * normed, axis=-1, keepdims=True)
    return inv * (grad_norm - mean_grad - normed * mean_cross)


def halves_turned(v):
    parts = []
    for h in range(v.shape[1] // HD):
        lo = v[:, h * HD : h * HD + HD // 2]
        hi = v[:, h * HD + HD // 2 : (h + 1) * HD]
        parts += [-hi, lo]
    return jnp.concatenate(parts, axis=1)


def halves_back(v):
    parts = []
    for h in range(v.shape[1] // HD):
        lo = v[:, h * HD : h * HD + HD // 2]
        hi = v[:, h * HD + HD // 2 : (h + 1) * HD]
        parts += [hi, -lo]
    return jnp.concatenate(parts, axis=1)


def tables(block, heads):
    cos, sin = block[:, :HD], block[:, HD:]
    return jnp.concatenate([cos] * heads, axis=1), jnp.concatenate([sin] * heads, axis=1)


MESH = pl.DeviceIdType.MESH
PIECE = 256
HALVED = 3


def sds(shape, dtype):
    return jax.ShapeDtypeStruct(shape, dtype)


def split3(v):
    hi = v.astype(BF).astype(F)
    mid = (v - hi).astype(BF).astype(F)
    return hi, mid, v - hi - mid


def pick(index, values):
    out = jnp.int32(values[0])
    for i, v in enumerate(values[1:], 1):
        out = jnp.where(index == i, jnp.int32(v), out)
    return out


MLP_ORDER = [(1, 0), (1, 1), (3, 0), (2, 0), (1, 2), (0, 0), (3, 1), (2, 1), (0, 1), (0, 2), (3, 2), (2, 2)]
CROSS = [(768, 256), (1536, 256), (1024, 256), (1792, 256), (1280, 256), (2048, 256), (0, 128), (128, 128), (256, 128), (384, 128), (512, 128), (640, 128)]
SMALL_INPUTS = ("mask", "gain1", "gain2", "dbias", "upb", "adab", "time", "noise")


def block_kernel(n_dp, names, *args):
    ref = dict(zip(names, args))
    g = lambda *keys: [ref[key] for key in keys]
    tok_h, cot_h, prefix, ada_h, table_h, wt_h, wo_h, wu_h, wd_h = g("tok_h", "cot_h", "prefix", "ada_h", "table_h", "wt_h", "wo_h", "wu_h", "wd_h")
    out_o, gtok_o, grads_o, mods_o, small_o, wmu, wmd = g("out_o", "gtok_o", "grads_o", "mods_o", "small_o", "wmu", "wmd")
    w, wsu, wsd, rb, rx, sx, g0, sb, ry, rz, exv = g("w", "wsu", "wsd", "rb", "rx", "sx", "g0", "sb", "ry", "rz", "exv")
    tok, cs, h1o, h1p, q, k, v, att, st, km = g("tok", "cs", "h1o", "h1p", "q", "k", "v", "att", "st", "km")
    branch, mixed, h2, gm, bm, gh, dk, dv, dq, parr, dwo2 = g(
        "branch", "mixed", "h2", "gm", "bm", "gh", "dk", "dv", "dq", "parr", "dwo2"
    )
    vecs, mod, nz, bus, gub, sums, mods, cse, cre, xse, xre, bse, bre = g(
        "vecs", "mod", "nz", "bus", "gub", "sums", "mods", "cse", "cre", "xse", "xre", "bse", "bre"
    )
    rows, d = tok.shape
    width = q.shape[2]
    heads = width // HD
    cond = ada_h.shape[0]
    tile = 256
    dp = lax.axis_index("dp")
    t = lax.axis_index("tensor")
    xb, cb = t // 2, t % 2
    bits = [1 << i for i in range(n_dp.bit_length() - 1)]
    bit = [(dp // b) % 2 for b in bits]
    core = (dp, t + 1 - 2 * cb)
    chip = (dp, t + 2 - 4 * xb)
    peer = [(dp + b - 2 * b * v_, t) for b, v_ in zip(bits, bit)]
    yb = bit[0]

    corner = (dp + 2 - 4 * bit[1] + 4 - 8 * bit[2], t)
    barrier = pltpu.get_barrier_semaphore()
    for other in [core, chip, corner] + peer:
        pl.semaphore_signal(barrier, inc=1, device_id=other, device_id_type=MESH)
    pl.semaphore_wait(barrier, 3 + len(peer))

    def remote(src, dst, name, index, to):
        return pltpu.make_async_remote_copy(
            src_ref=src, dst_ref=dst, send_sem=ref[name + "_s"].at[index], recv_sem=ref[name + "_r"].at[index], device_id=to, device_id_type=MESH
        )

    def local(src, dst, index):
        return pltpu.make_async_copy(src, dst, ref["loc"].at[index])

    def at(start, size, mult=8):
        return pl.ds(start if isinstance(start, int) else pl.multiple_of(start, mult), size)

    att_src = [(wt_h, 0), (wt_h, width), (wt_h, 2 * width), (wo_h, 0)]
    hw = width // 2

    def part(r, j, which):
        if j < 4:
            return w.at[r, at(j * width + which * hw, hw, 32)]
        c, kind = (j - 4) // 2, (j - 4) % 2
        span = at(c * PIECE + which * 128, 128, 128)
        return wmd.at[r, span] if kind else wmu.at[r, :, span]

    def own_part(j, which):
        if j < 4:
            src, base = att_src[j]
            return src.at[at(base + which * hw, hw, 32)]
        c, kind = (j - 4) // 2, (j - 4) % 2
        span = at(c * PIECE + which * 128, 128, 128)
        return wd_h.at[span] if kind else wu_h.at[:, span]

    def far(j):
        return remote(own_part(j, yb), part(2, j, yb), "far", j, chip)

    def side(j):
        return remote(part(2, j, yb), part(2, j, yb), "side", j, peer[0])

    def cross(j, which):
        p = part(2, j, (yb + which) % 2)
        return remote(p, part(3, j, (yb + which) % 2), "cross", 2 * j + which, core)

    near = [
        remote(wt_h, w.at[1, pl.ds(0, 3 * width)], "near", 0, core),
        remote(wo_h, w.at[1, pl.ds(3 * width, width)], "near", 1, core),
        remote(wu_h, wmu.at[1], "near", 2, core),
        remote(wd_h, wmd.at[1], "near", 3, core),
    ]
    n_parts = 10

    def arrived(j):
        far(j).wait_recv()
        side(j).start()
        cross(j, 0).start()

    def passed(j):
        side(j).wait_recv()
        cross(j, 1).start()

    ada = sb
    loads = [local(ada_h.at[:, pl.ds(i * d, d)], ada.at[pl.ds(i * cond, cond)], i) for i in range(6)]
    load_tok, load_cot = local(tok_h, tok, 6), local(cot_h, h2, 7)
    load_cs = [local(table_h.at[at(cb * rows, rows)], cs.at[pl.ds(0, rows)], 8), local(table_h.at[at((1 - cb) * rows, rows)], cs.at[pl.ds(rows, rows)], 9)]
    load_w = [local(wt_h, w.at[0, pl.ds(0, 3 * width)], 10), local(wo_h, w.at[0, pl.ds(3 * width, width)], 11)]
    load_small = [local(ref[name], ref[name + "_v"], 52 + i) for i, name in enumerate(SMALL_INPUTS)]
    mask_v, gain1_v, gain2_v, dbias_v, upb_v, adab_v, time_v, noise_v = [ref[name + "_v"] for name in SMALL_INPUTS]
    for c in load_small + loads + [load_tok]:
        c.start()
    for c in load_small:
        c.wait()
    bus[0] = jnp.broadcast_to(upb_v[...].astype(F).reshape(1, -1), bus.shape[1:])
    bias_near, bias_far = remote(bus.at[0], bus.at[1], "bias", 0, core), remote(bus.at[0], bus.at[2], "bias", 1, chip)
    bias_cross = remote(bus.at[2], bus.at[3], "bias", 2, core)
    bias_near.start()
    bias_far.start()
    for j in range(n_parts):
        far(j).start()
    near[0].start()
    for c in load_w + load_cs + [load_cot]:
        c.start()

    for i, one in enumerate((mask_v, gain1_v, gain2_v, dbias_v)):
        vecs[i : i + 1, :] = one[...].astype(F).reshape(1, d)
    tv = jnp.where(xb == 0, time_v[0:1, :].astype(F), time_v[1:2, :].astype(F))
    s = jnp.broadcast_to(tv, (16, cond))
    s = s / (1.0 + jnp.exp(-s))
    stacked = jnp.concatenate(split3(s), axis=0).astype(BF)
    for i in range(6):
        loads[i].wait()
        m = nn(stacked, ada[pl.ds(i * cond, cond), :])
        mod[i : i + 1, :] = m[0:1] + m[16:17] + m[32:33] + adab_v[pl.ds(i * d, d)].astype(F).reshape(1, d)
    place = lax.broadcasted_iota(jnp.int32, (4, 128), 0) * 128 + lax.broadcasted_iota(jnp.int32, (4, 128), 1) + cb * rows
    limit = jnp.where(xb == 0, prefix[0], prefix[1])
    on = jnp.where((noise_v[...] == 1) & (place >= limit), 1.0, 0.0)
    on = jnp.concatenate([on, jnp.zeros((12, 128), F)], axis=0).astype(BF)
    eye = jnp.where(lax.broadcasted_iota(jnp.int32, (128, 128), 0) == lax.broadcasted_iota(jnp.int32, (128, 128), 1), 1.0, 0.0).astype(BF)
    cols = nt(eye, on)
    for i in range(4):
        nz[i * 128 : (i + 1) * 128, :] = cols[:, i : i + 1]
    load_tok.wait()

    def inputs_at(rs):
        return jnp.where(nz[rs, :] > 0.5, vecs[0:1, :], tok[rs, :].astype(F))

    every = pl.ds(0, rows)
    n1, _ = normalize(inputs_at(every))
    h1o[...] = (n1 * vecs[1:2, :] * (1.0 + mod[1:2, :]) + mod[0:1, :]).astype(BF)
    h1_copy = remote(h1o, h1p, "h1", 0, core)
    h1_copy.start()
    load_cot.wait()
    gmv = (mod[5:6, :] * h2[...].astype(F)).astype(BF)
    gm[...] = gmv
    sums[4:5, :] = jnp.sum(gmv.astype(F), axis=0, keepdims=True)
    for c in load_cs + load_w[:1]:
        c.wait()
    h1_copy.wait()
    for c in near[1:]:
        c.start()

    lane_q = lax.broadcasted_iota(jnp.int32, (rows, width), 1) // HD
    lane = lax.broadcasted_iota(jnp.int32, (tile, width), 1) // HD
    lane_s = lax.broadcasted_iota(jnp.int32, (tile, 128), 1)

    def project(r):
        cos, sin = tables(cs[0:rows, :], heads)
        qv = nt(h1o[...], w[r, 0:width, :])
        qv = (qv * cos + halves_turned(qv) * sin).astype(BF)
        q[r] = qv
        qf = qv.astype(F)
        for h in range(heads):
            km[h, 0:rows, :] = jnp.where(lane_q == h, qf, 0.0).astype(BF)
        kv = nt(h1o[...], w[r, width : 2 * width, :])
        k[r, 0:rows, :] = (kv * cos + halves_turned(kv) * sin).astype(BF)
        v[r, 0:rows, :] = nt(h1o[...], w[r, 2 * width : 3 * width, :]).astype(BF)
        cos, sin = tables(cs[rows : 2 * rows, :], heads)
        kv = nt(h1p[...], w[r, width : 2 * width, :])
        k[r, rows : 2 * rows, :] = (kv * cos + halves_turned(kv) * sin).astype(BF)
        v[r, rows : 2 * rows, :] = nt(h1p[...], w[r, 2 * width : 3 * width, :]).astype(BF)

    def attend(r, i):
        rs = at(i * tile, tile, tile)
        acc = jnp.zeros((tile, width), F)
        stats = jnp.zeros((tile, 128), F)
        for h in range(heads):
            s = nt(km[h, rs, :], k[r])
            m = jnp.max(s, axis=1, keepdims=True)
            e = jnp.exp2((s - m) * EXP_SCALE)
            total = jnp.sum(e, axis=1, keepdims=True)
            p = (e * (1.0 / total)).astype(BF)
            acc = jnp.where(lane == h, nn(p, v[r]), acc)
            stats = jnp.where(lane_s == h, m * EXP_SCALE + jnp.log2(total), stats)
        att[r, rs, :] = acc.astype(BF)
        dq[rs, 0:128] = stats

    def at_step(step, todo):
        for key, fns in todo.items():

            @pl.when(step == key)
            def _():
                for fn in fns:
                    fn()

    def wait_near(i):
        return near[i].wait_recv

    def wait_cross(j):
        def go():
            cross(j, 0).wait_recv()
            cross(j, 1).wait_recv()

        return go

    arrive = lambda j: functools.partial(arrived, j)
    go_on = lambda j: functools.partial(passed, j)
    per_r = rows // tile

    def bias_on():
        bias_far.wait_recv()
        bias_cross.start()

    fwd_plan = {
        0: [arrive(0)],
        1: [arrive(1), bias_on],
        2: [wait_near(0), arrive(2), go_on(0)],
        3: [arrive(3), go_on(1)],
        4: [go_on(2)],
        5: [arrive(4), go_on(3)],
        6: [wait_cross(0), wait_cross(1), wait_cross(2)],
        7: [arrive(5), go_on(4)],
    }

    def fwd_body(it, carry):
        r, i = it // per_r, it % per_r
        at_step(it, fwd_plan)

        @pl.when(i == 0)
        def _():
            project(r)

        attend(r, i)

        @pl.when(i == per_r - 1)
        def _():
            st[r] = dq[:, 0:128].T[0:8, :]

        return carry

    lax.fori_loop(0, 4 * per_r, fwd_body, 0)
    arrived(6)
    load_w[1].wait()
    wait_near(1)()
    wait_cross(3)()

    def mid_body(i, carry):
        rs = at(i * tile, tile, tile)
        b = nn(att[0, rs, :], w[0, 3 * width : 4 * width, :])
        for r in range(1, 4):
            b = b + nn(att[r, rs, :], w[r, 3 * width : 4 * width, :])
        x = inputs_at(rs) + mod[2:3, :] * b
        n2, _ = normalize(x)
        branch[rs, :] = b
        mixed[rs, :] = x
        h2[rs, :] = (n2 * vecs[2:3, :] * (1.0 + mod[4:5, :]) + mod[3:4, :]).astype(BF)
        bm[rs, :] = jnp.zeros((tile, d), F)
        gh[rs, :] = jnp.zeros((tile, d), F)
        return carry

    lax.fori_loop(0, per_r, mid_body, 0)
    load_cot = local(cot_h, tok, 7)
    load_cot.start()

    def cross_send(n):
        base, size = CROSS[n]
        return remote(sx.at[pl.ds(base, size)], rx.at[pl.ds(base, size)], "gx", n, chip)

    def line_peer(m):
        return (dp + (2 - 4 * bit[1] if m & 2 else 0) + (4 - 8 * bit[2] if m & 1 else 0), t)

    def half_at(n, other=False):
        base, size = CROSS[n]
        return at(base + ((1 - yb) if other else yb) * (size // 2), size // 2, 16)

    def line_at(n, m=0):
        base, size = CROSS[n]
        rank = 2 * (1 - bit[1] if m & 2 else bit[1]) + (1 - bit[2] if m & 1 else bit[2])
        return at(base + yb * (size // 2) + rank * (size // 8), size // 8, 16)

    def out_half(n):
        base, size = CROSS[n]
        return pl.ds(base, size // 2)

    def out_line(n, m):
        base, size = CROSS[n]
        return pl.ds(base + size // 2 + (m - 1) * (size // 8), size // 8)

    def in_half(n):
        base, size = CROSS[n]
        return pl.ds(base // 2, size // 2)

    def in_line(n, m):
        base, size = CROSS[n]
        return pl.ds(base * 3 // 8 + (m - 1) * (size // 8), size // 8)

    def send_y(n):
        return remote(rx.at[out_half(n)], ry.at[in_half(n)], "gy", n, peer[0])

    def send_line(n, m):
        return remote(rx.at[out_line(n, m)], rz.at[in_line(n, m)], "gz", 3 * n + m - 1, line_peer(m))

    def back_far(n):
        return remote(sx.at[line_at(n)], sx.at[line_at(n)], "aw", n, peer[2])

    def back_near(n):
        base, size = CROSS[n]
        two = at(base + yb * (size // 2) + bit[1] * (size // 4), size // 4, 16)
        return remote(sx.at[two], sx.at[two], "az", n, peer[1])

    def back_y(n):
        return remote(sx.at[half_at(n)], sx.at[half_at(n)], "ay", n, peer[0])

    def more(e, n):
        return remote(g0.at[line_at(n)], ref["ex"].at[e, n, pl.ds(0, CROSS[n][1] // 8)], "ge", e * len(CROSS) + n, peer[HALVED + e])

    def stage_x(n):
        base, size = CROSS[n]
        cross_send(n).wait()
        g0[pl.ds(base, size), :] = g0[pl.ds(base, size), :] + rx[pl.ds(base, size), :].astype(F)
        rx[out_half(n), :] = g0[half_at(n, True), :].astype(BF)
        send_y(n).start()

    def stage_y(n):
        send_y(n).wait_recv()
        g0[half_at(n), :] = g0[half_at(n), :] + ry[in_half(n), :].astype(F)
        for m in (1, 2, 3):
            rx[out_line(n, m), :] = g0[line_at(n, m), :].astype(BF)
            send_line(n, m).start()

    def stage_z(n):
        for m in (1, 2, 3):
            send_line(n, m).wait_recv()
        got = [rz[in_line(n, m), :].astype(F) for m in (1, 2, 3)]
        total = g0[line_at(n), :] + ((got[0] + got[1]) + got[2])
        for e in range(len(bits) - HALVED):
            g0[line_at(n), :] = total
            more(e, n).start()
            more(e, n).wait()
            room = pl.ds(0, CROSS[n][1] // 8)
            fill = local(ref["ex"].at[e, n, room], exv.at[room], 36)
            fill.start()
            fill.wait()
            total = total + exv[room, :]
        sx[line_at(n), :] = total.astype(BF)
        back_far(n).start()

    def stage_a(n):
        back_far(n).wait_recv()
        back_near(n).start()

    def stage_b(n):
        back_near(n).wait_recv()
        back_y(n).start()

    def result(n):
        base, size = CROSS[n]
        return local(sx.at[pl.ds(base, size)], grads_o.at[pl.ds(base, size)], 14 + n)

    def stage_c(n):
        back_y(n).wait_recv()
        result(n).start()

    def stage_end(n):
        send_y(n).wait_send()
        for m in (1, 2, 3):
            send_line(n, m).wait_send()
        back_far(n).wait_send()
        back_near(n).wait_send()
        back_y(n).wait_send()
        result(n).wait()

    stages = dict(X=stage_x, Y=stage_y, Z=stage_z, A=stage_a, B=stage_b, C=stage_c)

    def run(text):
        for i in range(0, len(text), 2):
            stages[text[i]](int(text[i + 1], 16))

    steps = len(MLP_ORDER)

    def core_slot(step):
        return 2 * (sum(1 for r, _ in MLP_ORDER[:step] if r % 2) % 3)

    def give(step, kind):
        r, c = MLP_ORDER[step]
        slot = core_slot(step) + kind
        row = (3 * kind + c) * PIECE
        return remote(sb.at[pl.ds(slot * PIECE, PIECE)], rb.at[r // 2, pl.ds(row, PIECE)], "give", 2 * step + kind, core)

    def fetch(step, slot, own):
        r = pick(step, [r for r, _ in MLP_ORDER])
        c = pick(step, [c for _, c in MLP_ORDER])
        span = at(c * PIECE, PIECE, PIECE)
        up, down = (wu_h, wd_h) if own else (wmu.at[r], wmd.at[r])
        return [
            pltpu.make_async_copy(up.at[:, span], wsu.at[slot], ref["wst"].at[slot, 0]),
            pltpu.make_async_copy(down.at[span], wsd.at[slot], ref["wst"].at[slot, 1]),
        ]

    bias_near.wait_recv()
    for i in (2, 3):
        near[i].wait_recv()
    for c in fetch(0, 0, False):
        c.start()

    mlp_plan = {
        0: [go_on(5)],
        1: [wait_cross(4), wait_cross(5), arrive(7), go_on(6)],
        3: [arrive(8), go_on(7)],
        5: [wait_cross(6), wait_cross(7), arrive(9)],
        7: [go_on(8)],
        9: [go_on(9), wait_cross(8), wait_cross(9)],
    }

    def mlp_body(step, carry):
        slot = step % 2
        r = pick(step, [r for r, _ in MLP_ORDER])
        c = pick(step, [c for _, c in MLP_ORDER])
        at_step(step, mlp_plan)
        for cp in fetch(step, slot, False):
            cp.wait()

        nxt = pick(step, [r for r, _ in MLP_ORDER[1:]] + [4])

        @pl.when((nxt > 0) & (nxt < 4))
        def _():
            for cp in fetch(step + 1, 1 - slot, False):
                cp.start()

        @pl.when(nxt == 0)
        def _():
            for cp in fetch(step + 1, 1 - slot, True):
                cp.start()

        @pl.when(step == 0)
        def _():
            bias_cross.wait_recv()

        cols = at(c * PIECE, PIECE, PIECE)
        u = nn(h2[...], wsu[slot]) + bus[r, 0:1, cols]
        th = jnp.tanh(GELU_COEF * (u + CUBIC_COEF * u * u * u))
        act = (0.5 * u * (1.0 + th)).astype(BF)
        slope = 0.5 * (1.0 + th) + 0.5 * u * (1.0 - th * th) * GELU_COEF * (1.0 + 3.0 * CUBIC_COEF * u * u)
        gu_f = (nt(gm[...], wsd[slot]) * slope).astype(BF).astype(F)
        gu = gu_f.astype(BF)
        gub[r, 0:1, cols] = jnp.sum(gu_f, axis=0, keepdims=True)
        bm[...] += nn(act, wsd[slot])
        gh[...] += nt(gu, wsu[slot])
        ds_ = (tn(gu, h2[...]), tn(act, gm[...]))
        for i, (r_, c_) in enumerate(MLP_ORDER):

            @pl.when(step == i)
            def _():
                rows_ = [pl.ds((3 + 3 * kind + c_) * PIECE, PIECE) for kind in range(2)]
                inbox = [pl.ds((3 * kind + c_) * PIECE, PIECE) for kind in range(2)]
                if r_ % 2:
                    before = [j for j in range(i) if MLP_ORDER[j][0] % 2 and core_slot(j) == core_slot(i)]
                    for kind in range(2):
                        if before:
                            give(before[-1], kind).wait_send()
                        sb[pl.ds((core_slot(i) + kind) * PIECE, PIECE), :] = ds_[kind].astype(BF)
                        give(i, kind).start()
                else:
                    origin = MLP_ORDER.index((r_ + 1, c_))
                    for kind in range(2):
                        give(origin, kind).wait_recv()
                        total = ds_[kind] + rb[r_ // 2, inbox[kind], :].astype(F)
                        if r_ == 2:
                            sx[rows_[kind], :] = total.astype(BF)
                            cross_send(CROSS.index(((3 + 3 * kind + c_) * PIECE, PIECE))).start()
                        else:
                            g0[rows_[kind], :] = total

        return carry

    lax.fori_loop(0, steps, mlp_body, 0)
    odd = [i for i, (r, _) in enumerate(MLP_ORDER) if r % 2]
    for i in odd[-3:]:
        for kind in range(2):
            give(i, kind).wait_send()

    load_cot.wait()
    run("X0")
    gba = h1p

    def post_body(i, carry):
        rs = at(i * tile, tile, tile)
        x = mixed[rs, :]
        n2, inv = normalize(x)
        c = tok[rs, :].astype(F)
        bmlp = bm[rs, :] + vecs[3:4, :]
        h2[rs, :] = (x + mod[5:6, :] * bmlp).astype(BF)
        gr = gh[rs, :]
        gs = gr * (1.0 + mod[4:5, :])
        gmix = c + layer_back(gs * vecs[2:3, :], n2, inv)
        mixed[rs, :] = gmix
        gba[rs, :] = (mod[2:3, :] * gmix).astype(BF)
        part_sums = [gs * n2, gmix * branch[rs, :], gr, gr * n2 * vecs[2:3, :], c * bmlp]
        for row, val in zip((3, 10, 11, 12, 13), part_sums):
            got = jnp.sum(val, axis=0, keepdims=True)

            @pl.when(i == 0)
            def _():
                sums[row : row + 1, :] = got

            @pl.when(i > 0)
            def _():
                sums[row : row + 1, :] += got

        return carry

    lax.fori_loop(0, per_r, post_body, 0)
    store_out = local(h2, out_o, 26)
    store_out.start()
    load_tok = local(tok_h, tok, 6)
    load_tok.start()
    for r in range(4):
        wo = w[r, 3 * width : 4 * width, :]
        dw = tn(att[r], gba[...])
        att[r] = nt(gba[...], wo).astype(BF)
        if r == 0:
            g0[pl.ds(3 * width, width), :] = dw
        elif r == 2:
            dwo2[...] = dw
        else:
            sb[pl.ds((3 - r) // 2 * 4 * width + 3 * width, width), :] = dw.astype(BF)

    lane_k = lax.broadcasted_iota(jnp.int32, (2 * rows, width), 1) // HD

    def back_tile(r, i, it):
        @pl.when(i == 0)
        def _():
            kf = k[r].astype(F)
            for h in range(heads):
                km[h] = jnp.where(lane_k == h, kf, 0.0).astype(BF)
            dk[...] = jnp.zeros_like(dk)
            dv[...] = jnp.zeros_like(dv)

        rs = at(i * tile, tile, tile)
        qt = q[r, rs, :].astype(F)
        gt = att[r, rs, :].astype(F)
        acc = jnp.zeros((tile, width), F)
        for h in range(heads):
            back_events(it, h)
            qm = jnp.where(lane == h, qt, 0.0).astype(BF)
            gmh = jnp.where(lane == h, gt, 0.0).astype(BF)
            p = jnp.exp2(nt(k[r], qm) * EXP_SCALE - st[r, h : h + 1, rs])
            dpr = nt(v[r], gmh)
            inner = jnp.sum(p * dpr, axis=0, keepdims=True)
            ds_ = (p * (dpr - inner)).astype(BF)
            dv[...] += nn(p.astype(BF), gmh)
            dk[...] += nn(ds_, qm)
            acc = acc + tn(ds_, km[h])
        dq[rs, :] = acc

    def par_copy(r):
        lanes = pl.ds((r % 2) * 2 * width, 2 * width)
        return remote(branch.at[:, lanes], parr.at[r % 2], "par", r, core)

    def finish_back(r):
        cos, sin = tables(cs[0:rows, :], heads)
        gq = dq[...] * SCALE
        q[r] = (gq * cos + halves_back(gq * sin)).astype(BF)
        lanes = slice((r % 2) * 2 * width, (r % 2) * 2 * width + 2 * width)
        bm[:, lanes] = jnp.concatenate([dk[0:rows, :] * SCALE, dv[0:rows, :]], axis=1)
        if r < 2:
            par_copy(r + 2).wait_send()
            if r == 1:
                pl.semaphore_wait(ref["credit"], 1)
        branch[:, lanes] = jnp.concatenate([dk[rows : 2 * rows, :] * SCALE, dv[rows : 2 * rows, :]], axis=1)
        par_copy(r).start()

    def hand(r):
        base = (3 - r) // 2 * 4 * width
        return remote(sb.at[pl.ds(base, 4 * width)], rb.at[r // 2, pl.ds(0, 4 * width)], "hand", r // 2, core)

    def weight_grads(r):
        par_copy(r ^ 1).wait_recv()
        cos, sin = tables(cs[0:rows, :], heads)
        lanes = slice((r % 2) * 2 * width, (r % 2) * 2 * width + 2 * width)
        gkv = bm[:, lanes] + parr[(r ^ 1) % 2]
        gk = gkv[:, :width]
        gk = (gk * cos + halves_back(gk * sin)).astype(BF)
        gv = gkv[:, width:].astype(BF)
        parts = (q[r], gk, gv)
        if r % 2 == 0:
            hand(r + 1).wait_recv()
        back = 0.0 if r == 3 else gh[...]
        for i, p_ in enumerate(parts):
            place_ = pl.ds(i * width, width)
            back = back + nn(p_, w[r, i * width : (i + 1) * width, :])
            dw = tn(p_, h1o[...])
            if r % 2:
                sb[pl.ds((3 - r) // 2 * 4 * width + i * width, width), :] = dw.astype(BF)
            else:
                dw = dw + rb[r // 2, place_, :].astype(F)
                if r == 2:
                    sx[place_, :] = dw.astype(BF)
                else:
                    g0[place_, :] = dw
        gh[...] = back
        place_ = pl.ds(3 * width, width)
        if r % 2:
            hand(r).start()
        elif r == 2:
            sx[place_, :] = (dwo2[...] + rb[1, place_, :].astype(F)).astype(BF)
            for n in range(6, len(CROSS)):
                cross_send(n).start()
        else:
            g0[place_, :] = g0[place_, :] + rb[0, place_, :].astype(F)

    def give_credit():
        pl.semaphore_signal(ref["credit"], inc=1, device_id=core, device_id_type=MESH)

    back_plan = [
        {0: "X1", 2: "Y1X2", 4: "Z1Y2", 5: "A1Y3X4B0Z2", 7: "Y4Z3X5"},
        {4: "X3A0", 6: "B1", 7: "A2"},
        {0: "Y0", 2: "Z0"},
    ]

    def back_events(it, h):
        at_step(it, {key: [functools.partial(run, text)] for key, text in back_plan[h].items()})

    def back_body(it, carry):
        i = it % per_r
        back_tile(3 - it // per_r, i, it)
        for r in range(4):

            @pl.when(it == (3 - r) * per_r + per_r - 1)
            def _():
                finish_back(r)

        @pl.when(it == 2 * per_r)
        def _():
            weight_grads(3)
            weight_grads(2)
            give_credit()

        return carry

    lax.fori_loop(0, 4 * per_r, back_body, 0)
    run("C0")
    weight_grads(1)
    run("Z4C1")
    weight_grads(0)

    hand(1).wait_send()
    hand(3).wait_send()
    store_out.wait()
    load_tok.wait()
    run("X6X7B2A3Y5X8")

    def tail_body(i, carry):
        rs = at(i * tile, tile, tile)
        on_ = nz[rs, :] > 0.5
        n1_, inv = normalize(inputs_at(rs))
        gr = gh[rs, :]
        gs = gr * (1.0 + mod[1:2, :])
        gi = mixed[rs, :] + layer_back(gs * vecs[1:2, :], n1_, inv)
        mixed[rs, :] = jnp.where(on_, 0.0, gi)
        part_sums = [gs * n1_, jnp.where(on_, gi, 0.0), gr, gr * n1_ * vecs[1:2, :]]
        for row, val in zip((1, 2, 8, 9), part_sums):
            got = jnp.sum(val, axis=0, keepdims=True)

            @pl.when(i == 0)
            def _():
                sums[row : row + 1, :] = got

            @pl.when(i > 0)
            def _():
                sums[row : row + 1, :] += got

        return carry

    lax.fori_loop(0, per_r, tail_body, 0)
    store_tok = local(mixed, gtok_o, 27)
    store_tok.start()
    run("A4")

    none = jnp.zeros((2, d), F)
    cse[0:8, :] = jnp.concatenate([sums[8:14, :], none], axis=0)
    cse[8:16, :] = jnp.concatenate([gub[1, 0:1, :], gub[3, 0:1, :], sums[1:5, :], none], axis=0)
    core_sum = remote(cse, cre, "sc", 0, core)
    core_sum.start()
    me = 2 * dp + xb
    chip_sum = remote(xse, xre, "sx", 0, chip)
    chip_mods = remote(mods.at[me], mods.at[me], "sx", 1, chip)

    def peer_sums(i):
        block = pl.ds((dp // bits[i]) * bits[i] * 2, 2 * bits[i])
        return remote(bse.at[i], bre.at[i], "sd", 2 * i, peer[i]), remote(mods.at[block], mods.at[block], "sd", 2 * i + 1, peer[i])

    def sums_on(i):
        if i == 0:
            core_sum.wait_recv()
            tv_row = jnp.concatenate([tv, jnp.zeros((1, d - cond), F)], axis=1)
            mods[me] = jnp.concatenate([cse[0:6, :] + cre[0:6, :], tv_row, jnp.zeros((1, d), F)], axis=0)
            xse[...] = jnp.concatenate([gub[2, 0:1, :] + cre[9:10, :], cse[10:14, :] + cre[10:14, :], jnp.zeros((3, d), F)], axis=0)
            chip_sum.start()
            chip_mods.start()
            return
        if i == 1:
            chip_sum.wait_recv()
            cur = jnp.concatenate([gub[0, 0:1, :] + cre[8:9, :] + xre[0:1, :], xse[1:8, :] + xre[1:8, :]], axis=0)
            chip_mods.wait()
        else:
            one, two = peer_sums(i - 2)
            one.wait_recv()
            two.wait()
            cur = bse[i - 2] + bre[i - 2]
        if i - 1 < len(bits):
            bse[i - 1] = cur
            for c in peer_sums(i - 1):
                c.start()
        else:
            small_o[...] = cur

    run("Y6X9B3Y7")
    sums_on(0)
    run("Z5XaB4C2Z6Y8")
    sums_on(1)
    run("XbZ7A5Y9A6Z8C3A7")
    for i in range(2, len(bits) - 1):
        sums_on(i)
    run("B5YaZ9B6A8B7C4Za")
    sums_on(len(bits) - 1)
    run("YbA9B8AaC5ZbB9C6")
    sums_on(len(bits))
    run("BaC7AbC8C9Bb")
    sums_on(len(bits) + 1)
    store_mods = local(mods, mods_o, 28)
    store_mods.start()
    run("CaCb")
    for n in range(len(CROSS)):
        stage_end(n)
    for c in [store_mods, store_tok]:
        c.wait()
    for c in [core_sum, chip_sum] + [peer_sums(i)[0] for i in range(len(bits))]:
        c.wait_send()
    for c in near + [bias_near, bias_far, bias_cross]:
        c.wait_send()
    for j in range(n_parts):
        far(j).wait_send()
        side(j).wait_send()
        cross(j, 0).wait_send()
        cross(j, 1).wait_send()
    for r in range(2):
        par_copy(r).wait_send()


def finish_kernel(n_dp, grads_h, out_h, tok_h, mods_h, small_h, ada_h, time_h, out_o, gtok_o, gqkv_o, gout_o, gup_o, gdown_o, gada_o, gtime_o, gadab_o, gmask_o, ga_o, gm_o, gub_o, gdb_o, grads, wide, outv, tokv, mods, ada, adag, small, time, gtv, gbv, row0, row1, row2, row3, row4, sem):
    d = grads.shape[1]
    width = gout_o.shape[0]
    cond = ada.shape[0]
    seqs = mods.shape[0]
    dp = lax.axis_index("dp")

    def copy(src, dst, index):
        return pltpu.make_async_copy(src, dst, sem.at[index])

    span = lambda p: pl.ds(p * PIECE, PIECE)
    load_mods, load_ada = copy(mods_h, mods, 0), copy(ada_h, ada, 1)
    load_tok, load_out = copy(tok_h, tokv, 2), copy(out_h, outv, 3)
    pieces = [copy(grads_h.at[span(p)], grads.at[span(p)], 4 + p) for p in range(9)]
    rowv = (row0, row1, row2, row3, row4)
    load_small = [copy(small_h, small, 36), copy(time_h, time, 37)]
    for c in load_small + [load_mods] + pieces + [load_tok, load_out, load_ada]:
        c.start()
    stores = []

    def store(src, dst):
        stores.append(copy(src, dst, 13 + len(stores) if len(stores) < 23 else 15 + len(stores)))
        stores[-1].start()

    for c in load_small:
        c.wait()
    for row, o in enumerate((gub_o, ga_o, gmask_o, gm_o, gdb_o)):
        rowv[row][...] = small[row : row + 1, :].reshape(d)
        store(rowv[row], o)
    head = 3 * width
    for p in range(9):
        pieces[p].wait()
        if 3 <= p < 6:
            for b in range(3):
                wide[span(p), span(b)] = grads[span(p), span(b)].astype(F).T
                store(wide.at[span(p), span(b)], gup_o.at[span(b), span(p - 3)])
        else:
            wide[span(p), :] = grads[span(p), :].astype(F)
            if p >= 6:
                store(wide.at[span(p)], gdown_o.at[span(p - 6)])
            elif p == 2:
                store(wide.at[pl.ds(0, head)], gqkv_o)
                store(wide.at[pl.ds(head, width)], gout_o)
    load_tok.wait()
    store(tokv, gtok_o)
    load_out.wait()
    store(outv, out_o)
    load_mods.wait()
    total = mods[0]
    for s_ in range(1, seqs):
        total = total + mods[s_]
    tall = jnp.concatenate([mods[s_, 6:7, 0:cond] for s_ in range(seqs)], axis=0)
    left = split3(tall / (1.0 + jnp.exp(-tall)))
    lhs = jnp.concatenate([left[0], left[0], left[1], left[0], left[2], left[1]], axis=0).astype(BF)
    for j in range(6):
        gbv[pl.ds(j * d, d)] = total[j : j + 1, :].reshape(d)
        right = split3(jnp.concatenate([mods[s_, j : j + 1, :] for s_ in range(seqs)], axis=0))
        rhs = jnp.concatenate([right[0], right[1], right[0], right[2], right[0], right[1]], axis=0).astype(BF)
        adag[j] = tn(lhs, rhs)
        store(adag.at[j], gada_o.at[:, pl.ds(j * d, d)])
    load_ada.wait()
    acc = jnp.zeros((48, cond), F)
    for j in range(6):
        pairs = jnp.concatenate([mods[2 * dp, j : j + 1, :], mods[2 * dp + 1, j : j + 1, :], jnp.zeros((14, d), F)], axis=0)
        acc = acc + nt(jnp.concatenate(split3(pairs), axis=0).astype(BF), ada[:, pl.ds(j * d, d)])
    te = time[...].astype(F)
    sig = 1.0 / (1.0 + jnp.exp(-te))
    gtv[...] = (acc[0:2] + acc[16:18] + acc[32:34]) * sig * (1.0 + te * (1.0 - sig))
    store(gtv, gtime_o)
    store(gbv, gadab_o)
    for c in stores:
        c.wait()


def rotary_block():
    freq = np.float32(10000.0) ** (np.float32(-2.0) * np.arange(HD // 2, dtype=np.float32) / np.float32(HD))
    angle = np.arange(LEN, dtype=np.float32)[:, None] * freq[None, :].astype(np.float32)
    angle = np.concatenate([angle, angle], axis=1)
    return np.concatenate([np.cos(angle), np.sin(angle)], axis=1).astype(np.float32)


def per_device(tokens, time_emb, prefix_len, noise_mask, mask_embed, gain_attn, gain_mlp, ada_weight, ada_bias, qkv_weight, out_weight, up_weight, up_bias, down_weight, down_bias, cotangent):
    rows, d = tokens.shape
    n_dp = lax.axis_size("dp")
    width = qkv_weight.shape[2]
    cond = time_emb.shape[1]
    hidden = up_weight.shape[1]
    n_bits = n_dp.bit_length() - 1
    assert lax.axis_size("tensor") == 4 and time_emb.shape[0] == 2 and 2 * rows == LEN
    assert n_dp == 1 << n_bits and n_bits >= HALVED and 4 * width == hidden == 3 * PIECE == d
    wt = qkv_weight.transpose(1, 2, 0).reshape(3 * width, d)
    table = jnp.asarray(rotary_block())
    a = pl.BlockSpec(memory_space=pl.ANY)
    m = pl.BlockSpec(memory_space=pltpu.VMEM)
    smem = pl.BlockSpec(memory_space=pltpu.SMEM)
    total = 4 * width + 2 * hidden
    noise = noise_mask.reshape(4, rows // 4)
    small_in = (mask_embed, gain_attn, gain_mlp, down_bias, up_bias, ada_bias, time_emb, noise)
    ins = [("tok_h", tokens, a), ("cot_h", cotangent, a), ("prefix", prefix_len, smem)]
    ins += [(name, value, a) for name, value in zip(SMALL_INPUTS, small_in)]
    ins += [("ada_h", ada_weight, a), ("table_h", table, a), ("wt_h", wt, a), ("wo_h", out_weight, a), ("wu_h", up_weight, a), ("wd_h", down_weight, a)]
    outs = [
        ("out_o", (rows, d), BF, a), ("gtok_o", (rows, d), F, a), ("grads_o", (total, d), BF, a), ("mods_o", (2 * n_dp, 8, d), F, a), ("small_o", (8, d), F, m),
        ("wmu", (4, d, hidden), BF, a), ("wmd", (4, hidden, d), BF, a),
    ]
    n_pieces = len(CROSS)
    extra = max(n_bits - HALVED, 1)
    if n_bits > HALVED:
        outs.append(("ex", (extra, n_pieces, 32, d), F, a))
    vmem = [
        ("w", (4, 4 * width, d), BF), ("wsu", (2, d, PIECE), BF), ("wsd", (2, PIECE, d), BF), ("rb", (2, 2 * hidden, d), BF), ("rx", (total, d), BF), ("sx", (total, d), BF),
        ("g0", (total, d), F), ("sb", (6 * PIECE, d), BF), ("ry", (total // 2, d), BF), ("rz", (total * 3 // 8, d), BF), ("exv", (32, d), F),
        ("tok", (rows, d), BF), ("cs", (2 * rows, 2 * HD), F), ("h1o", (rows, d), BF), ("h1p", (rows, d), BF),
        ("q", (4, rows, width), BF), ("k", (4, 2 * rows, width), BF), ("v", (4, 2 * rows, width), BF), ("att", (4, rows, width), BF), ("st", (4, 8, rows), F),
        ("km", (width // HD, 2 * rows, width), BF), ("branch", (rows, d), F), ("mixed", (rows, d), F), ("h2", (rows, d), BF), ("gm", (rows, d), BF),
        ("bm", (rows, d), F), ("gh", (rows, d), F), ("dk", (2 * rows, width), F), ("dv", (2 * rows, width), F), ("dq", (rows, width), F),
        ("parr", (2, rows, 2 * width), F), ("dwo2", (width, d), F), ("vecs", (8, d), F), ("mod", (8, d), F), ("nz", (rows, 1), F),
        ("bus", (4, 8, hidden), F), ("gub", (4, 8, hidden), F), ("sums", (16, d), F), ("mods", (2 * n_dp, 8, d), F), ("cse", (16, d), F), ("cre", (16, d), F),
        ("xse", (8, d), F), ("xre", (8, d), F), ("bse", (n_bits, 8, d), F), ("bre", (n_bits, 8, d), F),
    ]
    vmem += [(name + "_v", value.shape, value.dtype) for name, value in zip(SMALL_INPUTS, small_in)]
    pairs = [
        ("far", 10), ("side", 10), ("cross", 20), ("near", 4), ("bias", 3), ("h1", 1), ("give", 24), ("gx", n_pieces), ("gy", n_pieces), ("gz", 3 * n_pieces), ("aw", n_pieces), ("az", n_pieces), ("ay", n_pieces),
        ("ge", n_pieces * extra), ("par", 4), ("hand", 2), ("sc", 1), ("sx", 2), ("sd", 2 * n_bits),
    ]
    dma = pltpu.SemaphoreType.DMA
    sems = [("loc", dma((60,))), ("wst", dma((2, 2))), ("credit", pltpu.SemaphoreType.REGULAR)]
    for name, n in pairs:
        sems += [(name + "_s", dma((n,))), (name + "_r", dma((n,)))]
    names = [i[0] for i in ins] + [o[0] for o in outs] + [x[0] for x in vmem] + [x[0] for x in sems]
    res = pl.pallas_call(
        functools.partial(block_kernel, n_dp, names),
        out_shape=tuple(sds(shape, dtype) for _, shape, dtype, _ in outs),
        in_specs=[i[2] for i in ins],
        out_specs=tuple(o[3] for o in outs),
        scratch_shapes=[pltpu.VMEM(shape, dtype) for _, shape, dtype in vmem] + [x[1] for x in sems],
        compiler_params=pltpu.CompilerParams(vmem_limit_bytes=63 * MIB + 3 * MIB // 4, collective_id=0, has_side_effects=True),
        cost_estimate=pl.CostEstimate(flops=4 * 10**10, bytes_accessed=10**8, transcendentals=0),
        name="block",
    )(*[i[1] for i in ins])
    out16, gtok, grads, mods, small = res[:5]
    vecs = [sds((d,), F)] * 5
    finals = [sds((rows, d), BF), sds((rows, d), F), sds((3 * width, d), F), sds((width, d), F), sds((d, hidden), F), sds((hidden, d), F), sds((cond, 6 * d), F)]
    done = pl.pallas_call(
        functools.partial(finish_kernel, n_dp),
        out_shape=tuple(finals + [sds((2, cond), F), sds((6 * d,), F)] + vecs),
        in_specs=[a] * 7,
        out_specs=tuple([a] * (len(finals) + 7)),
        scratch_shapes=[
            pltpu.VMEM((total, d), BF), pltpu.VMEM((total, d), F), pltpu.VMEM((rows, d), BF), pltpu.VMEM((rows, d), F), pltpu.VMEM(mods.shape, F),
            pltpu.VMEM(ada_weight.shape, BF), pltpu.VMEM((6, cond, d), F), pltpu.VMEM((8, d), F), pltpu.VMEM((2, cond), BF), pltpu.VMEM((2, cond), F), pltpu.VMEM((6 * d,), F),
            *[pltpu.VMEM((d,), F)] * 5, dma((60,)),
        ],
        compiler_params=pltpu.CompilerParams(vmem_limit_bytes=63 * MIB),
        cost_estimate=pl.CostEstimate(flops=10**8, bytes_accessed=2 * 10**7, transcendentals=0),
        name="finish",
    )(grads, out16, gtok, mods, small, ada_weight, time_emb)
    output, grad_tokens, gqkv, gout, gup, gdown, grad_ada, grad_time, grad_adab, g_mask, g_attn, g_mlp, g_upb, g_db = done
    return (output, grad_tokens, grad_time, g_mask, g_attn, g_mlp, grad_ada, grad_adab, gqkv.reshape(3, width, d).transpose(2, 0, 1), gout, gup, g_upb, gdown, g_db)


def solution(mesh):
    group = ("dp", "tensor")
    in_specs = (P(group, None), P("dp", None), P("dp"), P(group), P(), P(), P(), P(), P(), P(None, None, "tensor"), P("tensor", None), P(None, "tensor"), P("tensor"), P("tensor", None), P(), P(group, None))
    out_specs = (P(group, None), P(group, None), P("dp", None), P(), P(), P(), P(), P(), P(None, None, "tensor"), P("tensor", None), P(None, "tensor"), P("tensor"), P("tensor", None), P())
    return jax.shard_map(per_device, mesh=mesh, in_specs=in_specs, out_specs=out_specs, check_vma=False)
```
